512 devices in a mesh: branch: 8 (over y_lo, x), sky: 64 (over z, y_hi, core).
Axes of the slice: x: 4, y: 4 (y_hi: 2, y_lo: 2; y = y_hi * 2 + y_lo), z: 16, core: 2. Of those that a mesh axis runs over, the one named last changes fastest.
Arguments:
- sky_maps: bfloat16 [8, 64, 16384], P('branch', None, 'sky'), may hold values from -6 to 6
- footprint: int32 [8, 16384], P('branch', 'sky'), may hold values 0 or 1
- neighbours: int32 [9, 16384], P(None, 'sky'), may hold values from -1 to 16383, as said below
- enc_weight: bfloat16 [8, 6, 9, 64, 64], P('branch'), may hold values from -0.1875 to 0.1875
- join_weight: bfloat16 [256, 512], P(None, 'branch'), may hold values from -0.25 to 0.25
- dec_weight: bfloat16 [9, 256, 256], P(None, 'branch'), may hold values from -0.125 to 0.125
- cotangent: bfloat16 [256, 16384], P('branch', 'sky'), may hold values from -6 to 6
Outputs:
- map_grads: bfloat16 [8, 64, 16384], P('branch', None, 'sky')
- weight_grads: float32 [8, 6, 9, 64, 64], P('branch')
The draws below stay inside these ranges and needn't reach their ends.
Inputs may be any that keep to these rules, and one draw needn't show every extreme that they name: `neighbours`: slot 4 of each row is the row itself; every other entry is -1 or a row index that differs from the row's own by at most 256.
All inputs are finite; a program needn't handle non-finite values. No bound on the sum of `footprint` on one device may be relied on, other than what follows from the above.
Results may differ from the reference program's by a relative error of at most 0.017.
Values may be sent and summed in bfloat16 or wider, within the bound.
No kernel may reach another device: no remote copies, remote signals or barrier semaphores. Data moves between devices by JAX's collectives and lax.ppermute only.
A program may use at most 64 MiB of HBM per device.

```python
import math
import jax
import jax.numpy as jnp
from jax import lax

C = 64
FD = 256
LAYERS = 6
TAPS = 9
ROW_DEV = 256
BINS = 8
ROWS = 16384


def draw_neighbours(key, part):
    draw_key, second = jax.random.split(key)
    offsets = jax.random.randint(draw_key, (9, ROWS), -ROW_DEV, ROW_DEV + 1)
    tap_index = jnp.arange(9, dtype=jnp.int32)[:, None]
    offsets = jnp.where(tap_index == 4, 0, offsets)
    absent = jax.random.randint(second, (9, ROWS), 0, 8)
    column = jnp.arange(ROWS, dtype=jnp.int32)[None, :]
    target = column + offsets
    retained = (target >= 0) & (target < ROWS) & ((absent > 0) | (tap_index == 4))
    return jnp.where(retained, target, -1).astype(jnp.int32)


def plant(drawn, rng, smallest, largest):
    extent = drawn.shape
    index_at = [jax.random.randint(jax.random.fold_in(rng, axis), (), 0, extent[axis]) for axis in range(len(extent))]
    drawn = drawn.at[tuple(index_at)].set(smallest)
    longest = extent.index(max(extent))
    index_at[longest] = (index_at[longest] + 1) % extent[longest]
    return drawn.at[tuple(index_at)].set(largest)


def block_levels(key, shape, shards, smallest, high):
    level, own = 1.0, jax.random.fold_in(key, 6)
    for position, parts in shards:
        heights = jnp.exp(jax.random.uniform(jax.random.fold_in(own, position), (parts,), jnp.float32, smallest / len(shards), high / len(shards)))
        level = level * jnp.repeat(heights, shape[position] // parts).reshape([-1 if axis == position else 1 for axis in range(len(shape))])
    return level


def gaussian(stream_key, shape, deviation, most, pieces=(), held_as=jnp.bfloat16):
    factor_of = block_levels(stream_key, shape, pieces, -0.22, 0.18) if pieces else 1.0
    result = jax.random.normal(stream_key, shape, jnp.float32) * deviation * factor_of
    return jnp.minimum(jnp.maximum(result, -most), most).astype(held_as)


def setup_inputs(seed: int = 0) -> dict:
    seeds = jax.random.split(jax.random.key(seed), 8)
    sky_maps = gaussian(seeds[0], (BINS, C, ROWS), 1.0, 6.0, ((0, 8), (2, 64)))
    footprint = plant((jax.random.randint(seeds[1], (BINS, ROWS), 0, 4) < 3).astype(jnp.int32), jax.random.fold_in(seeds[1], 1), 0, 1)
    neighbours = draw_neighbours(jax.random.fold_in(seeds[7], 71), 0)
    enc_weight = gaussian(seeds[3], (BINS, LAYERS, TAPS, C, C), (18 * C) ** -0.5, 0.1875, ((0, 8),))
    join_weight = gaussian(seeds[4], (FD, BINS * C), (BINS * C) ** -0.5, 0.25, ((1, 8),))
    dec_weight = gaussian(seeds[5], (TAPS, FD, FD), (9 * FD) ** -0.5, 0.125, ((1, 8),))
    cotangent = gaussian(seeds[6], (FD, ROWS), 1.0, 6.0, ((0, 8), (1, 64)))
    return {"sky_maps": sky_maps, "footprint": footprint, "neighbours": neighbours, "enc_weight": enc_weight, "join_weight": join_weight, "dec_weight": dec_weight, "cotangent": cotangent}


def silu_slope(value):
    sigmoid = jax.nn.sigmoid(value)
    return sigmoid * (1.0 + value * (1.0 - sigmoid))

def reference(sky_maps, footprint, neighbours, enc_weight, join_weight, dec_weight, cotangent):
    present = neighbours >= 0
    clamped = jnp.where(present, neighbours, 0).astype(jnp.int32)
    bin_count = sky_maps.shape[0]
    channels = sky_maps.shape[1]
    row_total = sky_maps.shape[2]
    depth = enc_weight.shape[1]

    def pick(source, tap_index):
        gathered = jnp.take(source, clamped[tap_index], axis=1)
        return jnp.where(present[tap_index][None, :], gathered, jnp.zeros((), source.dtype))

    def place(target, contrib, tap_index):
        contrib = jnp.where(present[tap_index][None, :], contrib, 0.0)
        return target.at[:, clamped[tap_index]].add(contrib)
    saved_states = []
    saved_pre = []
    joining = jnp.zeros((join_weight.shape[0], row_total), jnp.float32)
    for bin_index in range(bin_count):
        retained = footprint[bin_index].astype(jnp.float32)[None, :]
        hidden = sky_maps[bin_index]
        states = []
        pres = []
        for layer_index in range(depth):
            preact = jnp.zeros((channels, row_total), jnp.float32)
            for tap_index in range(9):
                preact = preact + jnp.dot(enc_weight[bin_index, layer_index, tap_index], pick(hidden, tap_index), preferred_element_type=jnp.float32)
            states.append(hidden)
            pres.append(preact)
            hidden = (retained * (hidden.astype(jnp.float32) + jax.nn.silu(preact))).astype(jnp.bfloat16)
        saved_states.append(states)
        saved_pre.append(pres)
        joining = joining + jnp.dot(join_weight[:, bin_index * channels:(bin_index + 1) * channels], hidden, preferred_element_type=jnp.float32)
    slope = silu_slope(joining).astype(jnp.bfloat16)
    unit_acc = jnp.zeros((dec_weight.shape[2], row_total), jnp.float32)
    for tap_index in range(9):
        unit_acc = place(unit_acc, jnp.dot(dec_weight[tap_index].T, cotangent, preferred_element_type=jnp.float32), tap_index)
    unit_grad = (unit_acc * slope.astype(jnp.float32)).astype(jnp.bfloat16)
    normalizer = 1.0 / math.sqrt(row_total)
    map_list = []
    weight_list = []
    for bin_index in range(bin_count):
        retained = footprint[bin_index].astype(jnp.float32)[None, :]
        gradient = jnp.dot(join_weight[:, bin_index * channels:(bin_index + 1) * channels].T, unit_grad, preferred_element_type=jnp.float32)
        layer_grads = [None] * depth
        for layer_index in reversed(range(depth)):
            masked = retained * gradient
            act_grad = (masked * silu_slope(saved_pre[bin_index][layer_index])).astype(jnp.bfloat16)
            spread = jnp.zeros((channels, row_total), jnp.float32)
            tap_grads = []
            for tap_index in range(9):
                picked = pick(saved_states[bin_index][layer_index], tap_index)
                tap_grads.append(lax.dot_general(act_grad, picked, (((1,), (1,)), ((), ())), preferred_element_type=jnp.float32))
                spread = place(spread, jnp.dot(enc_weight[bin_index, layer_index, tap_index].T, act_grad, preferred_element_type=jnp.float32), tap_index)
            layer_grads[layer_index] = jnp.stack(tap_grads) * normalizer
            gradient = masked + spread
        map_list.append(gradient.astype(jnp.bfloat16))
        weight_list.append(jnp.stack(layer_grads))
    return (jnp.stack(map_list), jnp.stack(weight_list))
```

```python
import functools
import math

import jax
import jax.numpy as jnp
from jax import lax
from jax.experimental import pallas as pl
from jax.experimental.pallas import tpu as pltpu
from jax.sharding import Mesh, PartitionSpec as P

SKY = ("z", "yh", "core")
QUAD = ("yh", "core")
C = 64
R = 256
TAPS = 9
F32 = jnp.float32
BF16 = jnp.bfloat16
VMEM = pl.BlockSpec(memory_space=pltpu.VMEM)
SMEM = pl.BlockSpec(memory_space=pltpu.SMEM)


def shift(value, by):
    peers = lax.axis_size(SKY)
    return lax.ppermute(value, SKY, [(i, i + by) for i in range(peers) if 0 <= i + by < peers])


def widen(value):
    below = shift(value, 2)
    above = shift(value, -2)
    other = lax.ppermute(jnp.concatenate([value, below, above], axis=0), "core", [(0, 1), (1, 0)])
    return below, above, other


def inner(other, first, even, start, size):
    own = other[start : start + size]
    below = other[first + start : first + start + size]
    above = other[2 * first + start : 2 * first + start + size]
    return jnp.where(even, below, own), jnp.where(even, own, above)


def slope_of(value, sigmoid):
    return sigmoid * (1.0 + value * (1.0 - sigmoid))


def low_onehot(low):
    return (lax.broadcasted_iota(jnp.int32, (R, R), 0) == low).astype(BF16)


def conv(blocks, pos, weight, picked_ref):
    stack = jnp.concatenate(blocks, axis=0)
    for k in range(TAPS):
        if k == 4:
            column = blocks[1]
        else:
            at = pos[k : k + 1]
            block = at >> 8
            found = jnp.dot(stack, low_onehot(at & 255), preferred_element_type=F32)
            column = jnp.where(
                block == 0,
                found[:C],
                jnp.where(block == 1, found[C : 2 * C], jnp.where(block == 2, found[2 * C :], 0.0)),
            ).astype(BF16)
        picked_ref[k * C : (k + 1) * C, :] = column
    return jnp.dot(weight, picked_ref[...], preferred_element_type=F32)


def spread(act, pos, weight, parts):
    terms = lax.dot_general(weight, act, (((0,), (0,)), ((), ())), preferred_element_type=F32)
    total = None
    for k in range(TAPS):
        if k == 4:
            continue
        at = pos[k : k + 1]
        block = at >> 8
        term = terms[k * C : (k + 1) * C].astype(BF16)
        zero = jnp.zeros_like(term)
        sent = jnp.concatenate([jnp.where(block == part, term, zero) for part in parts], axis=0)
        added = lax.dot_general(
            sent, low_onehot(at & 255), (((1,), (1,)), ((), ())), preferred_element_type=F32
        )
        total = added if total is None else total + added
    out = {part: total[i * C : (i + 1) * C] for i, part in enumerate(parts)}
    if 1 in out:
        out[1] = out[1] + terms[4 * C : 5 * C]
    return out


def two_layers(blocks, pos, kept, w_ref, h_ref, picked_ref, slopes_ref, last_ref, scratch):
    middle = []
    for b in (1, 2, 3):
        target = picked_ref.at[0] if b == 2 else scratch.at[b // 2]
        pre = conv(blocks[b - 1 : b + 2], pos[b], w_ref[0], target)
        sigmoid = jax.nn.sigmoid(pre)
        slopes_ref[b - 1] = slope_of(pre, sigmoid)
        middle.append((kept[b] * (blocks[b].astype(F32) + pre * sigmoid)).astype(BF16))
    pre = conv(middle, pos[2], w_ref[1], picked_ref.at[1])
    sigmoid = jax.nn.sigmoid(pre)
    last_ref[...] = slope_of(pre, sigmoid)
    hidden = (kept[2] * (middle[1].astype(F32) + pre * sigmoid)).astype(BF16)
    if h_ref is not None:
        h_ref[...] = hidden
    return hidden


def first_kernel(
    par_ref, x_ref, below_ref, above_ref, other_ref, w_ref,
    h_ref, picked_ref, slopes_ref, last_ref, pos_ref, kept_ref, scratch,
):
    even = par_ref[0] == 0
    size = x_ref.shape[0]
    other = other_ref[...]
    meta_at = size - 16
    meta1, meta3 = inner(other, size, even, meta_at, 16)
    metas = [below_ref[meta_at:, :], meta1, x_ref[meta_at:, :], meta3, above_ref[meta_at:, :]]
    column = lax.broadcasted_iota(jnp.int32, (16, R), 1)
    pos, kept = [], []
    for b, meta in enumerate(metas):
        offset = meta.astype(F32)
        at = jnp.where(offset > 400.0, 768, offset.astype(jnp.int32) + column + R)
        pos_ref[16 * b : 16 * (b + 1), :] = at
        keep = offset[TAPS : TAPS + 1]
        kept_ref[b : b + 1, :] = keep
        pos.append(at)
        kept.append(keep)
    kept_ref[5:8, :] = jnp.zeros((3, R), F32)
    map1, map3 = inner(other, size, even, 0, C)
    blocks = [below_ref[:C, :], map1, x_ref[:C, :], map3, above_ref[:C, :]]
    two_layers(blocks, pos, kept, w_ref, h_ref, picked_ref, slopes_ref, last_ref, scratch)


def read_tables(pos_ref, kept_ref):
    pos = [pos_ref[16 * b : 16 * b + 16, :] for b in range(5)]
    kept = [kept_ref[b : b + 1, :] for b in range(5)]
    return pos, kept


def layers_kernel(
    par_ref, x_ref, below_ref, above_ref, other_ref, w_ref, pos_ref, kept_ref,
    h_ref, picked_ref, slopes_ref, last_ref, scratch,
):
    even = par_ref[0] == 0
    pos, kept = read_tables(pos_ref, kept_ref)
    one, three = inner(other_ref[...], C, even, 0, C)
    blocks = [below_ref[...], one, x_ref[...], three, above_ref[...]]
    two_layers(blocks, pos, kept, w_ref, h_ref, picked_ref, slopes_ref, last_ref, scratch)


def join_kernel(
    par_ref, x_ref, below_ref, above_ref, other_ref, w_ref, pos_ref, kept_ref, joinw_ref, unit_ref,
    share_ref, picked_ref, slopes_ref, last_ref, scratch,
):
    even = par_ref[0] == 0
    pos, kept = read_tables(pos_ref, kept_ref)
    one, three = inner(other_ref[...], C, even, 0, C)
    blocks = [below_ref[...], one, x_ref[...], three, above_ref[...]]
    hidden = two_layers(blocks, pos, kept, w_ref, None, picked_ref, slopes_ref, last_ref, scratch)
    partial = lax.dot_general(
        joinw_ref[...], hidden, (((0,), (0,)), ((), ())), preferred_element_type=F32
    ).astype(BF16)
    count = share_ref.shape[0]
    each = partial.shape[0] // count
    for c in range(count):
        share_ref[c, :each, :] = partial[c * each : (c + 1) * each]
        share_ref[c, each:, :] = unit_ref[c * each : (c + 1) * each, :]


def unit_kernel(par_ref, x_ref, other_ref, pos_ref, dec_ref, unit_ref, scratch):
    even = par_ref[0] == 0
    size = x_ref.shape[0]
    each = size - 16 - C
    one, three = inner(other_ref[...], size, even, C, each)
    sources = [one, x_ref[C : C + each, :], three]
    pos = [pos_ref[16 * b : 16 * b + 16, :] for b in (1, 2, 3)]
    for k in range(TAPS):
        if k == 4:
            scratch[k * each : (k + 1) * each, :] = sources[1]
            continue
        total = None
        for i in range(3):
            at = pos[i][k : k + 1]
            sent = jnp.where((at >> 8) == 2 - i, sources[i], jnp.zeros_like(sources[i]))
            added = lax.dot_general(
                sent, low_onehot(at & 255), (((1,), (1,)), ((), ())), preferred_element_type=F32
            )
            total = added if total is None else total + added
        scratch[k * each : (k + 1) * each, :] = total.astype(BF16)
    unit_ref[...] = jnp.dot(dec_ref[...], scratch[...], preferred_element_type=F32).astype(BF16)


def slope_kernel(parts_ref, out_ref):
    total = parts_ref[0].astype(F32)
    for i in range(1, parts_ref.shape[0]):
        total = total + parts_ref[i].astype(F32)
    each = total.shape[0] // 2
    joined = total[:each]
    slope = slope_of(joined, jax.nn.sigmoid(joined)).astype(BF16).astype(F32)
    grad = (total[each:] * slope).astype(BF16)
    for i in range(out_ref.shape[0]):
        out_ref[i] = grad


def head_kernel(unit_ref, joinw_ref, kept_ref, last_ref, pack_ref, masked_ref):
    gradient = jnp.dot(joinw_ref[...], unit_ref[...], preferred_element_type=F32)
    masked = kept_ref[2:3, :] * gradient
    masked_ref[...] = masked
    pack_ref[:C, :] = (masked * last_ref[...]).astype(BF16)
    pack_ref[C:, :] = masked.astype(BF16)


def weight_grad(act, picked):
    return lax.dot_general(
        act, picked, (((1,), (1,)), ((), ())), preferred_element_type=F32
    ).astype(BF16)


def back_kernel(final, *refs):
    if final:
        (par_ref, x_ref, below_ref, above_ref, other_ref, masked_ref, w_ref, pos_ref, kept_ref,
         picked_ref, slopes_ref, map_ref, grad_ref) = refs
    else:
        (par_ref, x_ref, below_ref, above_ref, other_ref, masked_ref, w_ref, pos_ref, kept_ref,
         picked_ref, slopes_ref, next_ref, pack_ref, out_ref, grad_ref) = refs
    even = par_ref[0] == 0
    pos, kept = read_tables(pos_ref, kept_ref)
    other = other_ref[...]
    act1, act3 = inner(other, 2 * C, even, 0, C)
    mask1, mask3 = inner(other, 2 * C, even, C, C)
    acts = [below_ref[:C, :], act1, x_ref[:C, :], act3, above_ref[:C, :]]
    masked = [mask1.astype(F32), masked_ref[...], mask3.astype(F32)]
    upper = w_ref[1]
    needed = [(2,), (1, 2), (0, 1, 2), (0, 1), (0,)]
    gradient = list(masked)
    for b in range(5):
        for part, value in spread(acts[b], pos[b], upper, needed[b]).items():
            gradient[b + part - 2] = gradient[b + part - 2] + value
    lower = [kept[i + 1] * gradient[i] for i in range(3)]
    low_acts = [(lower[i] * slopes_ref[i]).astype(BF16) for i in range(3)]
    grad_ref[1] = weight_grad(acts[2], picked_ref[1])
    grad_ref[0] = weight_grad(low_acts[1], picked_ref[0])
    result = lower[1]
    for i, part in ((0, 2), (1, 1), (2, 0)):
        result = result + spread(low_acts[i], pos[i + 1], w_ref[0], (part,))[part]
    if final:
        map_ref[...] = result.astype(BF16)
    else:
        out = kept[2] * result
        out_ref[...] = out
        pack_ref[:C, :] = (out * next_ref[...]).astype(BF16)
        pack_ref[C:, :] = out.astype(BF16)


def final_kernel(scale, sum_ref, out_ref):
    for layer in range(out_ref.shape[0]):
        for k in range(TAPS):
            out_ref[layer, k] = sum_ref[layer, :, k * C : (k + 1) * C].astype(F32) * scale


def sds(shape, dtype):
    return jax.ShapeDtypeStruct(shape, dtype)


def call(body, name, ins, outs, scratch=()):
    specs = [spec for spec, _ in ins]
    return pl.pallas_call(
        body,
        name=name,
        in_specs=specs,
        out_specs=[pl.BlockSpec(memory_space=pltpu.VMEM) for _ in outs],
        out_shape=outs,
        scratch_shapes=list(scratch),
    )(*[value for _, value in ins])


def v(value):
    return (VMEM, value)


def reduce_chunks(value, axes, parts):
    got = lax.all_to_all(value.reshape((parts, -1) + value.shape[1:]), axes, 0, 0, tiled=True)
    return jnp.sum(got.astype(F32), axis=0).astype(BF16)


def gather_chunks(value, axes, parts):
    got = lax.all_to_all(
        jnp.broadcast_to(value[None], (parts,) + value.shape), axes, 0, 0, tiled=True
    )
    return got.reshape((-1,) + value.shape[1:])


def per_device(sky_maps, footprint, neighbours, enc_weight, join_weight, dec_weight, cotangent):
    depth = enc_weight.shape[1]
    branches = lax.axis_size("branch")
    peers = lax.axis_size(SKY)
    par = lax.axis_index("core").astype(jnp.int32).reshape(1)
    rows = lax.axis_index(SKY) * R + lax.broadcasted_iota(jnp.int32, (TAPS, R), 1)
    offset = jnp.where(neighbours >= 0, neighbours - rows, 512).astype(BF16)
    pack = jnp.concatenate(
        [sky_maps[0], cotangent, offset, footprint.astype(BF16), jnp.zeros((6, R), BF16)], axis=0
    )
    weights = [
        jnp.transpose(enc_weight[0, i : i + 2], (0, 2, 1, 3)).reshape(2, C, TAPS * C)
        for i in range(0, depth, 2)
    ]
    joinw = join_weight.T
    dec = jnp.transpose(dec_weight, (2, 0, 1)).reshape(dec_weight.shape[2], -1)

    layer_outs = [
        sds((C, R), BF16), sds((2, TAPS * C, R), BF16), sds((3, C, R), F32), sds((C, R), F32),
    ]
    scratch = [pltpu.VMEM((2, TAPS * C, R), BF16)]
    below, above, other = widen(pack)
    hidden, picked, slopes, last, pos, kept = call(
        first_kernel, "layers01",
        [(SMEM, par), v(pack), v(below), v(above), v(other), v(weights[0])],
        layer_outs + [sds((80, R), jnp.int32), sds((8, R), F32)], scratch,
    )
    saved = [(picked, slopes, last)]
    unit = call(
        unit_kernel, "unit",
        [(SMEM, par), v(pack), v(other), v(pos), v(dec)],
        [sds((dec.shape[0], R), BF16)],
        [pltpu.VMEM((TAPS * cotangent.shape[0], R), BF16)],
    )[0]
    for group in range(1, depth // 2):
        below, above, other = widen(hidden)
        ins = [(SMEM, par), v(hidden), v(below), v(above), v(other), v(weights[group]), v(pos), v(kept)]
        if group < depth // 2 - 1:
            hidden, picked, slopes, last = call(layers_kernel, "layers", ins, layer_outs, scratch)
        else:
            share = sds((branches, 2 * (dec.shape[0] // branches), R), BF16)
            share, picked, slopes, last = call(
                join_kernel, "layersjoin", ins + [v(joinw), v(unit)],
                [share] + layer_outs[1:], scratch,
            )
        saved.append((picked, slopes, last))
    parts = lax.all_to_all(share, "branch", 0, 0, tiled=True)
    grads = call(
        slope_kernel, "slope", [v(parts)], [sds((branches, parts.shape[1] // 2, R), BF16)]
    )[0]
    unit_grad = lax.all_to_all(grads, "branch", 0, 0, tiled=True).reshape(-1, R)
    pack, masked = call(
        head_kernel, "head",
        [v(unit_grad), v(joinw), v(kept), v(saved[-1][2])],
        [sds((2 * C, R), BF16), sds((C, R), F32)],
    )
    weight_grads = [None] * (depth // 2)
    for group in reversed(range(depth // 2)):
        below, above, other = widen(pack)
        picked, slopes, _ = saved[group]
        ins = [
            (SMEM, par), v(pack), v(below), v(above), v(other), v(masked), v(weights[group]),
            v(pos), v(kept), v(picked), v(slopes),
        ]
        grad_out = sds((2, C, TAPS * C), BF16)
        if group:
            pack, masked, weight_grads[group] = call(
                functools.partial(back_kernel, False), "back", ins + [v(saved[group - 1][2])],
                [sds((2 * C, R), BF16), sds((C, R), F32), grad_out],
            )
        else:
            map_grads, weight_grads[group] = call(
                functools.partial(back_kernel, True), "backlast", ins, [sds((C, R), BF16), grad_out]
            )
    stacked = jnp.concatenate(weight_grads, axis=0).reshape(depth * C, TAPS * C)
    quads = lax.axis_size(QUAD)
    length = lax.axis_size("z")
    chunk = reduce_chunks(stacked, QUAD, quads)
    chunk = reduce_chunks(chunk, "z", length)
    chunk = gather_chunks(chunk, "z", length)
    total = gather_chunks(chunk, QUAD, quads).reshape(depth, C, TAPS * C)
    summed = call(
        functools.partial(final_kernel, 1.0 / math.sqrt(R * peers)), "final", [v(total)],
        [sds((depth, TAPS, C, C), F32)],
    )[0]
    return map_grads[None], summed[None]


def solution(mesh):
    branches, sky = mesh.devices.shape
    mesh = Mesh(mesh.devices.reshape(branches, sky // 4, 2, 2), ("branch",) + SKY)
    in_specs = (
        P("branch", None, SKY),
        P("branch", SKY),
        P(None, SKY),
        P("branch", None, None, None, None),
        P(None, "branch"),
        P(None, "branch", None),
        P("branch", SKY),
    )
    out_specs = (P("branch", None, SKY), P("branch", None, None, None, None))
    return jax.shard_map(
        per_device, mesh=mesh, in_specs=in_specs, out_specs=out_specs, check_vma=False
    )
```

```python
import functools
import math

import jax
import jax.numpy as jnp
from jax import lax
from jax.experimental import pallas as pl
from jax.experimental.pallas import tpu as pltpu
from jax.sharding import Mesh, PartitionSpec as P

SKY = ("z", "yh", "core")
QUAD = ("yh", "core")
C = 64
R = 256
TAPS = 9
F32 = jnp.float32
BF16 = jnp.bfloat16
VMEM = pl.BlockSpec(memory_space=pltpu.VMEM)
SMEM = pl.BlockSpec(memory_space=pltpu.SMEM)


def shift(value, by):
    peers = lax.axis_size(SKY)
    return lax.ppermute(value, SKY, [(i, i + by) for i in range(peers) if 0 <= i + by < peers])


def widen(value):
    below = shift(value, 2)
    above = shift(value, -2)
    other = lax.ppermute(jnp.concatenate([value, below, above], axis=0), "core", [(0, 1), (1, 0)])
    return below, above, other


def inner(other, first, even, start, size):
    own = other[start : start + size]
    below = other[first + start : first + start + size]
    above = other[2 * first + start : 2 * first + start + size]
    return jnp.where(even, below, own), jnp.where(even, own, above)


def slope_of(value, sigmoid):
    return sigmoid * (1.0 + value * (1.0 - sigmoid))


def low_onehot(low):
    return (lax.broadcasted_iota(jnp.int32, (R, R), 0) == low).astype(BF16)


def conv(blocks, pos, weight, picked_ref):
    stack = jnp.concatenate(blocks, axis=0)
    for k in range(TAPS):
        if k == 4:
            column = blocks[1]
        else:
            at = pos[k : k + 1]
            block = at >> 8
            found = jnp.dot(stack, low_onehot(at & 255), preferred_element_type=F32)
            column = jnp.where(
                block == 0,
                found[:C],
                jnp.where(block == 1, found[C : 2 * C], jnp.where(block == 2, found[2 * C :], 0.0)),
            ).astype(BF16)
        picked_ref[k * C : (k + 1) * C, :] = column
    return jnp.dot(weight, picked_ref[...], preferred_element_type=F32)


def spread(act, pos, weight, parts):
    terms = lax.dot_general(weight, act, (((0,), (0,)), ((), ())), preferred_element_type=F32)
    total = None
    for k in range(TAPS):
        if k == 4:
            continue
        at = pos[k : k + 1]
        block = at >> 8
        term = terms[k * C : (k + 1) * C].astype(BF16)
        zero = jnp.zeros_like(term)
        sent = jnp.concatenate([jnp.where(block == part, term, zero) for part in parts], axis=0)
        added = lax.dot_general(
            sent, low_onehot(at & 255), (((1,), (1,)), ((), ())), preferred_element_type=F32
        )
        total = added if total is None else total + added
    out = {part: total[i * C : (i + 1) * C] for i, part in enumerate(parts)}
    if 1 in out:
        out[1] = out[1] + terms[4 * C : 5 * C]
    return out


def two_layers(blocks, pos, kept, w_ref, h_ref, picked_ref, slopes_ref, last_ref, scratch):
    middle = []
    for b in (1, 2, 3):
        target = picked_ref.at[0] if b == 2 else scratch.at[b // 2]
        pre = conv(blocks[b - 1 : b + 2], pos[b], w_ref[0], target)
        sigmoid = jax.nn.sigmoid(pre)
        slopes_ref[b - 1] = slope_of(pre, sigmoid)
        middle.append((kept[b] * (blocks[b].astype(F32) + pre * sigmoid)).astype(BF16))
    pre = conv(middle, pos[2], w_ref[1], picked_ref.at[1])
    sigmoid = jax.nn.sigmoid(pre)
    last_ref[...] = slope_of(pre, sigmoid)
    hidden = (kept[2] * (middle[1].astype(F32) + pre * sigmoid)).astype(BF16)
    if h_ref is not None:
        h_ref[...] = hidden
    return hidden


def first_kernel(
    par_ref, x_ref, below_ref, above_ref, other_ref, w_ref,
    h_ref, picked_ref, slopes_ref, last_ref, pos_ref, kept_ref, scratch,
):
    even = par_ref[0] == 0
    size = x_ref.shape[0]
    other = other_ref[...]
    meta_at = size - 16
    meta1, meta3 = inner(other, size, even, meta_at, 16)
    metas = [below_ref[meta_at:, :], meta1, x_ref[meta_at:, :], meta3, above_ref[meta_at:, :]]
    column = lax.broadcasted_iota(jnp.int32, (16, R), 1)
    pos, kept = [], []
    for b, meta in enumerate(metas):
        offset = meta.astype(F32)
        at = jnp.where(offset > 400.0, 768, offset.astype(jnp.int32) + column + R)
        pos_ref[16 * b : 16 * (b + 1), :] = at
        keep = offset[TAPS : TAPS + 1]
        kept_ref[b : b + 1, :] = keep
        pos.append(at)
        kept.append(keep)
    kept_ref[5:8, :] = jnp.zeros((3, R), F32)
    map1, map3 = inner(other, size, even, 0, C)
    blocks = [below_ref[:C, :], map1, x_ref[:C, :], map3, above_ref[:C, :]]
    two_layers(blocks, pos, kept, w_ref, h_ref, picked_ref, slopes_ref, last_ref, scratch)


def read_tables(pos_ref, kept_ref):
    pos = [pos_ref[16 * b : 16 * b + 16, :] for b in range(5)]
    kept = [kept_ref[b : b + 1, :] for b in range(5)]
    return pos, kept


def layers_kernel(
    par_ref, x_ref, below_ref, above_ref, other_ref, w_ref, pos_ref, kept_ref,
    h_ref, picked_ref, slopes_ref, last_ref, scratch,
):
    even = par_ref[0] == 0
    pos, kept = read_tables(pos_ref, kept_ref)
    one, three = inner(other_ref[...], C, even, 0, C)
    blocks = [below_ref[...], one, x_ref[...], three, above_ref[...]]
    two_layers(blocks, pos, kept, w_ref, h_ref, picked_ref, slopes_ref, last_ref, scratch)


def last_layers_kernel(
    par_ref, x_ref, below_ref, above_ref, other_ref, w_ref, pos_ref, kept_ref,
    share_ref, picked_ref, slopes_ref, last_ref, scratch,
):
    even = par_ref[0] == 0
    pos, kept = read_tables(pos_ref, kept_ref)
    one, three = inner(other_ref[...], C, even, 0, C)
    blocks = [below_ref[...], one, x_ref[...], three, above_ref[...]]
    hidden = two_layers(blocks, pos, kept, w_ref, None, picked_ref, slopes_ref, last_ref, scratch)
    for i in range(share_ref.shape[0]):
        share_ref[i] = hidden


def pack_kernel(par_ref, maps_ref, cot_ref, near_ref, foot_ref, pack_ref):
    each = cot_ref.shape[0]
    row = par_ref[1] + lax.broadcasted_iota(jnp.int32, (TAPS, R), 1)
    near = near_ref[...]
    offset = jnp.where(near >= 0, near - row, 512).astype(F32)
    meta = jnp.concatenate(
        [offset, foot_ref[...].astype(F32), jnp.zeros((16 - TAPS - 1, R), F32)], axis=0
    )
    pack_ref[:C, :] = maps_ref[...]
    pack_ref[C : C + each, :] = cot_ref[...]
    pack_ref[C + each :, :] = meta.astype(BF16)


def bundle_kernel(par_ref, x_ref, other_ref, joinw_ref, dec_ref, out_ref):
    even = par_ref[0] == 0
    size = x_ref.shape[0]
    each = size - 16 - C
    one, three = inner(other_ref[...], size, even, C, each)
    for i in range(out_ref.shape[0]):
        out_ref[i, :each, :] = one
        out_ref[i, each : 2 * each, :] = x_ref[C : C + each, :]
        out_ref[i, 2 * each : 3 * each, :] = three
        out_ref[i, 3 * each : 3 * each + C, :] = joinw_ref[...]
        out_ref[i, 3 * each + C :, :] = dec_ref[...]


def unit_kernel(got_ref, pos_ref, unit_ref, join_ref):
    count, size, _ = got_ref.shape
    each = (size - C) // (3 + TAPS)
    pos = [pos_ref[16 * b : 16 * b + 16, :] for b in (1, 2, 3)]

    def rows(start, length):
        return jnp.concatenate([got_ref[d, start : start + length, :] for d in range(count)], axis=0)

    sources = [rows(each * i, each) for i in range(3)]
    unit = None
    for k in range(TAPS):
        if k == 4:
            total = sources[1]
        else:
            total = None
            for i in range(3):
                at = pos[i][k : k + 1]
                sent = jnp.where((at >> 8) == 2 - i, sources[i], jnp.zeros_like(sources[i]))
                added = lax.dot_general(
                    sent, low_onehot(at & 255), (((1,), (1,)), ((), ())), preferred_element_type=F32
                )
                total = added if total is None else total + added
            total = total.astype(BF16)
        dec = rows(3 * each + C + each * k, each)
        added = lax.dot_general(dec, total, (((0,), (0,)), ((), ())), preferred_element_type=F32)
        unit = added if unit is None else unit + added
    unit_ref[...] = unit
    join_ref[...] = jnp.transpose(rows(3 * each, C))


def head_kernel(
    hidden_ref, join_ref, unit_ref, joinw_ref, kept_ref, last_ref, pack_ref, masked_ref
):
    count = hidden_ref.shape[0]
    hidden = jnp.concatenate([hidden_ref[d] for d in range(count)], axis=0)
    joined = jnp.dot(join_ref[...], hidden, preferred_element_type=F32)
    slope = slope_of(joined, jax.nn.sigmoid(joined)).astype(BF16).astype(F32)
    unit_grad = (unit_ref[...] * slope).astype(BF16)
    gradient = jnp.dot(joinw_ref[...], unit_grad, preferred_element_type=F32)
    masked = kept_ref[2:3, :] * gradient
    masked_ref[...] = masked
    pack_ref[:C, :] = (masked * last_ref[...]).astype(BF16)
    pack_ref[C:, :] = masked.astype(BF16)


def weight_grad(act, picked):
    return lax.dot_general(
        act, picked, (((1,), (1,)), ((), ())), preferred_element_type=F32
    ).astype(BF16)


def beside_kernel(has_low, *refs):
    if has_low:
        x_ref, w_ref, pos_ref, picked_ref, low_ref, low_picked_ref, own_ref, grad_ref = refs
        grad_ref[...] = jnp.concatenate(
            [weight_grad(low_ref[C : 2 * C, :], low_picked_ref[0]),
             weight_grad(x_ref[:C, :], picked_ref[1])], axis=1,
        )
    else:
        x_ref, w_ref, pos_ref, picked_ref, own_ref, grad_ref = refs
        grad_ref[...] = weight_grad(x_ref[:C, :], picked_ref[1])
    for part, value in spread(x_ref[:C, :], pos_ref[32:48, :], w_ref[1], (0, 1, 2)).items():
        own_ref[part] = value


def upper_layer(
    par_ref, x_ref, below_ref, above_ref, other_ref, masked_ref, own_ref, w_ref, pos_ref, kept_ref,
    slopes_ref,
):
    even = par_ref[0] == 0
    pos, kept = read_tables(pos_ref, kept_ref)
    other = other_ref[...]
    act1, act3 = inner(other, 2 * C, even, 0, C)
    mask1, mask3 = inner(other, 2 * C, even, C, C)
    acts = [below_ref[:C, :], act1, None, act3, above_ref[:C, :]]
    gradient = [mask1.astype(F32), masked_ref[...], mask3.astype(F32)]
    gradient = [gradient[i] + own_ref[i] for i in range(3)]
    needed = [(2,), (1, 2), (), (0, 1), (0,)]
    for b in (0, 1, 3, 4):
        for part, value in spread(acts[b], pos[b], w_ref[1], needed[b]).items():
            gradient[b + part - 2] = gradient[b + part - 2] + value
    lower = [kept[i + 1] * gradient[i] for i in range(3)]
    low_acts = [(lower[i] * slopes_ref[i]).astype(BF16) for i in range(3)]
    return lower, low_acts


def lower_layer(own, low_acts, pos, weight):
    for i, part in ((0, 2), (1, 1), (2, 0)):
        own = own + spread(low_acts[i], pos[i + 1], weight, (part,))[part]
    return own


def back_kernel(
    par_ref, x_ref, below_ref, above_ref, other_ref, masked_ref, own_ref, w_ref, pos_ref, kept_ref,
    slopes_ref, next_ref, pack_ref, out_ref, low_ref,
):
    lower, low_acts = upper_layer(
        par_ref, x_ref, below_ref, above_ref, other_ref, masked_ref, own_ref, w_ref, pos_ref,
        kept_ref, slopes_ref,
    )
    pos, kept = read_tables(pos_ref, kept_ref)
    out = kept[2] * lower_layer(lower[1], low_acts, pos, w_ref[0])
    out_ref[...] = out
    pack_ref[:C, :] = (out * next_ref[...]).astype(BF16)
    pack_ref[C:, :] = out.astype(BF16)
    for i in range(3):
        low_ref[i * C : (i + 1) * C, :] = low_acts[i]


def last_back_kernel(
    par_ref, x_ref, below_ref, above_ref, other_ref, masked_ref, own_ref, w_ref, pos_ref, kept_ref,
    slopes_ref, picked_ref, grad5_ref, grad43_ref, grad21_ref, low_ref, out_ref, grads_ref,
):
    lower, low_acts = upper_layer(
        par_ref, x_ref, below_ref, above_ref, other_ref, masked_ref, own_ref, w_ref, pos_ref,
        kept_ref, slopes_ref,
    )
    out_ref[...] = lower[1]
    for i in range(3):
        low_ref[i * C : (i + 1) * C, :] = low_acts[i]
    grads_ref[:C, :] = grad43_ref[...]
    grads_ref[C : 2 * C, :] = grad21_ref[...]
    grads_ref[2 * C :, :] = jnp.concatenate(
        [weight_grad(low_acts[1], picked_ref[0]), grad5_ref[...]], axis=1
    )


def map_kernel(low_ref, own_ref, w_ref, pos_ref, map_ref):
    low_acts = [low_ref[i * C : (i + 1) * C, :] for i in range(3)]
    pos = [pos_ref[16 * b : 16 * b + 16, :] for b in range(5)]
    map_ref[...] = lower_layer(own_ref[...], low_acts, pos, w_ref[0]).astype(BF16)


def final_kernel(scale, sum_ref, out_ref):
    wide = TAPS * C
    for row, first, second in ((0, 4, 3), (1, 2, 1), (2, 0, 5)):
        for half, layer in ((0, first), (1, second)):
            for k in range(TAPS):
                at = half * wide + k * C
                out_ref[layer, k] = (
                    sum_ref[row * C : (row + 1) * C, at : at + C].astype(F32) * scale
                )


def sds(shape, dtype):
    return jax.ShapeDtypeStruct(shape, dtype)


def call(body, name, ins, outs, scratch=()):
    specs = [spec for spec, _ in ins]
    return pl.pallas_call(
        body,
        name=name,
        in_specs=specs,
        out_specs=[pl.BlockSpec(memory_space=pltpu.VMEM) for _ in outs],
        out_shape=outs,
        scratch_shapes=list(scratch),
    )(*[value for _, value in ins])


def v(value):
    return (VMEM, value)


def exchange(value, axes):
    return lax.all_to_all(value, axes, 0, 0, tiled=True)


def add_up(parts):
    return jnp.sum(parts.astype(F32), axis=0).astype(BF16)


def copies(value, count):
    return jnp.broadcast_to(value[None], (count,) + value.shape)


def sum_over_sky(value, quads, length):
    rows, lanes = value.shape
    chunk = add_up(exchange(value.reshape(quads, rows // quads, lanes), QUAD))
    tiles = (rows // quads // 8) * (lanes // 128)
    each = -(-tiles // length)
    chunk = chunk.reshape(rows // quads // 8, 8, lanes // 128, 128).transpose(0, 2, 1, 3)
    chunk = jnp.pad(chunk.reshape(tiles, 8, 128), ((0, each * length - tiles), (0, 0), (0, 0)))
    chunk = add_up(exchange(chunk.reshape(length, each, 8, 128), "z"))
    chunk = exchange(copies(chunk, length), "z").reshape(each * length, 8, 128)[:tiles]
    chunk = chunk.reshape(rows // quads // 8, lanes // 128, 8, 128).transpose(0, 2, 1, 3)
    return exchange(copies(chunk.reshape(rows // quads, lanes), quads), QUAD).reshape(rows, lanes)


def per_device(sky_maps, footprint, neighbours, enc_weight, join_weight, dec_weight, cotangent):
    depth = enc_weight.shape[1]
    branches = lax.axis_size("branch")
    peers = lax.axis_size(SKY)
    par = jnp.stack([lax.axis_index("core"), lax.axis_index(SKY) * R]).astype(jnp.int32)
    here = (SMEM, par)
    weights = [
        jnp.transpose(enc_weight[0, i : i + 2], (0, 2, 1, 3)).reshape(2, C, TAPS * C)
        for i in range(0, depth, 2)
    ]
    joinw = join_weight.T
    dec = dec_weight.reshape(-1, dec_weight.shape[2])
    each = cotangent.shape[0]
    full = dec.shape[1]
    half = sds((C, R), BF16)
    whole = sds((C, R), F32)
    pack = call(
        pack_kernel, "pack",
        [here, v(sky_maps[0]), v(cotangent), v(neighbours), v(footprint)],
        [sds((C + each + 16, R), BF16)],
    )[0]
    layer_outs = [half, sds((2, TAPS * C, R), BF16), sds((3, C, R), F32), whole]
    scratch = [pltpu.VMEM((2, TAPS * C, R), BF16)]
    below, above, other = widen(pack)
    hidden, picked, slopes, last, pos, kept = call(
        first_kernel, "layers01",
        [here, v(pack), v(below), v(above), v(other), v(weights[0])],
        layer_outs + [sds((80, R), jnp.int32), sds((8, R), F32)], scratch,
    )
    saved = [(picked, slopes, last)]
    bundle = call(
        bundle_kernel, "bundle", [here, v(pack), v(other), v(joinw), v(dec)],
        [sds((branches, 3 * each + C + dec.shape[0], R), BF16)],
    )[0]
    bundle = exchange(bundle, "branch")
    for group in range(1, depth // 2):
        below, above, other = widen(hidden)
        ins = [here, v(hidden), v(below), v(above), v(other), v(weights[group]), v(pos), v(kept)]
        if group < depth // 2 - 1:
            hidden, picked, slopes, last = call(layers_kernel, "layers", ins, layer_outs, scratch)
        else:
            share, picked, slopes, last = call(
                last_layers_kernel, "lastlayers", ins,
                [sds((branches, C, R), BF16)] + layer_outs[1:], scratch,
            )
        saved.append((picked, slopes, last))
    unit, join = call(
        unit_kernel, "unit", [v(bundle), v(pos)],
        [sds((full, R), F32), sds((full, branches * C), BF16)],
    )
    hiddens = exchange(share, "branch")
    pack, masked = call(
        head_kernel, "head",
        [v(hiddens), v(join), v(unit), v(joinw), v(kept), v(saved[-1][2])],
        [sds((2 * C, R), BF16), whole],
    )
    wide = TAPS * C
    grads = []
    low = None
    for group in reversed(range(depth // 2)):
        below, above, other = widen(pack)
        picked, slopes, _ = saved[group]
        beside = [v(pack), v(weights[group]), v(pos), v(picked)]
        if low is not None:
            beside = beside + [v(low), v(saved[group + 1][0])]
        own, grad = call(
            functools.partial(beside_kernel, low is not None), "beside", beside,
            [sds((3, C, R), F32), sds((C, wide if low is None else 2 * wide), BF16)],
        )
        grads.append(grad)
        ins = [
            here, v(pack), v(below), v(above), v(other), v(masked), v(own), v(weights[group]),
            v(pos), v(kept), v(slopes),
        ]
        if group:
            pack, masked, low = call(
                back_kernel, "back", ins + [v(saved[group - 1][2])],
                [sds((2 * C, R), BF16), whole, sds((3 * C, R), BF16)],
            )
        else:
            low, own, stacked = call(
                last_back_kernel, "lastback", ins + [v(picked)] + [v(g) for g in grads],
                [sds((3 * C, R), BF16), whole, sds((3 * C, 2 * wide), BF16)],
            )
    map_grads = call(
        map_kernel, "mapgrad", [v(low), v(own), v(weights[0]), v(pos)], [half]
    )[0]
    total = sum_over_sky(stacked, lax.axis_size(QUAD), lax.axis_size("z"))
    summed = call(
        functools.partial(final_kernel, 1.0 / math.sqrt(R * peers)), "final", [v(total)],
        [sds((depth, TAPS, C, C), F32)],
    )[0]
    return map_grads[None], summed[None]


def solution(mesh):
    branches, sky = mesh.devices.shape
    mesh = Mesh(mesh.devices.reshape(branches, sky // 4, 2, 2), ("branch",) + SKY)
    in_specs = (
        P("branch", None, SKY),
        P("branch", SKY),
        P(None, SKY),
        P("branch", None, None, None, None),
        P(None, "branch"),
        P(None, "branch", None),
        P("branch", SKY),
    )
    out_specs = (P("branch", None, SKY), P("branch", None, None, None, None))
    return jax.shard_map(
        per_device, mesh=mesh, in_specs=in_specs, out_specs=out_specs, check_vma=False
    )
```

```python
import functools
import math

import jax
import jax.numpy as jnp
from jax import lax
from jax.experimental import pallas as pl
from jax.experimental.pallas import tpu as pltpu
from jax.sharding import Mesh, PartitionSpec as P

SKY = ("z", "yh", "core")
QUAD = ("yh", "core")
C = 64
R = 256
TAPS = 9
LIMIT = 16 * 1024 * 1024
F32 = jnp.float32
BF16 = jnp.bfloat16
VMEM = pl.BlockSpec(memory_space=pltpu.VMEM)
SMEM = pl.BlockSpec(memory_space=pltpu.SMEM)
HBM = pl.BlockSpec(memory_space=pltpu.HBM)


def shift(value, by):
    peers = lax.axis_size(SKY)
    return lax.ppermute(value, SKY, [(i, i + by) for i in range(peers) if 0 <= i + by < peers])


def widen(value, after=()):
    below = shift(value, 2)
    above = shift(value, -2)
    rows = value.shape[0]
    stacked = call(
        stack_kernel, "stack",
        [v(value), v(below), v(above)] + [(pl.BlockSpec(memory_space=pl.ANY), x) for x in after],
        [sds((3 * rows, R), BF16)],
    )[0]
    other = lax.ppermute(stacked, "core", [(0, 1), (1, 0)])
    return below, above, other


def stack_kernel(*refs):
    out_ref = refs[-1]
    rows = refs[0].shape[0]
    for i in range(3):
        out_ref[i * rows : (i + 1) * rows, :] = refs[i][...]


def fetch(pairs, sems):
    copies = [pltpu.make_async_copy(src, dst, sems.at[i]) for i, (src, dst) in enumerate(pairs)]
    for copy in copies:
        copy.start()
    for copy in copies:
        copy.wait()


def inner(other, first, even, start, size):
    own = other[start : start + size]
    below = other[first + start : first + start + size]
    above = other[2 * first + start : 2 * first + start + size]
    return jnp.where(even, below, own), jnp.where(even, own, above)


def slope_of(value, sigmoid):
    return sigmoid * (1.0 + value * (1.0 - sigmoid))


def low_onehot(low):
    return (lax.broadcasted_iota(jnp.int32, (R, R), 0) == low).astype(BF16)


def conv(blocks, pos, weight, picked_ref):
    stack = jnp.concatenate(blocks, axis=0)
    for k in range(TAPS):
        if k == 4:
            column = blocks[1]
        else:
            at = pos[k : k + 1]
            block = at >> 8
            found = jnp.dot(stack, low_onehot(at & 255), preferred_element_type=F32)
            column = jnp.where(
                block == 0,
                found[:C],
                jnp.where(block == 1, found[C : 2 * C], jnp.where(block == 2, found[2 * C :], 0.0)),
            ).astype(BF16)
        picked_ref[k * C : (k + 1) * C, :] = column
    return jnp.dot(weight, picked_ref[...], preferred_element_type=F32)


def spread(act, pos, weight, parts):
    terms = lax.dot_general(weight, act, (((0,), (0,)), ((), ())), preferred_element_type=F32)
    total = None
    for k in range(TAPS):
        if k == 4:
            continue
        at = pos[k : k + 1]
        block = at >> 8
        term = terms[k * C : (k + 1) * C].astype(BF16)
        zero = jnp.zeros_like(term)
        sent = jnp.concatenate([jnp.where(block == part, term, zero) for part in parts], axis=0)
        added = lax.dot_general(
            sent, low_onehot(at & 255), (((1,), (1,)), ((), ())), preferred_element_type=F32
        )
        total = added if total is None else total + added
    out = {part: total[i * C : (i + 1) * C] for i, part in enumerate(parts)}
    if 1 in out:
        out[1] = out[1] + terms[4 * C : 5 * C]
    return out


def two_layers(blocks, pos, kept, w_ref, h_ref, picked_ref, slopes_ref, last_ref, scratch):
    middle = []
    for b in (1, 2, 3):
        target = picked_ref.at[0] if b == 2 else scratch.at[b // 2]
        pre = conv(blocks[b - 1 : b + 2], pos[b], w_ref[0], target)
        sigmoid = jax.nn.sigmoid(pre)
        slopes_ref[b - 1] = slope_of(pre, sigmoid)
        middle.append((kept[b] * (blocks[b].astype(F32) + pre * sigmoid)).astype(BF16))
    pre = conv(middle, pos[2], w_ref[1], picked_ref.at[1])
    sigmoid = jax.nn.sigmoid(pre)
    last_ref[...] = slope_of(pre, sigmoid)
    hidden = (kept[2] * (middle[1].astype(F32) + pre * sigmoid)).astype(BF16)
    if h_ref is not None:
        h_ref[...] = hidden
    return hidden


def first_kernel(
    par_ref, x_ref, below_ref, above_ref, other_ref, w_ref,
    h_ref, picked_ref, slopes_ref, last_ref, pos_ref, kept_ref, scratch,
):
    even = par_ref[0] == 0
    size = x_ref.shape[0]
    other = other_ref[...]
    meta_at = size - 16
    meta1, meta3 = inner(other, size, even, meta_at, 16)
    metas = [below_ref[meta_at:, :], meta1, x_ref[meta_at:, :], meta3, above_ref[meta_at:, :]]
    column = lax.broadcasted_iota(jnp.int32, (16, R), 1)
    pos, kept = [], []
    for b, meta in enumerate(metas):
        offset = meta.astype(F32)
        at = jnp.where(offset > 400.0, 768, offset.astype(jnp.int32) + column + R)
        pos_ref[16 * b : 16 * (b + 1), :] = at
        keep = offset[TAPS : TAPS + 1]
        kept_ref[b : b + 1, :] = keep
        pos.append(at)
        kept.append(keep)
    kept_ref[5:8, :] = jnp.zeros((3, R), F32)
    map1, map3 = inner(other, size, even, 0, C)
    blocks = [below_ref[:C, :], map1, x_ref[:C, :], map3, above_ref[:C, :]]
    two_layers(blocks, pos, kept, w_ref, h_ref, picked_ref, slopes_ref, last_ref, scratch)


def read_tables(pos_ref, kept_ref):
    pos = [pos_ref[16 * b : 16 * b + 16, :] for b in range(5)]
    kept = [kept_ref[b : b + 1, :] for b in range(5)]
    return pos, kept


def layers_kernel(
    par_ref, x_ref, below_ref, above_ref, other_ref, w_ref, pos_ref, kept_ref,
    h_ref, picked_ref, slopes_ref, last_ref, scratch,
):
    even = par_ref[0] == 0
    pos, kept = read_tables(pos_ref, kept_ref)
    one, three = inner(other_ref[...], C, even, 0, C)
    blocks = [below_ref[...], one, x_ref[...], three, above_ref[...]]
    two_layers(blocks, pos, kept, w_ref, h_ref, picked_ref, slopes_ref, last_ref, scratch)


def last_layers_kernel(
    par_ref, x_ref, below_ref, above_ref, other_ref, w_ref, pos_ref, kept_ref,
    share_ref, picked_ref, slopes_ref, last_ref, scratch,
):
    even = par_ref[0] == 0
    pos, kept = read_tables(pos_ref, kept_ref)
    one, three = inner(other_ref[...], C, even, 0, C)
    blocks = [below_ref[...], one, x_ref[...], three, above_ref[...]]
    hidden = two_layers(blocks, pos, kept, w_ref, None, picked_ref, slopes_ref, last_ref, scratch)
    for i in range(share_ref.shape[0]):
        share_ref[i] = hidden


def pack_kernel(
    par_ref, maps_hbm, cot_hbm, near_hbm, foot_hbm, pack_ref, near_ref, foot_ref, sems
):
    each = cot_hbm.shape[0]
    fetch(
        [(near_hbm, near_ref), (foot_hbm, foot_ref), (maps_hbm, pack_ref.at[pl.ds(0, C)]),
         (cot_hbm, pack_ref.at[pl.ds(C, each)])], sems,
    )
    row = par_ref[1] + lax.broadcasted_iota(jnp.int32, (TAPS, R), 1)
    near = near_ref[...]
    offset = jnp.where(near >= 0, near - row, 512).astype(F32)
    meta = jnp.concatenate(
        [offset, foot_ref[...].astype(F32), jnp.zeros((16 - TAPS - 1, R), F32)], axis=0
    )
    pack_ref[C + each :, :] = meta.astype(BF16)


def weights_kernel(w_hbm, *refs):
    outs, w_ref, sems = refs[:-2], refs[-2], refs[-1]
    fetch([(w_hbm, w_ref)], sems)
    for group, out_ref in enumerate(outs):
        for i in range(2):
            layer = 2 * group + i
            out_ref[i] = jnp.concatenate([w_ref[layer, k] for k in range(TAPS)], axis=1)


def bundle_kernel(
    par_ref, x_ref, other_ref, joinw_hbm, dec_hbm, _, out_ref, joinw_ref, dec_ref, sems
):
    fetch([(joinw_hbm, joinw_ref), (dec_hbm, dec_ref)], sems)
    even = par_ref[0] == 0
    size = x_ref.shape[0]
    each = size - 16 - C
    one, three = inner(other_ref[...], size, even, C, each)
    for i in range(out_ref.shape[0]):
        out_ref[i, :each, :] = one
        out_ref[i, each : 2 * each, :] = x_ref[C : C + each, :]
        out_ref[i, 2 * each : 3 * each, :] = three
        out_ref[i, 3 * each : 3 * each + C, :] = joinw_ref[...]
        out_ref[i, 3 * each + C :, :] = dec_ref[...]


def unit_kernel(got_ref, pos_ref, unit_ref, join_ref):
    count, size, _ = got_ref.shape
    each = (size - C) // (3 + TAPS)
    pos = [pos_ref[16 * b : 16 * b + 16, :] for b in (1, 2, 3)]

    def rows(start, length):
        return jnp.concatenate([got_ref[d, start : start + length, :] for d in range(count)], axis=0)

    sources = [rows(each * i, each) for i in range(3)]
    unit = None
    for k in range(TAPS):
        if k == 4:
            total = sources[1]
        else:
            total = None
            for i in range(3):
                at = pos[i][k : k + 1]
                sent = jnp.where((at >> 8) == 2 - i, sources[i], jnp.zeros_like(sources[i]))
                added = lax.dot_general(
                    sent, low_onehot(at & 255), (((1,), (1,)), ((), ())), preferred_element_type=F32
                )
                total = added if total is None else total + added
            total = total.astype(BF16)
        dec = rows(3 * each + C + each * k, each)
        added = lax.dot_general(dec, total, (((0,), (0,)), ((), ())), preferred_element_type=F32)
        unit = added if unit is None else unit + added
    unit_ref[...] = unit
    join_ref[...] = jnp.transpose(rows(3 * each, C))


def head_kernel(
    hidden_ref, join_ref, unit_ref, joinw_ref, kept_ref, last_ref, pack_ref, masked_ref
):
    count = hidden_ref.shape[0]
    hidden = jnp.concatenate([hidden_ref[d] for d in range(count)], axis=0)
    joined = jnp.dot(join_ref[...], hidden, preferred_element_type=F32)
    slope = slope_of(joined, jax.nn.sigmoid(joined)).astype(BF16).astype(F32)
    unit_grad = (unit_ref[...] * slope).astype(BF16)
    gradient = jnp.dot(joinw_ref[...], unit_grad, preferred_element_type=F32)
    masked = kept_ref[2:3, :] * gradient
    masked_ref[...] = masked
    pack_ref[:C, :] = (masked * last_ref[...]).astype(BF16)
    pack_ref[C:, :] = masked.astype(BF16)


def weight_grad(act, picked):
    return lax.dot_general(
        act, picked, (((1,), (1,)), ((), ())), preferred_element_type=F32
    ).astype(BF16)


def beside_kernel(has_low, *refs):
    if has_low:
        x_ref, w_ref, pos_ref, picked_ref, low_ref, low_picked_ref, own_ref, grad_ref = refs
        grad_ref[...] = jnp.concatenate(
            [weight_grad(low_ref[C : 2 * C, :], low_picked_ref[0]),
             weight_grad(x_ref[:C, :], picked_ref[1])], axis=1,
        )
    else:
        x_ref, w_ref, pos_ref, picked_ref, own_ref, grad_ref = refs
        grad_ref[...] = weight_grad(x_ref[:C, :], picked_ref[1])
    for part, value in spread(x_ref[:C, :], pos_ref[32:48, :], w_ref[1], (0, 1, 2)).items():
        own_ref[part] = value


def upper_layer(
    par_ref, x_ref, below_ref, above_ref, other_ref, masked_ref, own_ref, w_ref, pos_ref, kept_ref,
    slopes_ref,
):
    even = par_ref[0] == 0
    pos, kept = read_tables(pos_ref, kept_ref)
    other = other_ref[...]
    act1, act3 = inner(other, 2 * C, even, 0, C)
    mask1, mask3 = inner(other, 2 * C, even, C, C)
    acts = [below_ref[:C, :], act1, None, act3, above_ref[:C, :]]
    gradient = [mask1.astype(F32), masked_ref[...], mask3.astype(F32)]
    gradient = [gradient[i] + own_ref[i] for i in range(3)]
    needed = [(2,), (1, 2), (), (0, 1), (0,)]
    for b in (0, 1, 3, 4):
        for part, value in spread(acts[b], pos[b], w_ref[1], needed[b]).items():
            gradient[b + part - 2] = gradient[b + part - 2] + value
    lower = [kept[i + 1] * gradient[i] for i in range(3)]
    low_acts = [(lower[i] * slopes_ref[i]).astype(BF16) for i in range(3)]
    return lower, low_acts


def lower_layer(own, low_acts, pos, weight):
    for i, part in ((0, 2), (1, 1), (2, 0)):
        own = own + spread(low_acts[i], pos[i + 1], weight, (part,))[part]
    return own


def back_kernel(
    par_ref, x_ref, below_ref, above_ref, other_ref, masked_ref, own_ref, w_ref, pos_ref, kept_ref,
    slopes_ref, next_ref, pack_ref, out_ref, low_ref,
):
    lower, low_acts = upper_layer(
        par_ref, x_ref, below_ref, above_ref, other_ref, masked_ref, own_ref, w_ref, pos_ref,
        kept_ref, slopes_ref,
    )
    pos, kept = read_tables(pos_ref, kept_ref)
    out = kept[2] * lower_layer(lower[1], low_acts, pos, w_ref[0])
    out_ref[...] = out
    pack_ref[:C, :] = (out * next_ref[...]).astype(BF16)
    pack_ref[C:, :] = out.astype(BF16)
    for i in range(3):
        low_ref[i * C : (i + 1) * C, :] = low_acts[i]


def last_back_kernel(
    par_ref, x_ref, below_ref, above_ref, other_ref, masked_ref, own_ref, w_ref, pos_ref, kept_ref,
    slopes_ref, picked_ref, grad5_ref, grad43_ref, grad21_ref, low_ref, out_ref, grads_ref,
):
    lower, low_acts = upper_layer(
        par_ref, x_ref, below_ref, above_ref, other_ref, masked_ref, own_ref, w_ref, pos_ref,
        kept_ref, slopes_ref,
    )
    out_ref[...] = lower[1]
    for i in range(3):
        low_ref[i * C : (i + 1) * C, :] = low_acts[i]
    grads_ref[:C, :] = grad43_ref[...]
    grads_ref[C : 2 * C, :] = grad21_ref[...]
    grads_ref[2 * C :, :] = jnp.concatenate(
        [weight_grad(low_acts[1], picked_ref[0]), grad5_ref[...]], axis=1
    )


def map_kernel(low_ref, own_ref, w_ref, pos_ref, map_ref):
    low_acts = [low_ref[i * C : (i + 1) * C, :] for i in range(3)]
    pos = [pos_ref[16 * b : 16 * b + 16, :] for b in range(5)]
    map_ref[...] = lower_layer(own_ref[...], low_acts, pos, w_ref[0]).astype(BF16)


def final_kernel(scale, sum_ref, out_ref):
    wide = TAPS * C
    for row, first, second in ((0, 4, 3), (1, 2, 1), (2, 0, 5)):
        for half, layer in ((0, first), (1, second)):
            for k in range(TAPS):
                at = half * wide + k * C
                out_ref[layer, k] = (
                    sum_ref[row * C : (row + 1) * C, at : at + C].astype(F32) * scale
                )


def sds(shape, dtype):
    return jax.ShapeDtypeStruct(shape, dtype)


def call(body, name, ins, outs, scratch=(), limit=LIMIT):
    specs = [spec for spec, _ in ins]
    return pl.pallas_call(
        body,
        name=name,
        in_specs=specs,
        out_specs=[pl.BlockSpec(memory_space=pltpu.VMEM) for _ in outs],
        out_shape=outs,
        scratch_shapes=list(scratch),
        compiler_params=pltpu.CompilerParams(vmem_limit_bytes=limit),
    )(*[value for _, value in ins])


def v(value):
    return (VMEM, value)


def exchange(value, axes):
    return lax.all_to_all(value, axes, 0, 0, tiled=True)


def add_up(parts):
    return jnp.sum(parts.astype(F32), axis=0).astype(BF16)


def copies(value, count):
    return jnp.broadcast_to(value[None], (count,) + value.shape)


def sum_over_sky(value, quads, length):
    rows, lanes = value.shape
    chunk = add_up(exchange(value.reshape(quads, rows // quads, lanes), QUAD))
    tiles = (rows // quads // 8) * (lanes // 128)
    each = -(-tiles // length)
    chunk = chunk.reshape(rows // quads // 8, 8, lanes // 128, 128).transpose(0, 2, 1, 3)
    chunk = jnp.pad(chunk.reshape(tiles, 8, 128), ((0, each * length - tiles), (0, 0), (0, 0)))
    chunk = add_up(exchange(chunk.reshape(length, each, 8, 128), "z"))
    chunk = exchange(copies(chunk, length), "z").reshape(each * length, 8, 128)[:tiles]
    chunk = chunk.reshape(rows // quads // 8, lanes // 128, 8, 128).transpose(0, 2, 1, 3)
    return exchange(copies(chunk.reshape(rows // quads, lanes), quads), QUAD).reshape(rows, lanes)


def per_device(sky_maps, footprint, neighbours, enc_weight, join_weight, dec_weight, cotangent):
    depth = enc_weight.shape[1]
    branches = lax.axis_size("branch")
    peers = lax.axis_size(SKY)
    par = jnp.stack([lax.axis_index("core"), lax.axis_index(SKY) * R]).astype(jnp.int32)
    here = (SMEM, par)
    dma = pltpu.SemaphoreType.DMA
    weights = call(
        weights_kernel, "weights", [(HBM, enc_weight[0])],
        [sds((2, C, TAPS * C), BF16)] * (depth // 2),
        [pltpu.VMEM(enc_weight.shape[1:], BF16), dma((1,))], None,
    )
    joinw = join_weight.T
    dec = dec_weight.reshape(-1, dec_weight.shape[2])
    each = cotangent.shape[0]
    full = dec.shape[1]
    half = sds((C, R), BF16)
    whole = sds((C, R), F32)
    pack = call(
        pack_kernel, "pack",
        [here, (HBM, sky_maps[0]), (HBM, cotangent), (HBM, neighbours), (HBM, footprint)],
        [sds((C + each + 16, R), BF16)],
        [pltpu.VMEM((TAPS, R), jnp.int32), pltpu.VMEM((1, R), jnp.int32), dma((4,))], None,
    )[0]
    layer_outs = [half, sds((2, TAPS * C, R), BF16), sds((3, C, R), F32), whole]
    scratch = [pltpu.VMEM((2, TAPS * C, R), BF16)]
    below, above, other = widen(pack, [weights[0]])
    hidden, picked, slopes, last, pos, kept = call(
        first_kernel, "layers01",
        [here, v(pack), v(below), v(above), v(other), v(weights[0])],
        layer_outs + [sds((80, R), jnp.int32), sds((8, R), F32)], scratch,
    )
    saved = [(picked, slopes, last)]
    bundle = call(
        bundle_kernel, "bundle",
        [here, v(pack), v(other), (HBM, joinw), (HBM, dec), v(kept)],
        [sds((branches, 3 * each + C + dec.shape[0], R), BF16)],
        [pltpu.VMEM(joinw.shape, BF16), pltpu.VMEM(dec.shape, BF16), dma((2,))],
    )[0]
    bundle = exchange(bundle, "branch")
    for group in range(1, depth // 2):
        below, above, other = widen(hidden)
        ins = [here, v(hidden), v(below), v(above), v(other), v(weights[group]), v(pos), v(kept)]
        if group < depth // 2 - 1:
            hidden, picked, slopes, last = call(layers_kernel, "layers", ins, layer_outs, scratch)
        else:
            share, picked, slopes, last = call(
                last_layers_kernel, "lastlayers", ins,
                [sds((branches, C, R), BF16)] + layer_outs[1:], scratch,
            )
        saved.append((picked, slopes, last))
    unit, join = call(
        unit_kernel, "unit", [v(bundle), v(pos)],
        [sds((full, R), F32), sds((full, branches * C), BF16)], (), None,
    )
    hiddens = exchange(share, "branch")
    pack, masked = call(
        head_kernel, "head",
        [v(hiddens), v(join), v(unit), v(joinw), v(kept), v(saved[-1][2])],
        [sds((2 * C, R), BF16), whole], (), None,
    )
    wide = TAPS * C
    grads = []
    low = None
    for group in reversed(range(depth // 2)):
        picked, slopes, _ = saved[group]
        beside = [v(pack), v(weights[group]), v(pos), v(picked)]
        if low is not None:
            beside = beside + [v(low), v(saved[group + 1][0])]
        own, grad = call(
            functools.partial(beside_kernel, low is not None), "beside", beside,
            [sds((3, C, R), F32), sds((C, wide if low is None else 2 * wide), BF16)],
        )
        grads.append(grad)
        below, above, other = widen(pack, [own])
        ins = [
            here, v(pack), v(below), v(above), v(other), v(masked), v(own), v(weights[group]),
            v(pos), v(kept), v(slopes),
        ]
        if group:
            pack, masked, low = call(
                back_kernel, "back", ins + [v(saved[group - 1][2])],
                [sds((2 * C, R), BF16), whole, sds((3 * C, R), BF16)],
            )
        else:
            low, own, stacked = call(
                last_back_kernel, "lastback", ins + [v(picked)] + [v(g) for g in grads],
                [sds((3 * C, R), BF16), whole, sds((3 * C, 2 * wide), BF16)],
            )
    map_grads = call(
        map_kernel, "mapgrad", [v(low), v(own), v(weights[0]), v(pos)], [half]
    )[0]
    total = sum_over_sky(stacked, lax.axis_size(QUAD), lax.axis_size("z"))
    summed = call(
        functools.partial(final_kernel, 1.0 / math.sqrt(R * peers)), "final", [v(total)],
        [sds((depth, TAPS, C, C), F32)],
    )[0]
    return map_grads[None], summed[None]


def solution(mesh):
    branches, sky = mesh.devices.shape
    mesh = Mesh(mesh.devices.reshape(branches, sky // 4, 2, 2), ("branch",) + SKY)
    in_specs = (
        P("branch", None, SKY),
        P("branch", SKY),
        P(None, SKY),
        P("branch", None, None, None, None),
        P(None, "branch"),
        P(None, "branch", None),
        P("branch", SKY),
    )
    out_specs = (P("branch", None, SKY), P("branch", None, None, None, None))
    return jax.shard_map(
        per_device, mesh=mesh, in_specs=in_specs, out_specs=out_specs, check_vma=False
    )
```

```python
import functools
import math

import jax
import jax.numpy as jnp
from jax import lax
from jax.experimental import pallas as pl
from jax.experimental.pallas import tpu as pltpu
from jax.sharding import Mesh, PartitionSpec as P

SKY = ("z", "yh", "core")
QUAD = ("yh", "core")
C = 64
R = 256
TAPS = 9
LIMIT = 16 * 1024 * 1024
F32 = jnp.float32
BF16 = jnp.bfloat16
VMEM = pl.BlockSpec(memory_space=pltpu.VMEM)
HBM = pl.BlockSpec(memory_space=pltpu.HBM)


def shift(value, by):
    peers = lax.axis_size(SKY)
    return lax.ppermute(value, SKY, [(i, i + by) for i in range(peers) if 0 <= i + by < peers])


def widen(value, after=()):
    below = shift(value, 2)
    above = shift(value, -2)
    rows = value.shape[0]
    stacked = call(
        stack_kernel, "stack",
        [v(value), v(below), v(above)] + [(pl.BlockSpec(memory_space=pl.ANY), x) for x in after],
        [sds((3 * rows, R), BF16)],
    )[0]
    other = lax.ppermute(stacked, "core", [(0, 1), (1, 0)])
    return below, above, other


def stack_kernel(*refs):
    out_ref = refs[-1]
    rows = refs[0].shape[0]
    for i in range(3):
        out_ref[i * rows : (i + 1) * rows, :] = refs[i][...]


def fetch(pairs, sems):
    copies = [pltpu.make_async_copy(src, dst, sems.at[i]) for i, (src, dst) in enumerate(pairs)]
    for copy in copies:
        copy.start()
    for copy in copies:
        copy.wait()


def inner(other, first, even, start, size):
    own = other[start : start + size]
    below = other[first + start : first + start + size]
    above = other[2 * first + start : 2 * first + start + size]
    return jnp.where(even, below, own), jnp.where(even, own, above)


def slope_of(value, sigmoid):
    return sigmoid * (1.0 + value * (1.0 - sigmoid))


def low_onehot(low):
    return (lax.broadcasted_iota(jnp.int32, (R, R), 0) == low).astype(BF16)


def conv(blocks, pos, weight, picked_ref):
    stack = jnp.concatenate(blocks, axis=0)
    for k in range(TAPS):
        if k == 4:
            column = blocks[1]
        else:
            at = pos[k : k + 1]
            block = at >> 8
            found = jnp.dot(stack, low_onehot(at & 255), preferred_element_type=F32)
            column = jnp.where(
                block == 0,
                found[:C],
                jnp.where(block == 1, found[C : 2 * C], jnp.where(block == 2, found[2 * C :], 0.0)),
            ).astype(BF16)
        picked_ref[k * C : (k + 1) * C, :] = column
    return jnp.dot(weight, picked_ref[...], preferred_element_type=F32)


def spread(act, pos, weight, parts):
    terms = lax.dot_general(weight, act, (((0,), (0,)), ((), ())), preferred_element_type=F32)
    total = None
    for k in range(TAPS):
        if k == 4:
            continue
        at = pos[k : k + 1]
        block = at >> 8
        term = terms[k * C : (k + 1) * C].astype(BF16)
        zero = jnp.zeros_like(term)
        sent = jnp.concatenate([jnp.where(block == part, term, zero) for part in parts], axis=0)
        added = lax.dot_general(
            sent, low_onehot(at & 255), (((1,), (1,)), ((), ())), preferred_element_type=F32
        )
        total = added if total is None else total + added
    out = {part: total[i * C : (i + 1) * C] for i, part in enumerate(parts)}
    if 1 in out:
        out[1] = out[1] + terms[4 * C : 5 * C]
    return out


def two_layers(blocks, pos, kept, w_ref, h_ref, picked_ref, slopes_ref, last_ref, scratch):
    middle = []
    for b in (1, 2, 3):
        target = picked_ref.at[0] if b == 2 else scratch.at[b // 2]
        pre = conv(blocks[b - 1 : b + 2], pos[b], w_ref[0], target)
        sigmoid = jax.nn.sigmoid(pre)
        slopes_ref[b - 1] = slope_of(pre, sigmoid)
        middle.append((kept[b] * (blocks[b].astype(F32) + pre * sigmoid)).astype(BF16))
    pre = conv(middle, pos[2], w_ref[1], picked_ref.at[1])
    sigmoid = jax.nn.sigmoid(pre)
    last_ref[...] = slope_of(pre, sigmoid)
    hidden = (kept[2] * (middle[1].astype(F32) + pre * sigmoid)).astype(BF16)
    if h_ref is not None:
        h_ref[...] = hidden
    return hidden


def first_kernel(
    x_ref, below_ref, above_ref, other_ref, w_ref,
    h_ref, picked_ref, slopes_ref, last_ref, pos_ref, kept_ref, scratch,
):
    even = lax.axis_index("core") == 0
    size = x_ref.shape[0]
    other = other_ref[...]
    meta_at = size - 16
    meta1, meta3 = inner(other, size, even, meta_at, 16)
    metas = [below_ref[meta_at:, :], meta1, x_ref[meta_at:, :], meta3, above_ref[meta_at:, :]]
    column = lax.broadcasted_iota(jnp.int32, (16, R), 1)
    pos, kept = [], []
    for b, meta in enumerate(metas):
        offset = meta.astype(F32)
        at = jnp.where(offset > 400.0, 768, offset.astype(jnp.int32) + column + R)
        pos_ref[16 * b : 16 * (b + 1), :] = at
        keep = offset[TAPS : TAPS + 1]
        kept_ref[b : b + 1, :] = keep
        pos.append(at)
        kept.append(keep)
    kept_ref[5:8, :] = jnp.zeros((3, R), F32)
    map1, map3 = inner(other, size, even, 0, C)
    blocks = [below_ref[:C, :], map1, x_ref[:C, :], map3, above_ref[:C, :]]
    two_layers(blocks, pos, kept, w_ref, h_ref, picked_ref, slopes_ref, last_ref, scratch)


def read_tables(pos_ref, kept_ref):
    pos = [pos_ref[16 * b : 16 * b + 16, :] for b in range(5)]
    kept = [kept_ref[b : b + 1, :] for b in range(5)]
    return pos, kept


def layers_kernel(
    x_ref, below_ref, above_ref, other_ref, w_ref, pos_ref, kept_ref,
    h_ref, picked_ref, slopes_ref, last_ref, scratch,
):
    even = lax.axis_index("core") == 0
    pos, kept = read_tables(pos_ref, kept_ref)
    one, three = inner(other_ref[...], C, even, 0, C)
    blocks = [below_ref[...], one, x_ref[...], three, above_ref[...]]
    two_layers(blocks, pos, kept, w_ref, h_ref, picked_ref, slopes_ref, last_ref, scratch)


def last_layers_kernel(
    x_ref, below_ref, above_ref, other_ref, w_ref, pos_ref, kept_ref, joinw_ref, unit_ref,
    share_ref, picked_ref, slopes_ref, last_ref, scratch,
):
    even = lax.axis_index("core") == 0
    pos, kept = read_tables(pos_ref, kept_ref)
    one, three = inner(other_ref[...], C, even, 0, C)
    blocks = [below_ref[...], one, x_ref[...], three, above_ref[...]]
    hidden = two_layers(blocks, pos, kept, w_ref, None, picked_ref, slopes_ref, last_ref, scratch)
    partial = lax.dot_general(
        joinw_ref[...], hidden, (((0,), (0,)), ((), ())), preferred_element_type=F32
    ).astype(BF16)
    count = share_ref.shape[0]
    each = partial.shape[0] // count
    for c in range(count):
        share_ref[c, :each, :] = partial[c * each : (c + 1) * each]
        share_ref[c, each:, :] = unit_ref[c * each : (c + 1) * each, :]


def pack_kernel(
    maps_hbm, cot_hbm, near_hbm, foot_hbm, pack_ref, near_ref, foot_ref, sems
):
    each = cot_hbm.shape[0]
    fetch(
        [(near_hbm, near_ref), (foot_hbm, foot_ref), (maps_hbm, pack_ref.at[pl.ds(0, C)]),
         (cot_hbm, pack_ref.at[pl.ds(C, each)])], sems,
    )
    row = lax.axis_index(SKY) * R + lax.broadcasted_iota(jnp.int32, (TAPS, R), 1)
    near = near_ref[...]
    offset = jnp.where(near >= 0, near - row, 512).astype(F32)
    meta = jnp.concatenate(
        [offset, foot_ref[...].astype(F32), jnp.zeros((16 - TAPS - 1, R), F32)], axis=0
    )
    pack_ref[C + each :, :] = meta.astype(BF16)


def weights_kernel(w_hbm, *refs):
    outs, w_ref, sems = refs[:-2], refs[-2], refs[-1]
    fetch([(w_hbm, w_ref)], sems)
    for group, out_ref in enumerate(outs):
        for i in range(2):
            layer = 2 * group + i
            out_ref[i] = jnp.concatenate([w_ref[layer, k] for k in range(TAPS)], axis=1)


def unit_kernel(x_ref, other_ref, pos_ref, dec_ref, unit_ref, scratch):
    even = lax.axis_index("core") == 0
    size = x_ref.shape[0]
    each = size - 16 - C
    one, three = inner(other_ref[...], size, even, C, each)
    sources = [one, x_ref[C : C + each, :], three]
    pos = [pos_ref[16 * b : 16 * b + 16, :] for b in (1, 2, 3)]
    for k in range(TAPS):
        if k == 4:
            scratch[k * each : (k + 1) * each, :] = sources[1]
            continue
        total = None
        for i in range(3):
            at = pos[i][k : k + 1]
            sent = jnp.where((at >> 8) == 2 - i, sources[i], jnp.zeros_like(sources[i]))
            added = lax.dot_general(
                sent, low_onehot(at & 255), (((1,), (1,)), ((), ())), preferred_element_type=F32
            )
            total = added if total is None else total + added
        scratch[k * each : (k + 1) * each, :] = total.astype(BF16)
    unit_ref[...] = lax.dot_general(
        dec_ref[...], scratch[...], (((0,), (0,)), ((), ())), preferred_element_type=F32
    ).astype(BF16)


def slope_kernel(parts_ref, out_ref):
    total = parts_ref[0].astype(F32)
    for i in range(1, parts_ref.shape[0]):
        total = total + parts_ref[i].astype(F32)
    each = total.shape[0] // 2
    joined = total[:each]
    slope = slope_of(joined, jax.nn.sigmoid(joined)).astype(BF16).astype(F32)
    grad = (total[each:] * slope).astype(BF16)
    for i in range(out_ref.shape[0]):
        out_ref[i] = grad


def head_kernel(unit_ref, joinw_ref, kept_ref, last_ref, pack_ref, masked_ref):
    unit_grad = jnp.concatenate([unit_ref[d] for d in range(unit_ref.shape[0])], axis=0)
    gradient = jnp.dot(joinw_ref[...], unit_grad, preferred_element_type=F32)
    masked = kept_ref[2:3, :] * gradient
    masked_ref[...] = masked
    pack_ref[:C, :] = (masked * last_ref[...]).astype(BF16)
    pack_ref[C:, :] = masked.astype(BF16)


def weight_grad(act, picked):
    return lax.dot_general(
        act, picked, (((1,), (1,)), ((), ())), preferred_element_type=F32
    ).astype(BF16)


def beside_kernel(has_low, *refs):
    if has_low:
        x_ref, w_ref, pos_ref, picked_ref, low_ref, low_picked_ref, own_ref, grad_ref = refs
        grad_ref[...] = jnp.concatenate(
            [weight_grad(low_ref[C : 2 * C, :], low_picked_ref[0]),
             weight_grad(x_ref[:C, :], picked_ref[1])], axis=1,
        )
    else:
        x_ref, w_ref, pos_ref, picked_ref, own_ref, grad_ref = refs
        grad_ref[...] = weight_grad(x_ref[:C, :], picked_ref[1])
    for part, value in spread(x_ref[:C, :], pos_ref[32:48, :], w_ref[1], (0, 1, 2)).items():
        own_ref[part] = value


def upper_layer(
    x_ref, below_ref, above_ref, other_ref, masked_ref, own_ref, w_ref, pos_ref, kept_ref,
    slopes_ref,
):
    even = lax.axis_index("core") == 0
    pos, kept = read_tables(pos_ref, kept_ref)
    other = other_ref[...]
    act1, act3 = inner(other, 2 * C, even, 0, C)
    mask1, mask3 = inner(other, 2 * C, even, C, C)
    acts = [below_ref[:C, :], act1, None, act3, above_ref[:C, :]]
    gradient = [mask1.astype(F32), masked_ref[...], mask3.astype(F32)]
    gradient = [gradient[i] + own_ref[i] for i in range(3)]
    needed = [(2,), (1, 2), (), (0, 1), (0,)]
    for b in (0, 1, 3, 4):
        for part, value in spread(acts[b], pos[b], w_ref[1], needed[b]).items():
            gradient[b + part - 2] = gradient[b + part - 2] + value
    lower = [kept[i + 1] * gradient[i] for i in range(3)]
    low_acts = [(lower[i] * slopes_ref[i]).astype(BF16) for i in range(3)]
    return lower, low_acts


def lower_layer(own, low_acts, pos, weight):
    for i, part in ((0, 2), (1, 1), (2, 0)):
        own = own + spread(low_acts[i], pos[i + 1], weight, (part,))[part]
    return own


def back_kernel(
    x_ref, below_ref, above_ref, other_ref, masked_ref, own_ref, w_ref, pos_ref, kept_ref,
    slopes_ref, next_ref, pack_ref, out_ref, low_ref,
):
    lower, low_acts = upper_layer(
        x_ref, below_ref, above_ref, other_ref, masked_ref, own_ref, w_ref, pos_ref,
        kept_ref, slopes_ref,
    )
    pos, kept = read_tables(pos_ref, kept_ref)
    out = kept[2] * lower_layer(lower[1], low_acts, pos, w_ref[0])
    out_ref[...] = out
    pack_ref[:C, :] = (out * next_ref[...]).astype(BF16)
    pack_ref[C:, :] = out.astype(BF16)
    for i in range(3):
        low_ref[i * C : (i + 1) * C, :] = low_acts[i]


def last_back_kernel(
    x_ref, below_ref, above_ref, other_ref, masked_ref, own_ref, w_ref, pos_ref, kept_ref,
    slopes_ref, picked_ref, grad5_ref, grad43_ref, grad21_ref, low_ref, out_ref, grads_ref,
):
    lower, low_acts = upper_layer(
        x_ref, below_ref, above_ref, other_ref, masked_ref, own_ref, w_ref, pos_ref,
        kept_ref, slopes_ref,
    )
    out_ref[...] = lower[1]
    for i in range(3):
        low_ref[i * C : (i + 1) * C, :] = low_acts[i]
    grads_ref[:C, :] = grad43_ref[...]
    grads_ref[C : 2 * C, :] = grad21_ref[...]
    grads_ref[2 * C :, :] = jnp.concatenate(
        [weight_grad(low_acts[1], picked_ref[0]), grad5_ref[...]], axis=1
    )


def map_kernel(low_ref, own_ref, w_ref, pos_ref, map_ref):
    low_acts = [low_ref[i * C : (i + 1) * C, :] for i in range(3)]
    pos = [pos_ref[16 * b : 16 * b + 16, :] for b in range(5)]
    map_ref[...] = lower_layer(own_ref[...], low_acts, pos, w_ref[0]).astype(BF16)


def final_kernel(scale, sum_ref, out_ref):
    wide = TAPS * C
    for row, first, second in ((0, 4, 3), (1, 2, 1), (2, 0, 5)):
        for half, layer in ((0, first), (1, second)):
            for k in range(TAPS):
                at = half * wide + k * C
                out_ref[layer, k] = (
                    sum_ref[row * C : (row + 1) * C, at : at + C].astype(F32) * scale
                )


def sds(shape, dtype):
    return jax.ShapeDtypeStruct(shape, dtype)


def call(body, name, ins, outs, scratch=(), limit=LIMIT):
    specs = [spec for spec, _ in ins]
    return pl.pallas_call(
        body,
        name=name,
        in_specs=specs,
        out_specs=[pl.BlockSpec(memory_space=pltpu.VMEM) for _ in outs],
        out_shape=outs,
        scratch_shapes=list(scratch),
        compiler_params=pltpu.CompilerParams(vmem_limit_bytes=limit),
    )(*[value for _, value in ins])


def v(value):
    return (VMEM, value)


def exchange(value, axes):
    return lax.all_to_all(value, axes, 0, 0, tiled=True)


def add_up(parts):
    return jnp.sum(parts.astype(F32), axis=0).astype(BF16)


def copies(value, count):
    return jnp.broadcast_to(value[None], (count,) + value.shape)


def sum_over_sky(value, quads, length):
    rows, lanes = value.shape
    chunk = add_up(exchange(value.reshape(quads, rows // quads, lanes), QUAD))
    tiles = (rows // quads // 8) * (lanes // 128)
    each = -(-tiles // length)
    chunk = chunk.reshape(rows // quads // 8, 8, lanes // 128, 128).transpose(0, 2, 1, 3)
    chunk = jnp.pad(chunk.reshape(tiles, 8, 128), ((0, each * length - tiles), (0, 0), (0, 0)))
    chunk = add_up(exchange(chunk.reshape(length, each, 8, 128), "z"))
    chunk = exchange(copies(chunk, length), "z").reshape(each * length, 8, 128)[:tiles]
    chunk = chunk.reshape(rows // quads // 8, lanes // 128, 8, 128).transpose(0, 2, 1, 3)
    return exchange(copies(chunk.reshape(rows // quads, lanes), quads), QUAD).reshape(rows, lanes)


def per_device(sky_maps, footprint, neighbours, enc_weight, join_weight, dec_weight, cotangent):
    depth = enc_weight.shape[1]
    branches = lax.axis_size("branch")
    peers = lax.axis_size(SKY)
    dma = pltpu.SemaphoreType.DMA
    weights = call(
        weights_kernel, "weights", [(HBM, enc_weight[0])],
        [sds((2, C, TAPS * C), BF16)] * (depth // 2),
        [pltpu.VMEM(enc_weight.shape[1:], BF16), dma((1,))],
    )
    joinw = join_weight.T
    dec = dec_weight.reshape(-1, dec_weight.shape[2])
    each = cotangent.shape[0]
    full = dec.shape[1]
    half = sds((C, R), BF16)
    whole = sds((C, R), F32)
    pack = call(
        pack_kernel, "pack",
        [(HBM, sky_maps[0]), (HBM, cotangent), (HBM, neighbours), (HBM, footprint)],
        [sds((C + each + 16, R), BF16)],
        [pltpu.VMEM((TAPS, R), jnp.int32), pltpu.VMEM((1, R), jnp.int32), dma((4,))], None,
    )[0]
    layer_outs = [half, sds((2, TAPS * C, R), BF16), sds((3, C, R), F32), whole]
    scratch = [pltpu.VMEM((2, TAPS * C, R), BF16)]
    below, above, other = widen(pack, [weights[0]])
    hidden, picked, slopes, last, pos, kept = call(
        first_kernel, "layers01",
        [v(pack), v(below), v(above), v(other), v(weights[0])],
        layer_outs + [sds((80, R), jnp.int32), sds((8, R), F32)], scratch,
    )
    saved = [(picked, slopes, last)]
    unit = call(
        unit_kernel, "unit", [v(pack), v(other), v(pos), v(dec)],
        [sds((full, R), BF16)], [pltpu.VMEM((TAPS * each, R), BF16)],
    )[0]
    for group in range(1, depth // 2):
        below, above, other = widen(hidden, [unit] if group == 1 else ())
        ins = [v(hidden), v(below), v(above), v(other), v(weights[group]), v(pos), v(kept)]
        if group < depth // 2 - 1:
            hidden, picked, slopes, last = call(layers_kernel, "layers", ins, layer_outs, scratch)
        else:
            share, picked, slopes, last = call(
                last_layers_kernel, "lastlayers", ins + [v(joinw), v(unit)],
                [sds((branches, 2 * each, R), BF16)] + layer_outs[1:], scratch,
            )
        saved.append((picked, slopes, last))
    parts = exchange(share, "branch")
    mine = call(slope_kernel, "slope", [v(parts)], [sds((branches, each, R), BF16)])[0]
    pack, masked = call(
        head_kernel, "head",
        [v(exchange(mine, "branch")), v(joinw), v(kept), v(saved[-1][2])],
        [sds((2 * C, R), BF16), whole],
    )
    wide = TAPS * C
    grads = []
    low = None
    for group in reversed(range(depth // 2)):
        picked, slopes, _ = saved[group]
        beside = [v(pack), v(weights[group]), v(pos), v(picked)]
        if low is not None:
            beside = beside + [v(low), v(saved[group + 1][0])]
        own, grad = call(
            functools.partial(beside_kernel, low is not None), "beside", beside,
            [sds((3, C, R), F32), sds((C, wide if low is None else 2 * wide), BF16)],
        )
        grads.append(grad)
        below, above, other = widen(pack, [own])
        ins = [
            v(pack), v(below), v(above), v(other), v(masked), v(own), v(weights[group]),
            v(pos), v(kept), v(slopes),
        ]
        if group:
            pack, masked, low = call(
                back_kernel, "back", ins + [v(saved[group - 1][2])],
                [sds((2 * C, R), BF16), whole, sds((3 * C, R), BF16)],
            )
        else:
            low, own, stacked = call(
                last_back_kernel, "lastback", ins + [v(picked)] + [v(g) for g in grads],
                [sds((3 * C, R), BF16), whole, sds((3 * C, 2 * wide), BF16)],
            )
    map_grads = call(
        map_kernel, "mapgrad", [v(low), v(own), v(weights[0]), v(pos)], [half]
    )[0]
    total = sum_over_sky(stacked, lax.axis_size(QUAD), lax.axis_size("z"))
    summed = call(
        functools.partial(final_kernel, 1.0 / math.sqrt(R * peers)), "final", [v(total)],
        [sds((depth, TAPS, C, C), F32)],
    )[0]
    return map_grads[None], summed[None]


def solution(mesh):
    branches, sky = mesh.devices.shape
    mesh = Mesh(mesh.devices.reshape(branches, sky // 4, 2, 2), ("branch",) + SKY)
    in_specs = (
        P("branch", None, SKY),
        P("branch", SKY),
        P(None, SKY),
        P("branch", None, None, None, None),
        P(None, "branch"),
        P(None, "branch", None),
        P("branch", SKY),
    )
    out_specs = (P("branch", None, SKY), P("branch", None, None, None, None))
    return jax.shard_map(
        per_device, mesh=mesh, in_specs=in_specs, out_specs=out_specs, check_vma=False
    )
```

```python
import functools
import math

import jax
import jax.numpy as jnp
from jax import lax
from jax.experimental import pallas as pl
from jax.experimental.pallas import tpu as pltpu
from jax.sharding import Mesh, PartitionSpec as P

SKY = ("z", "yh", "core")
QUAD = ("yh", "core")
C = 64
R = 256
TAPS = 9
LIMIT = 16 * 1024 * 1024
F32 = jnp.float32
BF16 = jnp.bfloat16
VMEM = pl.BlockSpec(memory_space=pltpu.VMEM)
HBM = pl.BlockSpec(memory_space=pltpu.HBM)


def swap_cores(value):
    return lax.ppermute(value, "core", [(0, 1), (1, 0)])


def widen(value, after=()):
    peers = lax.axis_size(SKY)
    pairs = [(i, i + 2) for i in range(0, peers - 2, 2)] + [(i, i - 2) for i in range(3, peers, 2)]
    got = lax.ppermute(value, SKY, pairs)
    if after:
        got = call(
            relay_kernel, "relay",
            [v(got)] + [(pl.BlockSpec(memory_space=pl.ANY), x) for x in after],
            [sds(value.shape, value.dtype)],
        )[0]
    return got, swap_cores(got)


def relay_kernel(*refs):
    refs[-1][...] = refs[0][...]


def ordered(got, other):
    even = lax.axis_index("core") == 0
    return jnp.where(even, got, other), jnp.where(even, other, got)


def own_of(first, second):
    return jnp.where(lax.axis_index("core") == 0, first, second)


def fetch(pairs, sems):
    copies = [pltpu.make_async_copy(src, dst, sems.at[i]) for i, (src, dst) in enumerate(pairs)]
    for copy in copies:
        copy.start()
    for copy in copies:
        copy.wait()


def inner(other, first, even, start, size):
    own = other[start : start + size]
    below = other[first + start : first + start + size]
    above = other[2 * first + start : 2 * first + start + size]
    return jnp.where(even, below, own), jnp.where(even, own, above)


def slope_of(value, sigmoid):
    return sigmoid * (1.0 + value * (1.0 - sigmoid))


def low_onehot(low):
    return (lax.broadcasted_iota(jnp.int32, (R, R), 0) == low).astype(BF16)


def conv(blocks, pos, weight, picked_ref):
    stack = jnp.concatenate(blocks, axis=0)
    for k in range(TAPS):
        if k == 4:
            column = blocks[1]
        else:
            at = pos[k : k + 1]
            block = at >> 8
            found = jnp.dot(stack, low_onehot(at & 255), preferred_element_type=F32)
            column = jnp.where(
                block == 0,
                found[:C],
                jnp.where(block == 1, found[C : 2 * C], jnp.where(block == 2, found[2 * C :], 0.0)),
            ).astype(BF16)
        picked_ref[k * C : (k + 1) * C, :] = column
    return jnp.dot(weight, picked_ref[...], preferred_element_type=F32)


def spread(act, pos, weight, parts):
    terms = lax.dot_general(weight, act, (((0,), (0,)), ((), ())), preferred_element_type=F32)
    total = None
    for k in range(TAPS):
        if k == 4:
            continue
        at = pos[k : k + 1]
        block = at >> 8
        term = terms[k * C : (k + 1) * C].astype(BF16)
        zero = jnp.zeros_like(term)
        sent = jnp.concatenate([jnp.where(block == part, term, zero) for part in parts], axis=0)
        added = lax.dot_general(
            sent, low_onehot(at & 255), (((1,), (1,)), ((), ())), preferred_element_type=F32
        )
        total = added if total is None else total + added
    out = {part: total[i * C : (i + 1) * C] for i, part in enumerate(parts)}
    if 1 in out:
        out[1] = out[1] + terms[4 * C : 5 * C]
    return out


def two_layers(blocks, pos, kept, w_ref, picked_ref, slopes_ref, last_ref, scratch):
    middle = []
    for b in (1, 2, 3, 4):
        target = picked_ref.at[0, b - 2] if b in (2, 3) else scratch.at[b // 4]
        pre = conv(blocks[b - 1 : b + 2], pos[b], w_ref[0], target)
        sigmoid = jax.nn.sigmoid(pre)
        slopes_ref[b - 1] = slope_of(pre, sigmoid)
        middle.append((kept[b] * (blocks[b].astype(F32) + pre * sigmoid)).astype(BF16))
    hidden = []
    for b in (2, 3):
        pre = conv(middle[b - 2 : b + 1], pos[b], w_ref[1], picked_ref.at[1, b - 2])
        sigmoid = jax.nn.sigmoid(pre)
        last_ref[b - 2] = slope_of(pre, sigmoid)
        hidden.append((kept[b] * (middle[b - 1].astype(F32) + pre * sigmoid)).astype(BF16))
    return hidden


def pair_kernel(own_ref, other_ref, out_ref):
    size = own_ref.shape[0]
    own, other = own_ref[...], other_ref[...]
    out_ref[:size, :] = own_of(own, other)
    out_ref[size:, :] = own_of(other, own)


def first_kernel(
    x_ref, got_ref, other_ref, w_ref,
    h_ref, picked_ref, slopes_ref, last_ref, pos_ref, kept_ref, near_pos_ref, near_cot_ref, scratch,
):
    size = x_ref.shape[0] // 2
    below, above = ordered(got_ref[...], other_ref[...])
    packs = [below[:size], below[size:], x_ref[:size, :], x_ref[size:, :], above[:size], above[size:]]
    column = lax.broadcasted_iota(jnp.int32, (16, R), 1)
    pos, kept = [], []
    for b, pack in enumerate(packs):
        offset = pack[size - 16 :].astype(F32)
        at = jnp.where(offset > 400.0, 768, offset.astype(jnp.int32) + column + R)
        pos_ref[16 * b : 16 * (b + 1), :] = at
        keep = offset[TAPS : TAPS + 1]
        kept_ref[b : b + 1, :] = keep
        pos.append(at)
        kept.append(keep)
    kept_ref[6:8, :] = jnp.zeros((2, R), F32)
    each = size - 16 - C
    for i in range(3):
        near_pos_ref[16 * i : 16 * (i + 1), :] = own_of(pos[i + 1], pos[i + 2])
        near_cot_ref[each * i : each * (i + 1), :] = own_of(
            packs[i + 1][C : C + each], packs[i + 2][C : C + each]
        )
    blocks = [pack[:C] for pack in packs]
    hidden = two_layers(blocks, pos, kept, w_ref, picked_ref, slopes_ref, last_ref, scratch)
    for i in range(2):
        h_ref[i * C : (i + 1) * C, :] = hidden[i]


def read_tables(pos_ref, kept_ref):
    pos = [pos_ref[16 * b : 16 * b + 16, :] for b in range(6)]
    kept = [kept_ref[b : b + 1, :] for b in range(6)]
    return pos, kept


def read_blocks(x_ref, got_ref, other_ref):
    below, above = ordered(got_ref[...], other_ref[...])
    return [below[:C], below[C:], x_ref[:C, :], x_ref[C:, :], above[:C], above[C:]]


def layers_kernel(
    x_ref, got_ref, other_ref, w_ref, pos_ref, kept_ref,
    h_ref, picked_ref, slopes_ref, last_ref, scratch,
):
    pos, kept = read_tables(pos_ref, kept_ref)
    blocks = read_blocks(x_ref, got_ref, other_ref)
    hidden = two_layers(blocks, pos, kept, w_ref, picked_ref, slopes_ref, last_ref, scratch)
    for i in range(2):
        h_ref[i * C : (i + 1) * C, :] = hidden[i]


def last_layers_kernel(
    x_ref, got_ref, other_ref, w_ref, pos_ref, kept_ref, joinw_ref, unit_ref,
    share_ref, picked_ref, slopes_ref, last_ref, scratch,
):
    pos, kept = read_tables(pos_ref, kept_ref)
    blocks = read_blocks(x_ref, got_ref, other_ref)
    hidden = two_layers(blocks, pos, kept, w_ref, picked_ref, slopes_ref, last_ref, scratch)
    partial = lax.dot_general(
        joinw_ref[...], own_of(*hidden), (((0,), (0,)), ((), ())), preferred_element_type=F32
    ).astype(BF16)
    count = share_ref.shape[0]
    each = partial.shape[0] // count
    for c in range(count):
        share_ref[c, :each, :] = partial[c * each : (c + 1) * each]
        share_ref[c, each:, :] = unit_ref[c * each : (c + 1) * each, :]


def pack_kernel(
    maps_hbm, cot_hbm, near_hbm, foot_hbm, pack_ref, near_ref, foot_ref, sems
):
    each = cot_hbm.shape[0]
    fetch(
        [(near_hbm, near_ref), (foot_hbm, foot_ref), (maps_hbm, pack_ref.at[pl.ds(0, C)]),
         (cot_hbm, pack_ref.at[pl.ds(C, each)])], sems,
    )
    row = lax.axis_index(SKY) * R + lax.broadcasted_iota(jnp.int32, (TAPS, R), 1)
    near = near_ref[...]
    offset = jnp.where(near >= 0, near - row, 512).astype(F32)
    meta = jnp.concatenate(
        [offset, foot_ref[...].astype(F32), jnp.zeros((16 - TAPS - 1, R), F32)], axis=0
    )
    pack_ref[C + each :, :] = meta.astype(BF16)


def weights_kernel(w_hbm, *refs):
    outs, w_ref, sems = refs[:-2], refs[-2], refs[-1]
    fetch([(w_hbm, w_ref)], sems)
    for group, out_ref in enumerate(outs):
        for i in range(2):
            layer = 2 * group + i
            out_ref[i] = jnp.concatenate([w_ref[layer, k] for k in range(TAPS)], axis=1)


def unit_kernel(cot_ref, pos_ref, dec_ref, unit_ref, scratch):
    each = cot_ref.shape[0] // 3
    sources = [cot_ref[each * i : each * (i + 1), :] for i in range(3)]
    pos = [pos_ref[16 * i : 16 * (i + 1), :] for i in range(3)]
    for k in range(TAPS):
        if k == 4:
            scratch[k * each : (k + 1) * each, :] = sources[1]
            continue
        total = None
        for i in range(3):
            at = pos[i][k : k + 1]
            sent = jnp.where((at >> 8) == 2 - i, sources[i], jnp.zeros_like(sources[i]))
            added = lax.dot_general(
                sent, low_onehot(at & 255), (((1,), (1,)), ((), ())), preferred_element_type=F32
            )
            total = added if total is None else total + added
        scratch[k * each : (k + 1) * each, :] = total.astype(BF16)
    unit_ref[...] = lax.dot_general(
        dec_ref[...], scratch[...], (((0,), (0,)), ((), ())), preferred_element_type=F32
    ).astype(BF16)


def slope_kernel(parts_ref, out_ref):
    total = parts_ref[0].astype(F32)
    for i in range(1, parts_ref.shape[0]):
        total = total + parts_ref[i].astype(F32)
    each = total.shape[0] // 2
    joined = total[:each]
    slope = slope_of(joined, jax.nn.sigmoid(joined)).astype(BF16).astype(F32)
    grad = (total[each:] * slope).astype(BF16)
    for i in range(out_ref.shape[0]):
        out_ref[i] = grad


def head_kernel(unit_ref, joinw_ref, kept_ref, last_ref, pack_ref):
    unit_grad = jnp.concatenate([unit_ref[d] for d in range(unit_ref.shape[0])], axis=0)
    gradient = jnp.dot(joinw_ref[...], unit_grad, preferred_element_type=F32)
    masked = own_of(kept_ref[2:3, :], kept_ref[3:4, :]) * gradient
    pack_ref[:C, :] = (masked * own_of(last_ref[0], last_ref[1])).astype(BF16)
    pack_ref[C:, :] = masked.astype(BF16)


def store_pack(pack_ref, masked_ref, acts, masked):
    for i in range(2):
        pack_ref[i * C : (i + 1) * C, :] = acts[i]
        masked_ref[i] = masked[i]
    pack_ref[2 * C :, :] = own_of(masked[1], masked[0]).astype(BF16)


def top_kernel(own_ref, other_ref, pack_ref, masked_ref):
    own, other = own_ref[...], other_ref[...]
    first, second = own_of(own, other), own_of(other, own)
    store_pack(
        pack_ref, masked_ref, [first[:C], second[:C]],
        [first[C:].astype(F32), second[C:].astype(F32)],
    )


def weight_grad(acts, picked):
    total = None
    for i in range(2):
        added = lax.dot_general(
            own_of(acts[i][: C // 2], acts[i][C // 2 :]), picked[i],
            (((1,), (1,)), ((), ())), preferred_element_type=F32,
        )
        total = added if total is None else total + added
    return total.astype(BF16)


def pair_of(ref):
    return [ref[:C, :], ref[C : 2 * C, :]]


def both(ref, layer):
    return [ref[layer, 0], ref[layer, 1]]


def beside_kernel(has_low, *refs):
    if has_low:
        x_ref, w_ref, pos_ref, picked_ref, low_ref, low_picked_ref, own_ref, grad_ref = refs
        grad_ref[...] = jnp.concatenate(
            [weight_grad(pair_of(low_ref), both(low_picked_ref, 0)),
             weight_grad(pair_of(x_ref), both(picked_ref, 1))], axis=1,
        )
    else:
        x_ref, w_ref, pos_ref, picked_ref, own_ref, grad_ref = refs
        grad_ref[...] = weight_grad(pair_of(x_ref), both(picked_ref, 1))
    first, second = [
        spread(act, pos_ref[16 * b : 16 * b + 16, :], w_ref[1], (0, 1, 2))
        for b, act in zip((2, 3), pair_of(x_ref))
    ]
    own_ref[0] = first[0]
    own_ref[1] = first[1] + second[0]
    own_ref[2] = first[2] + second[1]
    own_ref[3] = second[2]


def upper_layer(
    x_ref, got_ref, other_ref, masked_ref, own_ref, w_ref, pos_ref, kept_ref, slopes_ref
):
    pos, kept = read_tables(pos_ref, kept_ref)
    below, above = ordered(got_ref[...], other_ref[...])
    acts = {0: below[:C], 1: below[C : 2 * C], 4: above[:C], 5: above[C : 2 * C]}
    masked = [
        below[2 * C :].astype(F32), masked_ref[0], masked_ref[1], above[2 * C :].astype(F32)
    ]
    gradient = [masked[i] + own_ref[i] for i in range(4)]
    for b, parts in ((0, (2,)), (1, (1, 2)), (4, (0, 1)), (5, (0,))):
        for part, value in spread(acts[b], pos[b], w_ref[1], parts).items():
            gradient[b + part - 2] = gradient[b + part - 2] + value
    lower = [kept[i + 1] * gradient[i] for i in range(4)]
    low_acts = [(lower[i] * slopes_ref[i]).astype(BF16) for i in range(4)]
    return lower, low_acts


def back_kernel(
    x_ref, got_ref, other_ref, masked_ref, own_ref, w_ref, pos_ref, kept_ref, slopes_ref, next_ref,
    pack_ref, out_ref, low_ref,
):
    lower, low_acts = upper_layer(
        x_ref, got_ref, other_ref, masked_ref, own_ref, w_ref, pos_ref, kept_ref, slopes_ref
    )
    pos, kept = read_tables(pos_ref, kept_ref)
    result = [lower[1], lower[2]]
    for b, parts in ((1, (2,)), (2, (1, 2)), (3, (0, 1)), (4, (0,))):
        for part, value in spread(low_acts[b - 1], pos[b], w_ref[0], parts).items():
            result[b + part - 3] = result[b + part - 3] + value
    masked = [kept[2 + i] * result[i] for i in range(2)]
    acts = [(masked[i] * next_ref[i]).astype(BF16) for i in range(2)]
    store_pack(pack_ref, out_ref, acts, masked)
    for i in range(2):
        low_ref[i * C : (i + 1) * C, :] = low_acts[1 + i]


def last_back_kernel(
    x_ref, got_ref, other_ref, masked_ref, own_ref, w_ref, pos_ref, kept_ref, slopes_ref,
    picked_ref, grad5_ref, grad43_ref, grad21_ref, low_ref, out_ref, keep_ref, send_ref,
):
    lower, low_acts = upper_layer(
        x_ref, got_ref, other_ref, masked_ref, own_ref, w_ref, pos_ref, kept_ref, slopes_ref
    )
    out_ref[...] = own_of(lower[1], lower[2])
    for i in range(3):
        low_ref[i * C : (i + 1) * C, :] = own_of(low_acts[i], low_acts[i + 1])
    last = jnp.concatenate(
        [weight_grad(low_acts[1:3], both(picked_ref, 0)), grad5_ref[...]], axis=1
    )
    middle = grad21_ref[...]
    first = jnp.concatenate([grad43_ref[...], middle[: C // 4]], axis=0)
    second = jnp.concatenate([middle[C // 4 :], last], axis=0)
    low_half = lax.axis_index("yh") == 0
    keep_ref[...] = jnp.where(low_half, first, second)
    send_ref[...] = jnp.where(low_half, second, first)


def map_kernel(low_ref, own_ref, w_ref, pos_ref, map_ref):
    own = own_ref[...]
    for i, part in ((0, 2), (1, 1), (2, 0)):
        act = low_ref[i * C : (i + 1) * C, :]
        own = own + spread(act, pos_ref[16 * i : 16 * (i + 1), :], w_ref[0], (part,))[part]
    map_ref[...] = own.astype(BF16)


def final_kernel(scale, sum_ref, out_ref):
    wide = TAPS * C
    half_rows = C // 2
    for core in range(2):
        rows = jnp.concatenate([sum_ref[core], sum_ref[2 + core]], axis=0).astype(F32) * scale
        for slot, pair in enumerate(((4, 3), (2, 1), (0, 5))):
            for half, layer in enumerate(pair):
                for k in range(TAPS):
                    at = half * wide + k * C
                    out_ref[layer, k, core * half_rows : (core + 1) * half_rows, :] = rows[
                        slot * half_rows : (slot + 1) * half_rows, at : at + C
                    ]


def sds(shape, dtype):
    return jax.ShapeDtypeStruct(shape, dtype)


def call(body, name, ins, outs, scratch=(), limit=LIMIT):
    specs = [spec for spec, _ in ins]
    return pl.pallas_call(
        body,
        name=name,
        in_specs=specs,
        out_specs=[pl.BlockSpec(memory_space=pltpu.VMEM) for _ in outs],
        out_shape=outs,
        scratch_shapes=list(scratch),
        compiler_params=pltpu.CompilerParams(vmem_limit_bytes=limit),
    )(*[value for _, value in ins])


def v(value):
    return (VMEM, value)


def exchange(value, axes):
    return lax.all_to_all(value, axes, 0, 0, tiled=True)


def add_up(parts):
    return jnp.sum(parts.astype(F32), axis=0).astype(BF16)


def copies(value, count):
    return jnp.broadcast_to(value[None], (count,) + value.shape)


def sum_over_sky(keep, send, quads, length):
    rows, lanes = keep.shape
    got = lax.ppermute(send, "yh", [(0, 1), (1, 0)])
    chunk = (keep.astype(F32) + got.astype(F32)).astype(BF16)
    tiles = (rows // 8) * (lanes // 128)
    each = -(-tiles // length)
    chunk = chunk.reshape(rows // 8, 8, lanes // 128, 128).transpose(0, 2, 1, 3)
    chunk = jnp.pad(chunk.reshape(tiles, 8, 128), ((0, each * length - tiles), (0, 0), (0, 0)))
    chunk = add_up(exchange(chunk.reshape(length, each, 8, 128), "z"))
    chunk = exchange(copies(chunk, length), "z").reshape(each * length, 8, 128)[:tiles]
    chunk = chunk.reshape(rows // 8, lanes // 128, 8, 128).transpose(0, 2, 1, 3)
    return exchange(copies(chunk.reshape(rows, lanes), quads), QUAD)


def per_device(sky_maps, footprint, neighbours, enc_weight, join_weight, dec_weight, cotangent):
    depth = enc_weight.shape[1]
    branches = lax.axis_size("branch")
    peers = lax.axis_size(SKY)
    dma = pltpu.SemaphoreType.DMA
    weights = call(
        weights_kernel, "weights", [(HBM, enc_weight[0])],
        [sds((2, C, TAPS * C), BF16)] * (depth // 2),
        [pltpu.VMEM(enc_weight.shape[1:], BF16), dma((1,))],
    )
    joinw = join_weight.T
    dec = dec_weight.reshape(-1, dec_weight.shape[2])
    each = cotangent.shape[0]
    full = dec.shape[1]
    wide = TAPS * C
    size = C + each + 16
    pack = call(
        pack_kernel, "pack",
        [(HBM, sky_maps[0]), (HBM, cotangent), (HBM, neighbours), (HBM, footprint)],
        [sds((size, R), BF16)],
        [pltpu.VMEM((TAPS, R), jnp.int32), pltpu.VMEM((1, R), jnp.int32), dma((4,))], None,
    )[0]
    pack = call(
        pair_kernel, "pair", [v(pack), v(swap_cores(pack))], [sds((2 * size, R), BF16)]
    )[0]
    pair = sds((2, C, R), F32)
    layer_outs = [sds((2 * C, R), BF16), sds((2, 2, wide, R), BF16), sds((4, C, R), F32), pair]
    scratch = [pltpu.VMEM((2, wide, R), BF16)]
    got, other = widen(pack, [weights[0]])
    hidden, picked, slopes, last, pos, kept, near_pos, near_cot = call(
        first_kernel, "layers01", [v(pack), v(got), v(other), v(weights[0])],
        layer_outs
        + [sds((96, R), jnp.int32), sds((8, R), F32), sds((48, R), jnp.int32),
           sds((3 * each, R), BF16)],
        scratch,
    )
    saved = [(picked, slopes, last)]
    unit = call(
        unit_kernel, "unit", [v(near_cot), v(near_pos), v(dec)],
        [sds((full, R), BF16)], [pltpu.VMEM((TAPS * each, R), BF16)],
    )[0]
    for group in range(1, depth // 2):
        got, other = widen(hidden, [unit] if group == 1 else ())
        ins = [v(hidden), v(got), v(other), v(weights[group]), v(pos), v(kept)]
        if group < depth // 2 - 1:
            hidden, picked, slopes, last = call(layers_kernel, "layers", ins, layer_outs, scratch)
        else:
            share, picked, slopes, last = call(
                last_layers_kernel, "lastlayers", ins + [v(joinw), v(unit)],
                [sds((branches, 2 * each, R), BF16)] + layer_outs[1:], scratch,
            )
        saved.append((picked, slopes, last))
    parts = exchange(share, "branch")
    mine = call(slope_kernel, "slope", [v(parts)], [sds((branches, each, R), BF16)])[0]
    top = call(
        head_kernel, "head",
        [v(exchange(mine, "branch")), v(joinw), v(kept), v(saved[-1][2])], [sds((2 * C, R), BF16)],
    )[0]
    pack_outs = [sds((3 * C, R), BF16), pair]
    pack, masked = call(top_kernel, "top", [v(top), v(swap_cores(top))], pack_outs)
    grads = []
    low = None
    for group in reversed(range(depth // 2)):
        picked, slopes, _ = saved[group]
        beside = [v(pack), v(weights[group]), v(pos), v(picked)]
        if low is not None:
            beside = beside + [v(low), v(saved[group + 1][0])]
        own, grad = call(
            functools.partial(beside_kernel, low is not None), "beside", beside,
            [sds((4, C, R), F32), sds((C // 2, wide if low is None else 2 * wide), BF16)],
        )
        grads.append(grad)
        got, other = widen(pack, [own])
        ins = [
            v(pack), v(got), v(other), v(masked), v(own), v(weights[group]), v(pos), v(kept),
            v(slopes),
        ]
        if group:
            pack, masked, low = call(
                back_kernel, "back", ins + [v(saved[group - 1][2])],
                pack_outs + [sds((2 * C, R), BF16)],
            )
        else:
            half = sds((3 * C // 4, 2 * wide), BF16)
            low, own, keep, send = call(
                last_back_kernel, "lastback", ins + [v(picked)] + [v(g) for g in grads],
                [sds((3 * C, R), BF16), sds((C, R), F32), half, half],
            )
    map_grads = call(
        map_kernel, "mapgrad", [v(low), v(own), v(weights[0]), v(near_pos)], [sds((C, R), BF16)]
    )[0]
    total = sum_over_sky(keep, send, lax.axis_size(QUAD), lax.axis_size("z"))
    summed = call(
        functools.partial(final_kernel, 1.0 / math.sqrt(R * peers)), "final", [v(total)],
        [sds((depth, TAPS, C, C), F32)],
    )[0]
    return map_grads[None], summed[None]


def solution(mesh):
    branches, sky = mesh.devices.shape
    mesh = Mesh(mesh.devices.reshape(branches, sky // 4, 2, 2), ("branch",) + SKY)
    in_specs = (
        P("branch", None, SKY),
        P("branch", SKY),
        P(None, SKY),
        P("branch", None, None, None, None),
        P(None, "branch"),
        P(None, "branch", None),
        P("branch", SKY),
    )
    out_specs = (P("branch", None, SKY), P("branch", None, None, None, None))
    return jax.shard_map(
        per_device, mesh=mesh, in_specs=in_specs, out_specs=out_specs, check_vma=False
    )
```

```python
import functools
import math

import jax
import jax.numpy as jnp
from jax import lax
from jax.experimental import pallas as pl
from jax.experimental.pallas import tpu as pltpu
from jax.sharding import Mesh, PartitionSpec as P

SKY = ("z", "yh", "core")
C = 64
R = 256
TAPS = 9
LIMIT = 16 * 1024 * 1024
F32 = jnp.float32
BF16 = jnp.bfloat16
VMEM = pl.BlockSpec(memory_space=pltpu.VMEM)
HBM = pl.BlockSpec(memory_space=pltpu.HBM)


def swap_cores(value):
    return lax.ppermute(value, "core", [(0, 1), (1, 0)])


def widen(value, after=()):
    peers = lax.axis_size(SKY)
    pairs = [(i, i + 2) for i in range(0, peers - 2, 2)] + [(i, i - 2) for i in range(3, peers, 2)]
    got = lax.ppermute(value, SKY, pairs)
    if after:
        got = call(
            relay_kernel, "relay",
            [v(got)] + [(pl.BlockSpec(memory_space=pl.ANY), x) for x in after],
            [sds(value.shape, value.dtype)],
        )[0]
    return got, swap_cores(got)


def relay_kernel(*refs):
    refs[-1][...] = refs[0][...]


def ordered(got, other):
    got, other = got[...], other[...]
    return own_of(got, other), own_of(other, got)


def own_of(first, second):
    return jnp.where(lax.axis_index("core") == 0, first, second)


def fetch(pairs, sems):
    copies = [pltpu.make_async_copy(src, dst, sems.at[i]) for i, (src, dst) in enumerate(pairs)]
    for copy in copies:
        copy.start()
    for copy in copies:
        copy.wait()


def inner(other, first, even, start, size):
    own = other[start : start + size]
    below = other[first + start : first + start + size]
    above = other[2 * first + start : 2 * first + start + size]
    return jnp.where(even, below, own), jnp.where(even, own, above)


def slope_of(value, sigmoid):
    return sigmoid * (1.0 + value * (1.0 - sigmoid))


def low_onehot(low):
    return (lax.broadcasted_iota(jnp.int32, (R, R), 0) == low).astype(BF16)


def conv(blocks, pos, weight, picked_ref):
    stack = jnp.concatenate(blocks, axis=0)
    for k in range(TAPS):
        if k == 4:
            column = blocks[1]
        else:
            at = pos[k : k + 1]
            block = at >> 8
            found = jnp.dot(stack, low_onehot(at & 255), preferred_element_type=F32)
            column = jnp.where(
                block == 0,
                found[:C],
                jnp.where(block == 1, found[C : 2 * C], jnp.where(block == 2, found[2 * C :], 0.0)),
            ).astype(BF16)
        picked_ref[k * C : (k + 1) * C, :] = column
    return jnp.dot(weight, picked_ref[...], preferred_element_type=F32)


def spread(act, pos, weight, parts):
    terms = lax.dot_general(weight, act, (((0,), (0,)), ((), ())), preferred_element_type=F32)
    total = None
    for k in range(TAPS):
        if k == 4:
            continue
        at = pos[k : k + 1]
        block = at >> 8
        term = terms[k * C : (k + 1) * C].astype(BF16)
        zero = jnp.zeros_like(term)
        sent = jnp.concatenate([jnp.where(block == part, term, zero) for part in parts], axis=0)
        added = lax.dot_general(
            sent, low_onehot(at & 255), (((1,), (1,)), ((), ())), preferred_element_type=F32
        )
        total = added if total is None else total + added
    out = {part: total[i * C : (i + 1) * C] for i, part in enumerate(parts)}
    if 1 in out:
        out[1] = out[1] + terms[4 * C : 5 * C]
    return out


def two_layers(blocks, pos, kept, w_ref, picked_ref, slopes_ref, last_ref, scratch):
    middle = []
    for b in (1, 2, 3, 4):
        target = picked_ref.at[0, b - 2] if b in (2, 3) else scratch.at[b // 4]
        pre = conv(blocks[b - 1 : b + 2], pos[b], w_ref[0], target)
        sigmoid = jax.nn.sigmoid(pre)
        slopes_ref[b - 1] = slope_of(pre, sigmoid)
        middle.append((kept[b] * (blocks[b].astype(F32) + pre * sigmoid)).astype(BF16))
    hidden = []
    for b in (2, 3):
        pre = conv(middle[b - 2 : b + 1], pos[b], w_ref[1], picked_ref.at[1, b - 2])
        sigmoid = jax.nn.sigmoid(pre)
        last_ref[b - 2] = slope_of(pre, sigmoid)
        hidden.append((kept[b] * (middle[b - 1].astype(F32) + pre * sigmoid)).astype(BF16))
    return hidden


def pair_kernel(own_ref, other_ref, out_ref, sent_ref):
    size = own_ref.shape[0]
    each = size - 16 - C
    own, other = own_ref[...], other_ref[...]
    first, second = own_of(own, other), own_of(other, own)
    out_ref[:size, :] = first
    out_ref[size:, :] = second
    sent_ref[:C, :] = first[:C]
    sent_ref[C : 2 * C, :] = second[:C]
    sent_ref[2 * C : 2 * C + 16, :] = first[C + each :]
    sent_ref[2 * C + 16 : 2 * C + 32, :] = second[C + each :]
    sent_ref[2 * C + 32 :, :] = own_of(second, first)[C : C + each]


def first_kernel(
    x_ref, got_ref, other_ref, w_ref,
    h_ref, picked_ref, slopes_ref, last_ref, pos_ref, kept_ref, near_pos_ref, near_cot_ref, scratch,
):
    size = x_ref.shape[0] // 2
    below, above = ordered(got_ref, other_ref)
    each = size - 16 - C
    pair = [x_ref[:size, :], x_ref[size:, :]]
    metas = [
        below[2 * C : 2 * C + 16], below[2 * C + 16 : 2 * C + 32], pair[0][C + each :],
        pair[1][C + each :], above[2 * C : 2 * C + 16], above[2 * C + 16 : 2 * C + 32],
    ]
    cots = [below[2 * C + 32 :], pair[0][C : C + each], pair[1][C : C + each], above[2 * C + 32 :]]
    blocks = [below[:C], below[C : 2 * C], pair[0][:C], pair[1][:C], above[:C], above[C : 2 * C]]
    column = lax.broadcasted_iota(jnp.int32, (16, R), 1)
    pos, kept = [], []
    for b, meta in enumerate(metas):
        offset = meta.astype(F32)
        at = jnp.where(offset > 400.0, 768, offset.astype(jnp.int32) + column + R)
        pos_ref[16 * b : 16 * (b + 1), :] = at
        keep = offset[TAPS : TAPS + 1]
        kept_ref[b : b + 1, :] = keep
        pos.append(at)
        kept.append(keep)
    kept_ref[6:8, :] = jnp.zeros((2, R), F32)
    for i in range(3):
        near_pos_ref[16 * i : 16 * (i + 1), :] = own_of(pos[i + 1], pos[i + 2])
        near_cot_ref[each * i : each * (i + 1), :] = own_of(cots[i], cots[i + 1])
    hidden = two_layers(blocks, pos, kept, w_ref, picked_ref, slopes_ref, last_ref, scratch)
    for i in range(2):
        h_ref[i * C : (i + 1) * C, :] = hidden[i]


def read_tables(pos_ref, kept_ref):
    pos = [pos_ref[16 * b : 16 * b + 16, :] for b in range(6)]
    kept = [kept_ref[b : b + 1, :] for b in range(6)]
    return pos, kept


def read_blocks(x_ref, got_ref, other_ref):
    below, above = ordered(got_ref, other_ref)
    return [below[:C], below[C:], x_ref[:C, :], x_ref[C:, :], above[:C], above[C:]]


def layers_kernel(
    x_ref, got_ref, other_ref, w_ref, pos_ref, kept_ref,
    h_ref, picked_ref, slopes_ref, last_ref, scratch,
):
    pos, kept = read_tables(pos_ref, kept_ref)
    blocks = read_blocks(x_ref, got_ref, other_ref)
    hidden = two_layers(blocks, pos, kept, w_ref, picked_ref, slopes_ref, last_ref, scratch)
    for i in range(2):
        h_ref[i * C : (i + 1) * C, :] = hidden[i]


def last_layers_kernel(
    x_ref, got_ref, other_ref, w_ref, pos_ref, kept_ref, joinw_ref, unit_ref,
    share_ref, picked_ref, slopes_ref, last_ref, scratch,
):
    pos, kept = read_tables(pos_ref, kept_ref)
    blocks = read_blocks(x_ref, got_ref, other_ref)
    hidden = two_layers(blocks, pos, kept, w_ref, picked_ref, slopes_ref, last_ref, scratch)
    partial = lax.dot_general(
        joinw_ref[...], own_of(*hidden), (((0,), (0,)), ((), ())), preferred_element_type=F32
    ).astype(BF16)
    count = share_ref.shape[0]
    each = partial.shape[0] // count
    for c in range(count):
        share_ref[c, :each, :] = partial[c * each : (c + 1) * each]
        share_ref[c, each:, :] = unit_ref[c * each : (c + 1) * each, :]


def pack_kernel(
    maps_hbm, cot_hbm, near_hbm, foot_hbm, pack_ref, near_ref, foot_ref, sems
):
    each = cot_hbm.shape[0]
    fetch(
        [(near_hbm, near_ref), (foot_hbm, foot_ref), (maps_hbm, pack_ref.at[pl.ds(0, C)]),
         (cot_hbm, pack_ref.at[pl.ds(C, each)])], sems,
    )
    row = lax.axis_index(SKY) * R + lax.broadcasted_iota(jnp.int32, (TAPS, R), 1)
    near = near_ref[...]
    offset = jnp.where(near >= 0, near - row, 512).astype(F32)
    meta = jnp.concatenate(
        [offset, foot_ref[...].astype(F32), jnp.zeros((16 - TAPS - 1, R), F32)], axis=0
    )
    pack_ref[C + each :, :] = meta.astype(BF16)


def weights_kernel(w_hbm, *refs):
    outs, w_ref, sems = refs[:-2], refs[-2], refs[-1]
    fetch([(w_hbm, w_ref)], sems)
    for group, out_ref in enumerate(outs):
        for i in range(2):
            layer = 2 * group + i
            out_ref[i] = jnp.concatenate([w_ref[layer, k] for k in range(TAPS)], axis=1)


def unit_kernel(cot_ref, pos_ref, dec_ref, unit_ref, scratch):
    each = cot_ref.shape[0] // 3
    sources = [cot_ref[each * i : each * (i + 1), :] for i in range(3)]
    pos = [pos_ref[16 * i : 16 * (i + 1), :] for i in range(3)]
    for k in range(TAPS):
        if k == 4:
            scratch[k * each : (k + 1) * each, :] = sources[1]
            continue
        total = None
        for i in range(3):
            at = pos[i][k : k + 1]
            sent = jnp.where((at >> 8) == 2 - i, sources[i], jnp.zeros_like(sources[i]))
            added = lax.dot_general(
                sent, low_onehot(at & 255), (((1,), (1,)), ((), ())), preferred_element_type=F32
            )
            total = added if total is None else total + added
        scratch[k * each : (k + 1) * each, :] = total.astype(BF16)
    unit_ref[...] = lax.dot_general(
        dec_ref[...], scratch[...], (((0,), (0,)), ((), ())), preferred_element_type=F32
    ).astype(BF16)


def slope_kernel(parts_ref, out_ref):
    total = parts_ref[0].astype(F32)
    for i in range(1, parts_ref.shape[0]):
        total = total + parts_ref[i].astype(F32)
    each = total.shape[0] // 2
    joined = total[:each]
    slope = slope_of(joined, jax.nn.sigmoid(joined)).astype(BF16).astype(F32)
    grad = (total[each:] * slope).astype(BF16)
    for i in range(out_ref.shape[0]):
        out_ref[i] = grad


def head_kernel(unit_ref, joinw_ref, kept_ref, last_ref, pack_ref):
    unit_grad = jnp.concatenate([unit_ref[d] for d in range(unit_ref.shape[0])], axis=0)
    gradient = jnp.dot(joinw_ref[...], unit_grad, preferred_element_type=F32)
    masked = own_of(kept_ref[2:3, :], kept_ref[3:4, :]) * gradient
    pack_ref[:C, :] = (masked * own_of(last_ref[0], last_ref[1])).astype(BF16)
    pack_ref[C:, :] = masked.astype(BF16)


def store_pack(pack_ref, masked_ref, acts, masked):
    for i in range(2):
        pack_ref[i * C : (i + 1) * C, :] = acts[i]
        masked_ref[i] = masked[i]
    pack_ref[2 * C :, :] = own_of(masked[1], masked[0]).astype(BF16)


def top_kernel(own_ref, other_ref, pack_ref, masked_ref):
    own, other = own_ref[...], other_ref[...]
    first, second = own_of(own, other), own_of(other, own)
    store_pack(
        pack_ref, masked_ref, [first[:C], second[:C]],
        [first[C:].astype(F32), second[C:].astype(F32)],
    )


def weight_grad(acts, picked):
    total = None
    for i in range(2):
        added = lax.dot_general(
            own_of(acts[i][: C // 2], acts[i][C // 2 :]), picked[i],
            (((1,), (1,)), ((), ())), preferred_element_type=F32,
        )
        total = added if total is None else total + added
    return total.astype(BF16)


def pair_of(ref):
    return [ref[:C, :], ref[C : 2 * C, :]]


def both(ref, layer):
    return [ref[layer, 0], ref[layer, 1]]


def beside_kernel(has_low, *refs):
    if has_low:
        x_ref, w_ref, pos_ref, picked_ref, low_ref, low_picked_ref, own_ref, grad_ref = refs
        grad_ref[...] = jnp.concatenate(
            [weight_grad(pair_of(low_ref), both(low_picked_ref, 0)),
             weight_grad(pair_of(x_ref), both(picked_ref, 1))], axis=1,
        )
    else:
        x_ref, w_ref, pos_ref, picked_ref, own_ref, grad_ref = refs
        grad_ref[...] = weight_grad(pair_of(x_ref), both(picked_ref, 1))
    first, second = [
        spread(act, pos_ref[16 * b : 16 * b + 16, :], w_ref[1], (0, 1, 2))
        for b, act in zip((2, 3), pair_of(x_ref))
    ]
    own_ref[0] = first[0]
    own_ref[1] = first[1] + second[0]
    own_ref[2] = first[2] + second[1]
    own_ref[3] = second[2]


def upper_layer(
    x_ref, got_ref, other_ref, masked_ref, own_ref, w_ref, pos_ref, kept_ref, slopes_ref
):
    pos, kept = read_tables(pos_ref, kept_ref)
    below, above = ordered(got_ref, other_ref)
    acts = {0: below[:C], 1: below[C : 2 * C], 4: above[:C], 5: above[C : 2 * C]}
    masked = [
        below[2 * C :].astype(F32), masked_ref[0], masked_ref[1], above[2 * C :].astype(F32)
    ]
    gradient = [masked[i] + own_ref[i] for i in range(4)]
    for b, parts in ((0, (2,)), (1, (1, 2)), (4, (0, 1)), (5, (0,))):
        for part, value in spread(acts[b], pos[b], w_ref[1], parts).items():
            gradient[b + part - 2] = gradient[b + part - 2] + value
    lower = [kept[i + 1] * gradient[i] for i in range(4)]
    low_acts = [(lower[i] * slopes_ref[i]).astype(BF16) for i in range(4)]
    return lower, low_acts


def back_kernel(
    x_ref, got_ref, other_ref, masked_ref, own_ref, w_ref, pos_ref, kept_ref, slopes_ref, next_ref,
    pack_ref, out_ref, low_ref,
):
    lower, low_acts = upper_layer(
        x_ref, got_ref, other_ref, masked_ref, own_ref, w_ref, pos_ref, kept_ref, slopes_ref
    )
    pos, kept = read_tables(pos_ref, kept_ref)
    result = [lower[1], lower[2]]
    for b, parts in ((1, (2,)), (2, (1, 2)), (3, (0, 1)), (4, (0,))):
        for part, value in spread(low_acts[b - 1], pos[b], w_ref[0], parts).items():
            result[b + part - 3] = result[b + part - 3] + value
    masked = [kept[2 + i] * result[i] for i in range(2)]
    acts = [(masked[i] * next_ref[i]).astype(BF16) for i in range(2)]
    store_pack(pack_ref, out_ref, acts, masked)
    for i in range(2):
        low_ref[i * C : (i + 1) * C, :] = low_acts[1 + i]


def last_back_kernel(
    x_ref, got_ref, other_ref, masked_ref, own_ref, w_ref, pos_ref, kept_ref, slopes_ref,
    picked_ref, grad5_ref, grad43_ref, grad21_ref, low_ref, out_ref, keep_ref, send_ref,
):
    lower, low_acts = upper_layer(
        x_ref, got_ref, other_ref, masked_ref, own_ref, w_ref, pos_ref, kept_ref, slopes_ref
    )
    out_ref[...] = own_of(lower[1], lower[2])
    for i in range(3):
        low_ref[i * C : (i + 1) * C, :] = own_of(low_acts[i], low_acts[i + 1])
    last = jnp.concatenate(
        [weight_grad(low_acts[1:3], both(picked_ref, 0)), grad5_ref[...]], axis=1
    )
    middle = grad21_ref[...]
    first = jnp.concatenate([grad43_ref[...], middle[: C // 4]], axis=0)
    second = jnp.concatenate([middle[C // 4 :], last], axis=0)
    low_half = lax.axis_index("yh") == 0
    keep_ref[...] = jnp.where(low_half, first, second)
    send_ref[...] = jnp.where(low_half, second, first)


def map_kernel(low_ref, own_ref, w_ref, pos_ref, map_ref, token_ref):
    own = own_ref[...]
    for i, part in ((0, 2), (1, 1), (2, 0)):
        act = low_ref[i * C : (i + 1) * C, :]
        own = own + spread(act, pos_ref[16 * i : 16 * (i + 1), :], w_ref[0], (part,))[part]
    map_ref[...] = own.astype(BF16)
    token_ref[...] = own[:8, :128]


def add_kernel(keep_ref, got_ref, _, out_ref):
    out_ref[...] = (keep_ref[...].astype(F32) + got_ref[...].astype(F32)).astype(BF16)


def rows_kernel(own_ref, got_ref, out_ref):
    rows = own_ref.shape[0]
    low_half = lax.axis_index("yh") == 0
    own, got = own_ref[...], got_ref[...]
    out_ref[:rows, :] = jnp.where(low_half, own, got)
    out_ref[rows:, :] = jnp.where(low_half, got, own)


def final_kernel(scale, own_ref, other_ref, out_ref):
    wide = TAPS * C
    half_rows = C // 2
    for core, sums in enumerate(ordered(own_ref, other_ref)):
        rows = sums.astype(F32) * scale
        for slot, pair in enumerate(((4, 3), (2, 1), (0, 5))):
            for half, layer in enumerate(pair):
                for k in range(TAPS):
                    at = half * wide + k * C
                    out_ref[layer, k, core * half_rows : (core + 1) * half_rows, :] = rows[
                        slot * half_rows : (slot + 1) * half_rows, at : at + C
                    ]


def sds(shape, dtype):
    return jax.ShapeDtypeStruct(shape, dtype)


def call(body, name, ins, outs, scratch=(), limit=LIMIT):
    specs = [spec for spec, _ in ins]
    return pl.pallas_call(
        body,
        name=name,
        in_specs=specs,
        out_specs=[pl.BlockSpec(memory_space=pltpu.VMEM) for _ in outs],
        out_shape=outs,
        scratch_shapes=list(scratch),
        compiler_params=pltpu.CompilerParams(vmem_limit_bytes=limit),
    )(*[value for _, value in ins])


def v(value):
    return (VMEM, value)


def exchange(value, axes):
    return lax.all_to_all(value, axes, 0, 0, tiled=True)


def add_up(parts):
    return jnp.sum(parts.astype(F32), axis=0).astype(BF16)


def copies(value, count):
    return jnp.broadcast_to(value[None], (count,) + value.shape)


def swap_halves(value):
    return lax.ppermute(value, "yh", [(0, 1), (1, 0)])


def sum_over_sky(keep, send, length, after):
    rows, lanes = keep.shape
    out = [sds(keep.shape, BF16)]
    any_space = pl.BlockSpec(memory_space=pl.ANY)
    chunk = call(
        add_kernel, "add", [v(keep), v(swap_halves(send)), (any_space, after)], out
    )[0]
    tiles = (rows // 8) * (lanes // 128)
    each = -(-tiles // length)
    chunk = chunk.reshape(rows // 8, 8, lanes // 128, 128).transpose(0, 2, 1, 3)
    chunk = jnp.pad(chunk.reshape(tiles, 8, 128), ((0, each * length - tiles), (0, 0), (0, 0)))
    chunk = add_up(exchange(chunk.reshape(length, each, 8, 128), "z"))
    chunk = exchange(copies(chunk, length), "z").reshape(each * length, 8, 128)[:tiles]
    chunk = chunk.reshape(rows // 8, lanes // 128, 8, 128).transpose(0, 2, 1, 3)
    chunk = chunk.reshape(rows, lanes)
    return call(
        rows_kernel, "rows", [v(chunk), v(swap_halves(chunk))], [sds((2 * rows, lanes), BF16)]
    )[0]


def per_device(sky_maps, footprint, neighbours, enc_weight, join_weight, dec_weight, cotangent):
    depth = enc_weight.shape[1]
    branches = lax.axis_size("branch")
    peers = lax.axis_size(SKY)
    dma = pltpu.SemaphoreType.DMA
    weights = call(
        weights_kernel, "weights", [(HBM, enc_weight[0])],
        [sds((2, C, TAPS * C), BF16)] * (depth // 2),
        [pltpu.VMEM(enc_weight.shape[1:], BF16), dma((1,))],
    )
    joinw = join_weight.T
    dec = dec_weight.reshape(-1, dec_weight.shape[2])
    each = cotangent.shape[0]
    full = dec.shape[1]
    wide = TAPS * C
    size = C + each + 16
    pack = call(
        pack_kernel, "pack",
        [(HBM, sky_maps[0]), (HBM, cotangent), (HBM, neighbours), (HBM, footprint)],
        [sds((size, R), BF16)],
        [pltpu.VMEM((TAPS, R), jnp.int32), pltpu.VMEM((1, R), jnp.int32), dma((4,))], None,
    )[0]
    pack, sent = call(
        pair_kernel, "pair", [v(pack), v(swap_cores(pack))],
        [sds((2 * size, R), BF16), sds((2 * C + 32 + each, R), BF16)],
    )
    pair = sds((2, C, R), F32)
    layer_outs = [sds((2 * C, R), BF16), sds((2, 2, wide, R), BF16), sds((4, C, R), F32), pair]
    scratch = [pltpu.VMEM((2, wide, R), BF16)]
    got, other = widen(sent, [weights[0]])
    hidden, picked, slopes, last, pos, kept, near_pos, near_cot = call(
        first_kernel, "layers01", [v(pack), v(got), v(other), v(weights[0])],
        layer_outs
        + [sds((96, R), jnp.int32), sds((8, R), F32), sds((48, R), jnp.int32),
           sds((3 * each, R), BF16)],
        scratch,
    )
    saved = [(picked, slopes, last)]
    unit = call(
        unit_kernel, "unit", [v(near_cot), v(near_pos), v(dec)],
        [sds((full, R), BF16)], [pltpu.VMEM((TAPS * each, R), BF16)],
    )[0]
    for group in range(1, depth // 2):
        got, other = widen(hidden, [unit] if group == 1 else ())
        ins = [v(hidden), v(got), v(other), v(weights[group]), v(pos), v(kept)]
        if group < depth // 2 - 1:
            hidden, picked, slopes, last = call(layers_kernel, "layers", ins, layer_outs, scratch)
        else:
            share, picked, slopes, last = call(
                last_layers_kernel, "lastlayers", ins + [v(joinw), v(unit)],
                [sds((branches, 2 * each, R), BF16)] + layer_outs[1:], scratch,
            )
        saved.append((picked, slopes, last))
    parts = exchange(share, "branch")
    mine = call(slope_kernel, "slope", [v(parts)], [sds((branches, each, R), BF16)])[0]
    top = call(
        head_kernel, "head",
        [v(exchange(mine, "branch")), v(joinw), v(kept), v(saved[-1][2])], [sds((2 * C, R), BF16)],
    )[0]
    pack_outs = [sds((3 * C, R), BF16), pair]
    pack, masked = call(top_kernel, "top", [v(top), v(swap_cores(top))], pack_outs)
    grads = []
    low = None
    for group in reversed(range(depth // 2)):
        picked, slopes, _ = saved[group]
        beside = [v(pack), v(weights[group]), v(pos), v(picked)]
        if low is not None:
            beside = beside + [v(low), v(saved[group + 1][0])]
        own, grad = call(
            functools.partial(beside_kernel, low is not None), "beside", beside,
            [sds((4, C, R), F32), sds((C // 2, wide if low is None else 2 * wide), BF16)],
        )
        grads.append(grad)
        got, other = widen(pack, [own])
        ins = [
            v(pack), v(got), v(other), v(masked), v(own), v(weights[group]), v(pos), v(kept),
            v(slopes),
        ]
        if group:
            pack, masked, low = call(
                back_kernel, "back", ins + [v(saved[group - 1][2])],
                pack_outs + [sds((2 * C, R), BF16)],
            )
        else:
            half = sds((3 * C // 4, 2 * wide), BF16)
            low, own, keep, send = call(
                last_back_kernel, "lastback", ins + [v(picked)] + [v(g) for g in grads],
                [sds((3 * C, R), BF16), sds((C, R), F32), half, half],
            )
    map_grads, token = call(
        map_kernel, "mapgrad", [v(low), v(own), v(weights[0]), v(near_pos)],
        [sds((C, R), BF16), sds((8, 128), F32)],
    )
    total = sum_over_sky(keep, send, lax.axis_size("z"), token)
    summed = call(
        functools.partial(final_kernel, 1.0 / math.sqrt(R * peers)), "final",
        [v(total), v(swap_cores(total))],
        [sds((depth, TAPS, C, C), F32)],
    )[0]
    return map_grads[None], summed[None]


def solution(mesh):
    branches, sky = mesh.devices.shape
    mesh = Mesh(mesh.devices.reshape(branches, sky // 4, 2, 2), ("branch",) + SKY)
    in_specs = (
        P("branch", None, SKY),
        P("branch", SKY),
        P(None, SKY),
        P("branch", None, None, None, None),
        P(None, "branch"),
        P(None, "branch", None),
        P("branch", SKY),
    )
    out_specs = (P("branch", None, SKY), P("branch", None, None, None, None))
    return jax.shard_map(
        per_device, mesh=mesh, in_specs=in_specs, out_specs=out_specs, check_vma=False
    )
```

```python
import functools
import math

import jax
import jax.numpy as jnp
from jax import lax
from jax.experimental import pallas as pl
from jax.experimental.pallas import tpu as pltpu
from jax.sharding import Mesh, PartitionSpec as P

SKY = ("z", "yh", "core")
C = 64
R = 256
TAPS = 9
LIMIT = 16 * 1024 * 1024
F32 = jnp.float32
BF16 = jnp.bfloat16
VMEM = pl.BlockSpec(memory_space=pltpu.VMEM)
HBM = pl.BlockSpec(memory_space=pltpu.HBM)


def swap_cores(value):
    return lax.ppermute(value, "core", [(0, 1), (1, 0)])


def widen(value, after=()):
    peers = lax.axis_size(SKY)
    pairs = [(i, i + 2) for i in range(0, peers - 2, 2)] + [(i, i - 2) for i in range(3, peers, 2)]
    got = lax.ppermute(value, SKY, pairs)
    if after:
        got = call(
            relay_kernel, "relay",
            [v(got)] + [(pl.BlockSpec(memory_space=pl.ANY), x) for x in after],
            [sds(value.shape, value.dtype)],
        )[0]
    return got, swap_cores(got)


def relay_kernel(*refs):
    refs[-1][...] = refs[0][...]


def ordered(got, other):
    got, other = got[...], other[...]
    return own_of(got, other), own_of(other, got)


def own_of(first, second):
    return jnp.where(lax.axis_index("core") == 0, first, second)


def fetch(pairs, sems):
    copies = [pltpu.make_async_copy(src, dst, sems.at[i]) for i, (src, dst) in enumerate(pairs)]
    for copy in copies:
        copy.start()
    for copy in copies:
        copy.wait()


def inner(other, first, even, start, size):
    own = other[start : start + size]
    below = other[first + start : first + start + size]
    above = other[2 * first + start : 2 * first + start + size]
    return jnp.where(even, below, own), jnp.where(even, own, above)


def slope_of(value, sigmoid):
    return sigmoid * (1.0 + value * (1.0 - sigmoid))


def low_onehot(low, dim=0):
    return (lax.broadcasted_iota(jnp.int32, (R, R), dim) == low).astype(BF16)


def low_table(tables):
    low = (tables & 255).astype(F32)
    padded = jnp.concatenate([low, jnp.zeros((128 - low.shape[0], R), F32)], axis=0)
    return jnp.transpose(padded).astype(jnp.int32)


def conv(blocks, pos, weight, picked_ref):
    stack = jnp.concatenate(blocks, axis=0)
    for k in range(TAPS):
        if k == 4:
            column = blocks[1]
        else:
            at = pos[k : k + 1]
            block = at >> 8
            found = jnp.dot(stack, low_onehot(at & 255), preferred_element_type=F32)
            column = jnp.where(
                block == 0,
                found[:C],
                jnp.where(block == 1, found[C : 2 * C], jnp.where(block == 2, found[2 * C :], 0.0)),
            ).astype(BF16)
        picked_ref[k * C : (k + 1) * C, :] = column
    return jnp.dot(weight, picked_ref[...], preferred_element_type=F32)


def spread(act, b, pos_ref, low_ref, weight, parts):
    terms = lax.dot_general(weight, act, (((0,), (0,)), ((), ())), preferred_element_type=F32)
    pos = pos_ref[16 * b : 16 * b + 16, :]
    total = None
    for k in range(TAPS):
        if k == 4:
            continue
        block = pos[k : k + 1] >> 8
        term = terms[k * C : (k + 1) * C].astype(BF16)
        zero = jnp.zeros_like(term)
        sent = jnp.concatenate([jnp.where(block == part, term, zero) for part in parts], axis=0)
        low = low_ref[:, 16 * b + k : 16 * b + k + 1]
        added = jnp.dot(sent, low_onehot(low, 1), preferred_element_type=F32)
        total = added if total is None else total + added
    out = {part: total[i * C : (i + 1) * C] for i, part in enumerate(parts)}
    if 1 in out:
        out[1] = out[1] + terms[4 * C : 5 * C]
    return out


def two_layers(blocks, pos, kept, w_ref, picked_ref, slopes_ref, last_ref, scratch):
    middle = []
    for b in (1, 2, 3, 4):
        target = picked_ref.at[0, b - 2] if b in (2, 3) else scratch.at[b // 4]
        pre = conv(blocks[b - 1 : b + 2], pos[b], w_ref[0], target)
        sigmoid = jax.nn.sigmoid(pre)
        slopes_ref[b - 1] = slope_of(pre, sigmoid)
        middle.append((kept[b] * (blocks[b].astype(F32) + pre * sigmoid)).astype(BF16))
    hidden = []
    for b in (2, 3):
        pre = conv(middle[b - 2 : b + 1], pos[b], w_ref[1], picked_ref.at[1, b - 2])
        sigmoid = jax.nn.sigmoid(pre)
        last_ref[b - 2] = slope_of(pre, sigmoid)
        hidden.append((kept[b] * (middle[b - 1].astype(F32) + pre * sigmoid)).astype(BF16))
    return hidden


def pair_kernel(own_ref, other_ref, out_ref, sent_ref):
    size = own_ref.shape[0]
    each = size - 16 - C
    own, other = own_ref[...], other_ref[...]
    first, second = own_of(own, other), own_of(other, own)
    out_ref[:size, :] = first
    out_ref[size:, :] = second
    sent_ref[:C, :] = first[:C]
    sent_ref[C : 2 * C, :] = second[:C]
    sent_ref[2 * C : 2 * C + 16, :] = first[C + each :]
    sent_ref[2 * C + 16 : 2 * C + 32, :] = second[C + each :]
    sent_ref[2 * C + 32 :, :] = own_of(second, first)[C : C + each]


def first_kernel(
    x_ref, got_ref, other_ref, w_ref,
    h_ref, picked_ref, slopes_ref, last_ref, pos_ref, kept_ref, low_ref, near_pos_ref, near_low_ref,
    cot_ref, scratch,
):
    size = x_ref.shape[0] // 2
    below, above = ordered(got_ref, other_ref)
    each = size - 16 - C
    pair = [x_ref[:size, :], x_ref[size:, :]]
    metas = [
        below[2 * C : 2 * C + 16], below[2 * C + 16 : 2 * C + 32], pair[0][C + each :],
        pair[1][C + each :], above[2 * C : 2 * C + 16], above[2 * C + 16 : 2 * C + 32],
    ]
    cots = [below[2 * C + 32 :], pair[0][C : C + each], pair[1][C : C + each], above[2 * C + 32 :]]
    blocks = [below[:C], below[C : 2 * C], pair[0][:C], pair[1][:C], above[:C], above[C : 2 * C]]
    column = lax.broadcasted_iota(jnp.int32, (16, R), 1)
    pos, kept = [], []
    for b, meta in enumerate(metas):
        offset = meta.astype(F32)
        at = jnp.where(offset > 400.0, 768, offset.astype(jnp.int32) + column + R)
        pos_ref[16 * b : 16 * (b + 1), :] = at
        keep = offset[TAPS : TAPS + 1]
        kept_ref[b : b + 1, :] = keep
        pos.append(at)
        kept.append(keep)
    kept_ref[6:8, :] = jnp.zeros((2, R), F32)
    near = jnp.concatenate([own_of(pos[i + 1], pos[i + 2]) for i in range(3)], axis=0)
    near_pos_ref[...] = near
    near_low_ref[...] = low_table(near)
    low_ref[...] = low_table(jnp.concatenate(pos, axis=0))
    for i in range(4):
        cot_ref[each * i : each * (i + 1), :] = cots[i]
    hidden = two_layers(blocks, pos, kept, w_ref, picked_ref, slopes_ref, last_ref, scratch)
    for i in range(2):
        h_ref[i * C : (i + 1) * C, :] = hidden[i]


def read_tables(pos_ref, kept_ref):
    pos = [pos_ref[16 * b : 16 * b + 16, :] for b in range(6)]
    kept = [kept_ref[b : b + 1, :] for b in range(6)]
    return pos, kept


def read_blocks(x_ref, got_ref, other_ref):
    below, above = ordered(got_ref, other_ref)
    return [below[:C], below[C:], x_ref[:C, :], x_ref[C:, :], above[:C], above[C:]]


def layers_kernel(
    x_ref, got_ref, other_ref, w_ref, pos_ref, kept_ref,
    h_ref, picked_ref, slopes_ref, last_ref, scratch,
):
    pos, kept = read_tables(pos_ref, kept_ref)
    blocks = read_blocks(x_ref, got_ref, other_ref)
    hidden = two_layers(blocks, pos, kept, w_ref, picked_ref, slopes_ref, last_ref, scratch)
    for i in range(2):
        h_ref[i * C : (i + 1) * C, :] = hidden[i]


def last_layers_kernel(
    x_ref, got_ref, other_ref, w_ref, pos_ref, kept_ref, joinw_ref, unit_ref,
    share_ref, picked_ref, slopes_ref, last_ref, scratch,
):
    pos, kept = read_tables(pos_ref, kept_ref)
    blocks = read_blocks(x_ref, got_ref, other_ref)
    hidden = two_layers(blocks, pos, kept, w_ref, picked_ref, slopes_ref, last_ref, scratch)
    count = share_ref.shape[0]
    each = share_ref.shape[1] // 4
    for i in range(2):
        partial = lax.dot_general(
            joinw_ref[...], hidden[i], (((0,), (0,)), ((), ())), preferred_element_type=F32
        ).astype(BF16)
        for c in range(count):
            share_ref[c, i * each : (i + 1) * each, :] = partial[c * each : (c + 1) * each]
            share_ref[c, (2 + i) * each : (3 + i) * each, :] = unit_ref[
                i, c * each : (c + 1) * each, :
            ]


def pack_kernel(
    maps_hbm, cot_hbm, near_hbm, foot_hbm, pack_ref, near_ref, foot_ref, sems
):
    each = cot_hbm.shape[0]
    fetch(
        [(near_hbm, near_ref), (foot_hbm, foot_ref), (maps_hbm, pack_ref.at[pl.ds(0, C)]),
         (cot_hbm, pack_ref.at[pl.ds(C, each)])], sems,
    )
    row = lax.axis_index(SKY) * R + lax.broadcasted_iota(jnp.int32, (TAPS, R), 1)
    near = near_ref[...]
    offset = jnp.where(near >= 0, near - row, 512).astype(F32)
    meta = jnp.concatenate(
        [offset, foot_ref[...].astype(F32), jnp.zeros((16 - TAPS - 1, R), F32)], axis=0
    )
    pack_ref[C + each :, :] = meta.astype(BF16)


def weights_kernel(w_hbm, *refs):
    outs, w_ref, sems = refs[:-2], refs[-2], refs[-1]
    fetch([(w_hbm, w_ref)], sems)
    for group, out_ref in enumerate(outs):
        for i in range(2):
            layer = 2 * group + i
            out_ref[i] = jnp.concatenate([w_ref[layer, k] for k in range(TAPS)], axis=1)


def unit_kernel(cot_ref, pos_ref, low_ref, dec_ref, unit_ref, scratch):
    each = cot_ref.shape[0] // 4
    cots = [cot_ref[each * i : each * (i + 1), :] for i in range(4)]
    targets = [(0,), (0, 1), (0, 1), (1,)]
    for k in range(TAPS):
        total = [None, None]
        for i in range(4):
            b = i + 1
            if k == 4:
                if b in (2, 3):
                    scratch[b - 2, k * each : (k + 1) * each, :] = cots[i]
                continue
            block = pos_ref[16 * b + k : 16 * b + k + 1, :] >> 8
            zero = jnp.zeros_like(cots[i])
            sent = jnp.concatenate(
                [jnp.where(block == t + 3 - b, cots[i], zero) for t in targets[i]], axis=0
            )
            low = low_ref[:, 16 * b + k : 16 * b + k + 1]
            added = jnp.dot(sent, low_onehot(low, 1), preferred_element_type=F32)
            for j, t in enumerate(targets[i]):
                part = added[j * each : (j + 1) * each]
                total[t] = part if total[t] is None else total[t] + part
        if k != 4:
            for t in range(2):
                scratch[t, k * each : (k + 1) * each, :] = total[t].astype(BF16)
    for t in range(2):
        unit_ref[t] = lax.dot_general(
            dec_ref[...], scratch[t], (((0,), (0,)), ((), ())), preferred_element_type=F32
        ).astype(BF16)


def slope_kernel(parts_ref, out_ref):
    total = parts_ref[0].astype(F32)
    for i in range(1, parts_ref.shape[0]):
        total = total + parts_ref[i].astype(F32)
    each = total.shape[0] // 2
    joined = total[:each]
    slope = slope_of(joined, jax.nn.sigmoid(joined)).astype(BF16).astype(F32)
    grad = (total[each:] * slope).astype(BF16)
    for i in range(out_ref.shape[0]):
        out_ref[i] = grad


def store_pack(pack_ref, masked_ref, acts, masked):
    for i in range(2):
        pack_ref[i * C : (i + 1) * C, :] = acts[i]
        masked_ref[i] = masked[i]
    pack_ref[2 * C :, :] = own_of(masked[1], masked[0]).astype(BF16)


def head_kernel(unit_ref, joinw_ref, kept_ref, last_ref, pack_ref, masked_ref):
    each = unit_ref.shape[1] // 2
    acts, masked = [], []
    for i in range(2):
        unit_grad = jnp.concatenate(
            [unit_ref[d, i * each : (i + 1) * each, :] for d in range(unit_ref.shape[0])], axis=0
        )
        gradient = jnp.dot(joinw_ref[...], unit_grad, preferred_element_type=F32)
        masked.append(kept_ref[2 + i : 3 + i, :] * gradient)
        acts.append((masked[i] * last_ref[i]).astype(BF16))
    store_pack(pack_ref, masked_ref, acts, masked)


def weight_grad(acts, picked):
    total = None
    for i in range(2):
        added = lax.dot_general(
            own_of(acts[i][: C // 2], acts[i][C // 2 :]), picked[i],
            (((1,), (1,)), ((), ())), preferred_element_type=F32,
        )
        total = added if total is None else total + added
    return total.astype(BF16)


def pair_of(ref):
    return [ref[:C, :], ref[C : 2 * C, :]]


def both(ref, layer):
    return [ref[layer, 0], ref[layer, 1]]


def beside_kernel(has_low, *refs):
    if has_low:
        x_ref, w_ref, pos_ref, low_ref, picked_ref, lower_ref, lower_picked_ref, own_ref, grad_ref = refs
        grad_ref[...] = jnp.concatenate(
            [weight_grad(pair_of(lower_ref), both(lower_picked_ref, 0)),
             weight_grad(pair_of(x_ref), both(picked_ref, 1))], axis=1,
        )
    else:
        x_ref, w_ref, pos_ref, low_ref, picked_ref, own_ref, grad_ref = refs
        grad_ref[...] = weight_grad(pair_of(x_ref), both(picked_ref, 1))
    first, second = [
        spread(act, b, pos_ref, low_ref, w_ref[1], (0, 1, 2))
        for b, act in zip((2, 3), pair_of(x_ref))
    ]
    own_ref[0] = first[0]
    own_ref[1] = first[1] + second[0]
    own_ref[2] = first[2] + second[1]
    own_ref[3] = second[2]


def upper_layer(
    x_ref, got_ref, other_ref, masked_ref, own_ref, w_ref, pos_ref, low_ref, kept_ref, slopes_ref
):
    below, above = ordered(got_ref, other_ref)
    acts = {0: below[:C], 1: below[C : 2 * C], 4: above[:C], 5: above[C : 2 * C]}
    masked = [
        below[2 * C :].astype(F32), masked_ref[0], masked_ref[1], above[2 * C :].astype(F32)
    ]
    gradient = [masked[i] + own_ref[i] for i in range(4)]
    for b, parts in ((0, (2,)), (1, (1, 2)), (4, (0, 1)), (5, (0,))):
        for part, value in spread(acts[b], b, pos_ref, low_ref, w_ref[1], parts).items():
            gradient[b + part - 2] = gradient[b + part - 2] + value
    lower = [kept_ref[i + 1 : i + 2, :] * gradient[i] for i in range(4)]
    low_acts = [(lower[i] * slopes_ref[i]).astype(BF16) for i in range(4)]
    return lower, low_acts


def back_kernel(
    x_ref, got_ref, other_ref, masked_ref, own_ref, w_ref, pos_ref, low_ref, kept_ref, slopes_ref,
    next_ref, pack_ref, out_ref, lower_ref,
):
    lower, low_acts = upper_layer(
        x_ref, got_ref, other_ref, masked_ref, own_ref, w_ref, pos_ref, low_ref, kept_ref,
        slopes_ref,
    )
    result = [lower[1], lower[2]]
    for b, parts in ((1, (2,)), (2, (1, 2)), (3, (0, 1)), (4, (0,))):
        for part, value in spread(low_acts[b - 1], b, pos_ref, low_ref, w_ref[0], parts).items():
            result[b + part - 3] = result[b + part - 3] + value
    masked = [kept_ref[2 + i : 3 + i, :] * result[i] for i in range(2)]
    acts = [(masked[i] * next_ref[i]).astype(BF16) for i in range(2)]
    store_pack(pack_ref, out_ref, acts, masked)
    for i in range(2):
        lower_ref[i * C : (i + 1) * C, :] = low_acts[1 + i]


def last_back_kernel(
    x_ref, got_ref, other_ref, masked_ref, own_ref, w_ref, pos_ref, low_ref, kept_ref, slopes_ref,
    picked_ref, grad5_ref, grad43_ref, grad21_ref, lower_ref, out_ref, keep_ref, send_ref,
):
    lower, low_acts = upper_layer(
        x_ref, got_ref, other_ref, masked_ref, own_ref, w_ref, pos_ref, low_ref, kept_ref,
        slopes_ref,
    )
    out_ref[...] = own_of(lower[1], lower[2])
    for i in range(3):
        lower_ref[i * C : (i + 1) * C, :] = own_of(low_acts[i], low_acts[i + 1])
    last = jnp.concatenate(
        [weight_grad(low_acts[1:3], both(picked_ref, 0)), grad5_ref[...]], axis=1
    )
    middle = grad21_ref[...]
    first = jnp.concatenate([grad43_ref[...], middle[: C // 4]], axis=0)
    second = jnp.concatenate([middle[C // 4 :], last], axis=0)
    low_half = lax.axis_index("yh") == 0
    keep_ref[...] = jnp.where(low_half, first, second)
    send_ref[...] = jnp.where(low_half, second, first)


def map_kernel(lower_ref, own_ref, w_ref, pos_ref, low_ref, map_ref, token_ref):
    own = own_ref[...]
    for i, part in ((0, 2), (1, 1), (2, 0)):
        act = lower_ref[i * C : (i + 1) * C, :]
        own = own + spread(act, i, pos_ref, low_ref, w_ref[0], (part,))[part]
    map_ref[...] = own.astype(BF16)
    token_ref[...] = own[:8, :128]


def add_kernel(keep_ref, got_ref, _, out_ref):
    out_ref[...] = (keep_ref[...].astype(F32) + got_ref[...].astype(F32)).astype(BF16)


def rows_kernel(own_ref, got_ref, out_ref):
    rows = own_ref.shape[0]
    low_half = lax.axis_index("yh") == 0
    own, got = own_ref[...], got_ref[...]
    out_ref[:rows, :] = jnp.where(low_half, own, got)
    out_ref[rows:, :] = jnp.where(low_half, got, own)


def final_kernel(scale, own_ref, other_ref, out_ref):
    wide = TAPS * C
    half_rows = C // 2
    for core, sums in enumerate(ordered(own_ref, other_ref)):
        rows = sums.astype(F32) * scale
        for slot, pair in enumerate(((4, 3), (2, 1), (0, 5))):
            for half, layer in enumerate(pair):
                for k in range(TAPS):
                    at = half * wide + k * C
                    out_ref[layer, k, core * half_rows : (core + 1) * half_rows, :] = rows[
                        slot * half_rows : (slot + 1) * half_rows, at : at + C
                    ]


def sds(shape, dtype):
    return jax.ShapeDtypeStruct(shape, dtype)


def call(body, name, ins, outs, scratch=(), limit=LIMIT):
    specs = [spec for spec, _ in ins]
    return pl.pallas_call(
        body,
        name=name,
        in_specs=specs,
        out_specs=[pl.BlockSpec(memory_space=pltpu.VMEM) for _ in outs],
        out_shape=outs,
        scratch_shapes=list(scratch),
        compiler_params=pltpu.CompilerParams(vmem_limit_bytes=limit),
    )(*[value for _, value in ins])


def v(value):
    return (VMEM, value)


def exchange(value, axes):
    return lax.all_to_all(value, axes, 0, 0, tiled=True)


def add_up(parts):
    return jnp.sum(parts.astype(F32), axis=0).astype(BF16)


def copies(value, count):
    return jnp.broadcast_to(value[None], (count,) + value.shape)


def swap_halves(value):
    return lax.ppermute(value, "yh", [(0, 1), (1, 0)])


def sum_over_sky(keep, send, length, after):
    rows, lanes = keep.shape
    out = [sds(keep.shape, BF16)]
    any_space = pl.BlockSpec(memory_space=pl.ANY)
    chunk = call(
        add_kernel, "add", [v(keep), v(swap_halves(send)), (any_space, after)], out
    )[0]
    tiles = (rows // 8) * (lanes // 128)
    each = -(-tiles // length)
    chunk = chunk.reshape(rows // 8, 8, lanes // 128, 128).transpose(0, 2, 1, 3)
    chunk = jnp.pad(chunk.reshape(tiles, 8, 128), ((0, each * length - tiles), (0, 0), (0, 0)))
    chunk = add_up(exchange(chunk.reshape(length, each, 8, 128), "z"))
    chunk = exchange(copies(chunk, length), "z").reshape(each * length, 8, 128)[:tiles]
    chunk = chunk.reshape(rows // 8, lanes // 128, 8, 128).transpose(0, 2, 1, 3)
    chunk = chunk.reshape(rows, lanes)
    return call(
        rows_kernel, "rows", [v(chunk), v(swap_halves(chunk))], [sds((2 * rows, lanes), BF16)]
    )[0]


def per_device(sky_maps, footprint, neighbours, enc_weight, join_weight, dec_weight, cotangent):
    depth = enc_weight.shape[1]
    branches = lax.axis_size("branch")
    peers = lax.axis_size(SKY)
    dma = pltpu.SemaphoreType.DMA
    weights = call(
        weights_kernel, "weights", [(HBM, enc_weight[0])],
        [sds((2, C, TAPS * C), BF16)] * (depth // 2),
        [pltpu.VMEM(enc_weight.shape[1:], BF16), dma((1,))],
    )
    joinw = join_weight.T
    dec = dec_weight.reshape(-1, dec_weight.shape[2])
    each = cotangent.shape[0]
    full = dec.shape[1]
    wide = TAPS * C
    size = C + each + 16
    pack = call(
        pack_kernel, "pack",
        [(HBM, sky_maps[0]), (HBM, cotangent), (HBM, neighbours), (HBM, footprint)],
        [sds((size, R), BF16)],
        [pltpu.VMEM((TAPS, R), jnp.int32), pltpu.VMEM((1, R), jnp.int32), dma((4,))], None,
    )[0]
    pack, sent = call(
        pair_kernel, "pair", [v(pack), v(swap_cores(pack))],
        [sds((2 * size, R), BF16), sds((2 * C + 32 + each, R), BF16)],
    )
    pair = sds((2, C, R), F32)
    layer_outs = [sds((2 * C, R), BF16), sds((2, 2, wide, R), BF16), sds((4, C, R), F32), pair]
    scratch = [pltpu.VMEM((2, wide, R), BF16)]
    got, other = widen(sent, [weights[0]])
    low_lanes = sds((R, 128), jnp.int32)
    hidden, picked, slopes, last, pos, kept, low, near_pos, near_low, cots = call(
        first_kernel, "layers01", [v(pack), v(got), v(other), v(weights[0])],
        layer_outs
        + [sds((96, R), jnp.int32), sds((8, R), F32), low_lanes, sds((48, R), jnp.int32),
           low_lanes, sds((4 * each, R), BF16)],
        scratch,
    )
    saved = [(picked, slopes, last)]
    unit = call(
        unit_kernel, "unit", [v(cots), v(pos), v(low), v(dec)],
        [sds((2, full, R), BF16)], [pltpu.VMEM((2, TAPS * each, R), BF16)],
    )[0]
    for group in range(1, depth // 2):
        got, other = widen(hidden, [unit] if group == 1 else ())
        ins = [v(hidden), v(got), v(other), v(weights[group]), v(pos), v(kept)]
        if group < depth // 2 - 1:
            hidden, picked, slopes, last = call(layers_kernel, "layers", ins, layer_outs, scratch)
        else:
            share, picked, slopes, last = call(
                last_layers_kernel, "lastlayers", ins + [v(joinw), v(unit)],
                [sds((branches, 4 * each, R), BF16)] + layer_outs[1:], scratch,
            )
        saved.append((picked, slopes, last))
    parts = exchange(share, "branch")
    mine = call(slope_kernel, "slope", [v(parts)], [sds((branches, 2 * each, R), BF16)])[0]
    pack_outs = [sds((3 * C, R), BF16), pair]
    pack, masked = call(
        head_kernel, "head",
        [v(exchange(mine, "branch")), v(joinw), v(kept), v(saved[-1][2])], pack_outs,
    )
    grads = []
    lower = None
    for group in reversed(range(depth // 2)):
        picked, slopes, _ = saved[group]
        beside = [v(pack), v(weights[group]), v(pos), v(low), v(picked)]
        if lower is not None:
            beside = beside + [v(lower), v(saved[group + 1][0])]
        own, grad = call(
            functools.partial(beside_kernel, lower is not None), "beside", beside,
            [sds((4, C, R), F32), sds((C // 2, wide if lower is None else 2 * wide), BF16)],
        )
        grads.append(grad)
        got, other = widen(pack, [own])
        ins = [
            v(pack), v(got), v(other), v(masked), v(own), v(weights[group]), v(pos), v(low),
            v(kept), v(slopes),
        ]
        if group:
            pack, masked, lower = call(
                back_kernel, "back", ins + [v(saved[group - 1][2])],
                pack_outs + [sds((2 * C, R), BF16)],
            )
        else:
            half = sds((3 * C // 4, 2 * wide), BF16)
            lower, own, keep, send = call(
                last_back_kernel, "lastback", ins + [v(picked)] + [v(g) for g in grads],
                [sds((3 * C, R), BF16), sds((C, R), F32), half, half],
            )
    map_grads, token = call(
        map_kernel, "mapgrad", [v(lower), v(own), v(weights[0]), v(near_pos), v(near_low)],
        [sds((C, R), BF16), sds((8, 128), F32)],
    )
    total = sum_over_sky(keep, send, lax.axis_size("z"), token)
    summed = call(
        functools.partial(final_kernel, 1.0 / math.sqrt(R * peers)), "final",
        [v(total), v(swap_cores(total))],
        [sds((depth, TAPS, C, C), F32)],
    )[0]
    return map_grads[None], summed[None]


def solution(mesh):
    branches, sky = mesh.devices.shape
    mesh = Mesh(mesh.devices.reshape(branches, sky // 4, 2, 2), ("branch",) + SKY)
    in_specs = (
        P("branch", None, SKY),
        P("branch", SKY),
        P(None, SKY),
        P("branch", None, None, None, None),
        P(None, "branch"),
        P(None, "branch", None),
        P("branch", SKY),
    )
    out_specs = (P("branch", None, SKY), P("branch", None, None, None, None))
    return jax.shard_map(
        per_device, mesh=mesh, in_specs=in_specs, out_specs=out_specs, check_vma=False
    )
```

```python
import functools
import math

import jax
import jax.numpy as jnp
from jax import lax
from jax.experimental import pallas as pl
from jax.experimental.pallas import tpu as pltpu
from jax.sharding import Mesh, PartitionSpec as P

SKY = ("z", "yh", "core")
C = 64
R = 256
TAPS = 9
LIMIT = 16 * 1024 * 1024
F32 = jnp.float32
BF16 = jnp.bfloat16
VMEM = pl.BlockSpec(memory_space=pltpu.VMEM)
HBM = pl.BlockSpec(memory_space=pltpu.HBM)


def swap_cores(value):
    return lax.ppermute(value, "core", [(0, 1), (1, 0)])


def widen(value, after=()):
    peers = lax.axis_size(SKY)
    pairs = [(i, i + 2) for i in range(0, peers - 2, 2)] + [(i, i - 2) for i in range(3, peers, 2)]
    got = lax.ppermute(value, SKY, pairs)
    if after:
        got = call(
            relay_kernel, "relay",
            [v(got)] + [(pl.BlockSpec(memory_space=pl.ANY), x) for x in after],
            [sds(value.shape, value.dtype)],
        )[0]
    return got, swap_cores(got)


def relay_kernel(*refs):
    refs[-1][...] = refs[0][...]


def ordered(got, other):
    got, other = got[...], other[...]
    return own_of(got, other), own_of(other, got)


def own_of(first, second):
    return jnp.where(lax.axis_index("core") == 0, first, second)


def fetch(pairs, sems):
    copies = [pltpu.make_async_copy(src, dst, sems.at[i]) for i, (src, dst) in enumerate(pairs)]
    for copy in copies:
        copy.start()
    for copy in copies:
        copy.wait()


def inner(other, first, even, start, size):
    own = other[start : start + size]
    below = other[first + start : first + start + size]
    above = other[2 * first + start : 2 * first + start + size]
    return jnp.where(even, below, own), jnp.where(even, own, above)


def slope_of(value, sigmoid):
    return sigmoid * (1.0 + value * (1.0 - sigmoid))


def low_onehot(low, dim=0):
    return (lax.broadcasted_iota(jnp.int32, (R, R), dim) == low).astype(BF16)


def low_table(tables):
    low = (tables & 255).astype(F32)
    padded = jnp.concatenate([low, jnp.zeros((128 - low.shape[0], R), F32)], axis=0)
    return jnp.transpose(padded).astype(jnp.int32)


def conv(blocks, pos, weight, picked_ref):
    stack = jnp.concatenate(blocks, axis=0)
    for k in range(TAPS):
        if k == 4:
            column = blocks[1]
        else:
            at = pos[k : k + 1]
            block = at >> 8
            found = jnp.dot(stack, low_onehot(at & 255), preferred_element_type=F32)
            column = jnp.where(
                block == 0,
                found[:C],
                jnp.where(block == 1, found[C : 2 * C], jnp.where(block == 2, found[2 * C :], 0.0)),
            ).astype(BF16)
        picked_ref[k * C : (k + 1) * C, :] = column
    return jnp.dot(weight, picked_ref[...], preferred_element_type=F32)


def spread(act, b, pos_ref, low_ref, weight, parts):
    terms = lax.dot_general(weight, act, (((0,), (0,)), ((), ())), preferred_element_type=F32)
    pos = pos_ref[16 * b : 16 * b + 16, :]
    total = None
    for k in range(TAPS):
        if k == 4:
            continue
        block = pos[k : k + 1] >> 8
        term = terms[k * C : (k + 1) * C].astype(BF16)
        zero = jnp.zeros_like(term)
        sent = jnp.concatenate([jnp.where(block == part, term, zero) for part in parts], axis=0)
        low = low_ref[:, 16 * b + k : 16 * b + k + 1]
        added = jnp.dot(sent, low_onehot(low, 1), preferred_element_type=F32)
        total = added if total is None else total + added
    out = {part: total[i * C : (i + 1) * C] for i, part in enumerate(parts)}
    if 1 in out:
        out[1] = out[1] + terms[4 * C : 5 * C]
    return out


def two_layers(blocks, pos, kept, w_ref, picked_ref, slopes_ref, last_ref, scratch):
    middle = []
    for b in (1, 2, 3, 4):
        target = picked_ref.at[0, b - 2] if b in (2, 3) else scratch.at[b // 4]
        pre = conv(blocks[b - 1 : b + 2], pos[b], w_ref[0], target)
        sigmoid = jax.nn.sigmoid(pre)
        slopes_ref[b - 1] = slope_of(pre, sigmoid)
        middle.append((kept[b] * (blocks[b].astype(F32) + pre * sigmoid)).astype(BF16))
    hidden = []
    for b in (2, 3):
        pre = conv(middle[b - 2 : b + 1], pos[b], w_ref[1], picked_ref.at[1, b - 2])
        sigmoid = jax.nn.sigmoid(pre)
        last_ref[b - 2] = slope_of(pre, sigmoid)
        hidden.append((kept[b] * (middle[b - 1].astype(F32) + pre * sigmoid)).astype(BF16))
    return hidden


def pair_kernel(own_ref, other_ref, out_ref, sent_ref):
    size = own_ref.shape[0]
    each = size - 16 - C
    own, other = own_ref[...], other_ref[...]
    first, second = own_of(own, other), own_of(other, own)
    out_ref[:size, :] = first
    out_ref[size:, :] = second
    sent_ref[:C, :] = first[:C]
    sent_ref[C : 2 * C, :] = second[:C]
    sent_ref[2 * C : 2 * C + 16, :] = first[C + each :]
    sent_ref[2 * C + 16 : 2 * C + 32, :] = second[C + each :]
    sent_ref[2 * C + 32 :, :] = own_of(second, first)[C : C + each]


def first_kernel(
    x_ref, got_ref, other_ref, w_ref,
    h_ref, picked_ref, slopes_ref, last_ref, pos_ref, kept_ref, low_ref, near_pos_ref, near_low_ref,
    cot_ref, scratch,
):
    size = x_ref.shape[0] // 2
    below, above = ordered(got_ref, other_ref)
    each = size - 16 - C
    pair = [x_ref[:size, :], x_ref[size:, :]]
    metas = [
        below[2 * C : 2 * C + 16], below[2 * C + 16 : 2 * C + 32], pair[0][C + each :],
        pair[1][C + each :], above[2 * C : 2 * C + 16], above[2 * C + 16 : 2 * C + 32],
    ]
    cots = [below[2 * C + 32 :], pair[0][C : C + each], pair[1][C : C + each], above[2 * C + 32 :]]
    blocks = [below[:C], below[C : 2 * C], pair[0][:C], pair[1][:C], above[:C], above[C : 2 * C]]
    column = lax.broadcasted_iota(jnp.int32, (16, R), 1)
    pos, kept = [], []
    for b, meta in enumerate(metas):
        offset = meta.astype(F32)
        at = jnp.where(offset > 400.0, 768, offset.astype(jnp.int32) + column + R)
        pos_ref[16 * b : 16 * (b + 1), :] = at
        keep = offset[TAPS : TAPS + 1]
        kept_ref[b : b + 1, :] = keep
        pos.append(at)
        kept.append(keep)
    kept_ref[6:8, :] = jnp.zeros((2, R), F32)
    near = jnp.concatenate([own_of(pos[i + 1], pos[i + 2]) for i in range(3)], axis=0)
    near_pos_ref[...] = near
    near_low_ref[...] = low_table(near)
    low_ref[...] = low_table(jnp.concatenate(pos, axis=0))
    for i in range(3):
        cot_ref[each * i : each * (i + 1), :] = own_of(cots[i], cots[i + 1])
    hidden = two_layers(blocks, pos, kept, w_ref, picked_ref, slopes_ref, last_ref, scratch)
    for i in range(2):
        h_ref[i * C : (i + 1) * C, :] = hidden[i]


def read_tables(pos_ref, kept_ref):
    pos = [pos_ref[16 * b : 16 * b + 16, :] for b in range(6)]
    kept = [kept_ref[b : b + 1, :] for b in range(6)]
    return pos, kept


def read_blocks(x_ref, got_ref, other_ref):
    below, above = ordered(got_ref, other_ref)
    return [below[:C], below[C:], x_ref[:C, :], x_ref[C:, :], above[:C], above[C:]]


def layers_kernel(
    x_ref, got_ref, other_ref, w_ref, pos_ref, kept_ref,
    h_ref, picked_ref, slopes_ref, last_ref, scratch,
):
    pos, kept = read_tables(pos_ref, kept_ref)
    blocks = read_blocks(x_ref, got_ref, other_ref)
    hidden = two_layers(blocks, pos, kept, w_ref, picked_ref, slopes_ref, last_ref, scratch)
    for i in range(2):
        h_ref[i * C : (i + 1) * C, :] = hidden[i]


def last_layers_kernel(
    x_ref, got_ref, other_ref, w_ref, pos_ref, kept_ref, joinw_ref, unit_ref,
    share_ref, picked_ref, slopes_ref, last_ref, scratch,
):
    pos, kept = read_tables(pos_ref, kept_ref)
    blocks = read_blocks(x_ref, got_ref, other_ref)
    hidden = two_layers(blocks, pos, kept, w_ref, picked_ref, slopes_ref, last_ref, scratch)
    partial = lax.dot_general(
        joinw_ref[...], own_of(*hidden), (((0,), (0,)), ((), ())), preferred_element_type=F32
    ).astype(BF16)
    count = share_ref.shape[0]
    each = partial.shape[0] // count
    for c in range(count):
        share_ref[c, :each, :] = partial[c * each : (c + 1) * each]
        share_ref[c, each:, :] = unit_ref[c * each : (c + 1) * each, :]


def pack_kernel(
    maps_hbm, cot_hbm, near_hbm, foot_hbm, pack_ref, near_ref, foot_ref, sems
):
    each = cot_hbm.shape[0]
    fetch(
        [(near_hbm, near_ref), (foot_hbm, foot_ref), (maps_hbm, pack_ref.at[pl.ds(0, C)]),
         (cot_hbm, pack_ref.at[pl.ds(C, each)])], sems,
    )
    row = lax.axis_index(SKY) * R + lax.broadcasted_iota(jnp.int32, (TAPS, R), 1)
    near = near_ref[...]
    offset = jnp.where(near >= 0, near - row, 512).astype(F32)
    meta = jnp.concatenate(
        [offset, foot_ref[...].astype(F32), jnp.zeros((16 - TAPS - 1, R), F32)], axis=0
    )
    pack_ref[C + each :, :] = meta.astype(BF16)


def weights_kernel(w_hbm, *refs):
    outs, w_ref, sems = refs[:-2], refs[-2], refs[-1]
    fetch([(w_hbm, w_ref)], sems)
    for group, out_ref in enumerate(outs):
        for i in range(2):
            layer = 2 * group + i
            out_ref[i] = jnp.concatenate([w_ref[layer, k] for k in range(TAPS)], axis=1)


def unit_kernel(cot_ref, pos_ref, low_ref, dec_ref, unit_ref, scratch):
    each = cot_ref.shape[0] // 3
    cots = [cot_ref[each * i : each * (i + 1), :] for i in range(3)]
    for k in range(TAPS):
        if k == 4:
            scratch[k * each : (k + 1) * each, :] = cots[1]
            continue
        total = None
        for i in range(3):
            block = pos_ref[16 * i + k : 16 * i + k + 1, :] >> 8
            sent = jnp.where(block == 2 - i, cots[i], jnp.zeros_like(cots[i]))
            low = low_ref[:, 16 * i + k : 16 * i + k + 1]
            added = jnp.dot(sent, low_onehot(low, 1), preferred_element_type=F32)
            total = added if total is None else total + added
        scratch[k * each : (k + 1) * each, :] = total.astype(BF16)
    unit_ref[...] = lax.dot_general(
        dec_ref[...], scratch[...], (((0,), (0,)), ((), ())), preferred_element_type=F32
    ).astype(BF16)


def slope_kernel(parts_ref, out_ref):
    total = parts_ref[0].astype(F32)
    for i in range(1, parts_ref.shape[0]):
        total = total + parts_ref[i].astype(F32)
    each = total.shape[0] // 2
    joined = total[:each]
    slope = slope_of(joined, jax.nn.sigmoid(joined)).astype(BF16).astype(F32)
    out_ref[...] = (total[each:] * slope).astype(BF16)


def copies_kernel(own_ref, other_ref, out_ref):
    each = own_ref.shape[0]
    first, second = ordered(own_ref, other_ref)
    for i in range(out_ref.shape[0]):
        out_ref[i, :each, :] = first
        out_ref[i, each:, :] = second


def store_pack(pack_ref, masked_ref, acts, masked):
    for i in range(2):
        pack_ref[i * C : (i + 1) * C, :] = acts[i]
        masked_ref[i] = masked[i]
    pack_ref[2 * C :, :] = own_of(masked[1], masked[0]).astype(BF16)


def head_kernel(unit_ref, joinw_ref, kept_ref, last_ref, pack_ref, masked_ref):
    each = unit_ref.shape[1] // 2
    acts, masked = [], []
    for i in range(2):
        unit_grad = jnp.concatenate(
            [unit_ref[d, i * each : (i + 1) * each, :] for d in range(unit_ref.shape[0])], axis=0
        )
        gradient = jnp.dot(joinw_ref[...], unit_grad, preferred_element_type=F32)
        masked.append(kept_ref[2 + i : 3 + i, :] * gradient)
        acts.append((masked[i] * last_ref[i]).astype(BF16))
    store_pack(pack_ref, masked_ref, acts, masked)


def weight_grad(acts, picked):
    total = None
    for i in range(2):
        added = lax.dot_general(
            own_of(acts[i][: C // 2], acts[i][C // 2 :]), picked[i],
            (((1,), (1,)), ((), ())), preferred_element_type=F32,
        )
        total = added if total is None else total + added
    return total.astype(BF16)


def pair_of(ref):
    return [ref[:C, :], ref[C : 2 * C, :]]


def both(ref, layer):
    return [ref[layer, 0], ref[layer, 1]]


def beside_kernel(has_low, *refs):
    if has_low:
        x_ref, w_ref, pos_ref, low_ref, picked_ref, lower_ref, lower_picked_ref, own_ref, grad_ref = refs
        grad_ref[...] = jnp.concatenate(
            [weight_grad(pair_of(lower_ref), both(lower_picked_ref, 0)),
             weight_grad(pair_of(x_ref), both(picked_ref, 1))], axis=1,
        )
    else:
        x_ref, w_ref, pos_ref, low_ref, picked_ref, own_ref, grad_ref = refs
        grad_ref[...] = weight_grad(pair_of(x_ref), both(picked_ref, 1))
    first, second = [
        spread(act, b, pos_ref, low_ref, w_ref[1], (0, 1, 2))
        for b, act in zip((2, 3), pair_of(x_ref))
    ]
    own_ref[0] = first[0]
    own_ref[1] = first[1] + second[0]
    own_ref[2] = first[2] + second[1]
    own_ref[3] = second[2]


def upper_layer(
    x_ref, got_ref, other_ref, masked_ref, own_ref, w_ref, pos_ref, low_ref, kept_ref, slopes_ref
):
    below, above = ordered(got_ref, other_ref)
    acts = {0: below[:C], 1: below[C : 2 * C], 4: above[:C], 5: above[C : 2 * C]}
    masked = [
        below[2 * C :].astype(F32), masked_ref[0], masked_ref[1], above[2 * C :].astype(F32)
    ]
    gradient = [masked[i] + own_ref[i] for i in range(4)]
    for b, parts in ((0, (2,)), (1, (1, 2)), (4, (0, 1)), (5, (0,))):
        for part, value in spread(acts[b], b, pos_ref, low_ref, w_ref[1], parts).items():
            gradient[b + part - 2] = gradient[b + part - 2] + value
    lower = [kept_ref[i + 1 : i + 2, :] * gradient[i] for i in range(4)]
    low_acts = [(lower[i] * slopes_ref[i]).astype(BF16) for i in range(4)]
    return lower, low_acts


def back_kernel(
    x_ref, got_ref, other_ref, masked_ref, own_ref, w_ref, pos_ref, low_ref, kept_ref, slopes_ref,
    next_ref, pack_ref, out_ref, lower_ref,
):
    lower, low_acts = upper_layer(
        x_ref, got_ref, other_ref, masked_ref, own_ref, w_ref, pos_ref, low_ref, kept_ref,
        slopes_ref,
    )
    result = [lower[1], lower[2]]
    for b, parts in ((1, (2,)), (2, (1, 2)), (3, (0, 1)), (4, (0,))):
        for part, value in spread(low_acts[b - 1], b, pos_ref, low_ref, w_ref[0], parts).items():
            result[b + part - 3] = result[b + part - 3] + value
    masked = [kept_ref[2 + i : 3 + i, :] * result[i] for i in range(2)]
    acts = [(masked[i] * next_ref[i]).astype(BF16) for i in range(2)]
    store_pack(pack_ref, out_ref, acts, masked)
    for i in range(2):
        lower_ref[i * C : (i + 1) * C, :] = low_acts[1 + i]


def last_back_kernel(
    x_ref, got_ref, other_ref, masked_ref, own_ref, w_ref, pos_ref, low_ref, kept_ref, slopes_ref,
    picked_ref, grad5_ref, grad43_ref, grad21_ref, lower_ref, out_ref, keep_ref, send_ref,
):
    lower, low_acts = upper_layer(
        x_ref, got_ref, other_ref, masked_ref, own_ref, w_ref, pos_ref, low_ref, kept_ref,
        slopes_ref,
    )
    out_ref[...] = own_of(lower[1], lower[2])
    for i in range(3):
        lower_ref[i * C : (i + 1) * C, :] = own_of(low_acts[i], low_acts[i + 1])
    last = jnp.concatenate(
        [weight_grad(low_acts[1:3], both(picked_ref, 0)), grad5_ref[...]], axis=1
    )
    middle = grad21_ref[...]
    first = jnp.concatenate([grad43_ref[...], middle[: C // 4]], axis=0)
    second = jnp.concatenate([middle[C // 4 :], last], axis=0)
    low_half = lax.axis_index("yh") == 0
    keep_ref[...] = jnp.where(low_half, first, second)
    send_ref[...] = jnp.where(low_half, second, first)


def map_kernel(lower_ref, own_ref, w_ref, pos_ref, low_ref, map_ref, token_ref):
    own = own_ref[...]
    for i, part in ((0, 2), (1, 1), (2, 0)):
        act = lower_ref[i * C : (i + 1) * C, :]
        own = own + spread(act, i, pos_ref, low_ref, w_ref[0], (part,))[part]
    map_ref[...] = own.astype(BF16)
    token_ref[...] = own[:8, :128]


def add_kernel(keep_ref, got_ref, _, out_ref):
    out_ref[...] = (keep_ref[...].astype(F32) + got_ref[...].astype(F32)).astype(BF16)


def rows_kernel(own_ref, got_ref, out_ref):
    rows = own_ref.shape[0]
    low_half = lax.axis_index("yh") == 0
    own, got = own_ref[...], got_ref[...]
    out_ref[:rows, :] = jnp.where(low_half, own, got)
    out_ref[rows:, :] = jnp.where(low_half, got, own)


def final_kernel(scale, own_ref, other_ref, out_ref):
    wide = TAPS * C
    half_rows = C // 2
    for core, sums in enumerate(ordered(own_ref, other_ref)):
        rows = sums.astype(F32) * scale
        for slot, pair in enumerate(((4, 3), (2, 1), (0, 5))):
            for half, layer in enumerate(pair):
                for k in range(TAPS):
                    at = half * wide + k * C
                    out_ref[layer, k, core * half_rows : (core + 1) * half_rows, :] = rows[
                        slot * half_rows : (slot + 1) * half_rows, at : at + C
                    ]


def sds(shape, dtype):
    return jax.ShapeDtypeStruct(shape, dtype)


def call(body, name, ins, outs, scratch=(), limit=LIMIT):
    specs = [spec for spec, _ in ins]
    return pl.pallas_call(
        body,
        name=name,
        in_specs=specs,
        out_specs=[pl.BlockSpec(memory_space=pltpu.VMEM) for _ in outs],
        out_shape=outs,
        scratch_shapes=list(scratch),
        compiler_params=pltpu.CompilerParams(vmem_limit_bytes=limit),
    )(*[value for _, value in ins])


def v(value):
    return (VMEM, value)


def exchange(value, axes):
    return lax.all_to_all(value, axes, 0, 0, tiled=True)


def add_up(parts):
    return jnp.sum(parts.astype(F32), axis=0).astype(BF16)


def copies(value, count):
    return jnp.broadcast_to(value[None], (count,) + value.shape)


def swap_halves(value):
    return lax.ppermute(value, "yh", [(0, 1), (1, 0)])


def sum_over_sky(keep, send, length, after):
    rows, lanes = keep.shape
    out = [sds(keep.shape, BF16)]
    any_space = pl.BlockSpec(memory_space=pl.ANY)
    chunk = call(
        add_kernel, "add", [v(keep), v(swap_halves(send)), (any_space, after)], out
    )[0]
    tiles = (rows // 8) * (lanes // 128)
    each = -(-tiles // length)
    chunk = chunk.reshape(rows // 8, 8, lanes // 128, 128).transpose(0, 2, 1, 3)
    chunk = jnp.pad(chunk.reshape(tiles, 8, 128), ((0, each * length - tiles), (0, 0), (0, 0)))
    chunk = add_up(exchange(chunk.reshape(length, each, 8, 128), "z"))
    chunk = exchange(copies(chunk, length), "z").reshape(each * length, 8, 128)[:tiles]
    chunk = chunk.reshape(rows // 8, lanes // 128, 8, 128).transpose(0, 2, 1, 3)
    chunk = chunk.reshape(rows, lanes)
    return call(
        rows_kernel, "rows", [v(chunk), v(swap_halves(chunk))], [sds((2 * rows, lanes), BF16)]
    )[0]


def per_device(sky_maps, footprint, neighbours, enc_weight, join_weight, dec_weight, cotangent):
    depth = enc_weight.shape[1]
    branches = lax.axis_size("branch")
    peers = lax.axis_size(SKY)
    dma = pltpu.SemaphoreType.DMA
    weights = call(
        weights_kernel, "weights", [(HBM, enc_weight[0])],
        [sds((2, C, TAPS * C), BF16)] * (depth // 2),
        [pltpu.VMEM(enc_weight.shape[1:], BF16), dma((1,))],
    )
    joinw = join_weight.T
    dec = dec_weight.reshape(-1, dec_weight.shape[2])
    each = cotangent.shape[0]
    full = dec.shape[1]
    wide = TAPS * C
    size = C + each + 16
    pack = call(
        pack_kernel, "pack",
        [(HBM, sky_maps[0]), (HBM, cotangent), (HBM, neighbours), (HBM, footprint)],
        [sds((size, R), BF16)],
        [pltpu.VMEM((TAPS, R), jnp.int32), pltpu.VMEM((1, R), jnp.int32), dma((4,))], None,
    )[0]
    pack, sent = call(
        pair_kernel, "pair", [v(pack), v(swap_cores(pack))],
        [sds((2 * size, R), BF16), sds((2 * C + 32 + each, R), BF16)],
    )
    pair = sds((2, C, R), F32)
    layer_outs = [sds((2 * C, R), BF16), sds((2, 2, wide, R), BF16), sds((4, C, R), F32), pair]
    scratch = [pltpu.VMEM((2, wide, R), BF16)]
    got, other = widen(sent, [weights[0]])
    low_lanes = sds((R, 128), jnp.int32)
    hidden, picked, slopes, last, pos, kept, low, near_pos, near_low, cots = call(
        first_kernel, "layers01", [v(pack), v(got), v(other), v(weights[0])],
        layer_outs
        + [sds((96, R), jnp.int32), sds((8, R), F32), low_lanes, sds((48, R), jnp.int32),
           low_lanes, sds((3 * each, R), BF16)],
        scratch,
    )
    saved = [(picked, slopes, last)]
    unit = call(
        unit_kernel, "unit", [v(cots), v(near_pos), v(near_low), v(dec)],
        [sds((full, R), BF16)], [pltpu.VMEM((TAPS * each, R), BF16)],
    )[0]
    for group in range(1, depth // 2):
        got, other = widen(hidden, [unit] if group == 1 else ())
        ins = [v(hidden), v(got), v(other), v(weights[group]), v(pos), v(kept)]
        if group < depth // 2 - 1:
            hidden, picked, slopes, last = call(layers_kernel, "layers", ins, layer_outs, scratch)
        else:
            share, picked, slopes, last = call(
                last_layers_kernel, "lastlayers", ins + [v(joinw), v(unit)],
                [sds((branches, 2 * each, R), BF16)] + layer_outs[1:], scratch,
            )
        saved.append((picked, slopes, last))
    parts = exchange(share, "branch")
    mine = call(slope_kernel, "slope", [v(parts)], [sds((each, R), BF16)])[0]
    mine = call(
        copies_kernel, "copies", [v(mine), v(swap_cores(mine))],
        [sds((branches, 2 * each, R), BF16)],
    )[0]
    pack_outs = [sds((3 * C, R), BF16), pair]
    pack, masked = call(
        head_kernel, "head",
        [v(exchange(mine, "branch")), v(joinw), v(kept), v(saved[-1][2])], pack_outs,
    )
    grads = []
    lower = None
    for group in reversed(range(depth // 2)):
        picked, slopes, _ = saved[group]
        beside = [v(pack), v(weights[group]), v(pos), v(low), v(picked)]
        if lower is not None:
            beside = beside + [v(lower), v(saved[group + 1][0])]
        own, grad = call(
            functools.partial(beside_kernel, lower is not None), "beside", beside,
            [sds((4, C, R), F32), sds((C // 2, wide if lower is None else 2 * wide), BF16)],
        )
        grads.append(grad)
        got, other = widen(pack, [own])
        ins = [
            v(pack), v(got), v(other), v(masked), v(own), v(weights[group]), v(pos), v(low),
            v(kept), v(slopes),
        ]
        if group:
            pack, masked, lower = call(
                back_kernel, "back", ins + [v(saved[group - 1][2])],
                pack_outs + [sds((2 * C, R), BF16)],
            )
        else:
            half = sds((3 * C // 4, 2 * wide), BF16)
            lower, own, keep, send = call(
                last_back_kernel, "lastback", ins + [v(picked)] + [v(g) for g in grads],
                [sds((3 * C, R), BF16), sds((C, R), F32), half, half],
            )
    map_grads, token = call(
        map_kernel, "mapgrad", [v(lower), v(own), v(weights[0]), v(near_pos), v(near_low)],
        [sds((C, R), BF16), sds((8, 128), F32)],
    )
    total = sum_over_sky(keep, send, lax.axis_size("z"), token)
    summed = call(
        functools.partial(final_kernel, 1.0 / math.sqrt(R * peers)), "final",
        [v(total), v(swap_cores(total))],
        [sds((depth, TAPS, C, C), F32)],
    )[0]
    return map_grads[None], summed[None]


def solution(mesh):
    branches, sky = mesh.devices.shape
    mesh = Mesh(mesh.devices.reshape(branches, sky // 4, 2, 2), ("branch",) + SKY)
    in_specs = (
        P("branch", None, SKY),
        P("branch", SKY),
        P(None, SKY),
        P("branch", None, None, None, None),
        P(None, "branch"),
        P(None, "branch", None),
        P("branch", SKY),
    )
    out_specs = (P("branch", None, SKY), P("branch", None, None, None, None))
    return jax.shard_map(
        per_device, mesh=mesh, in_specs=in_specs, out_specs=out_specs, check_vma=False
    )
```

```python
import functools
import math

import jax
import jax.numpy as jnp
from jax import lax
from jax.experimental import pallas as pl
from jax.experimental.pallas import tpu as pltpu
from jax.sharding import Mesh, PartitionSpec as P

SKY = ("z", "yh", "core")
C = 64
R = 256
TAPS = 9
LIMIT = 16 * 1024 * 1024
F32 = jnp.float32
BF16 = jnp.bfloat16
VMEM = pl.BlockSpec(memory_space=pltpu.VMEM)
HBM = pl.BlockSpec(memory_space=pltpu.HBM)


def swap_cores(value):
    return lax.ppermute(value, "core", [(0, 1), (1, 0)])


def widen(value, after=()):
    peers = lax.axis_size(SKY)
    pairs = [(i, i + 2) for i in range(0, peers - 2, 2)] + [(i, i - 2) for i in range(3, peers, 2)]
    got = lax.ppermute(value, SKY, pairs)
    if after:
        got = call(
            relay_kernel, "relay",
            [v(got)] + [(pl.BlockSpec(memory_space=pl.ANY), x) for x in after],
            [sds(value.shape, value.dtype)],
        )[0]
    return got, swap_cores(got)


def relay_kernel(*refs):
    refs[-1][...] = refs[0][...]


def ordered(got, other):
    got, other = got[...], other[...]
    return own_of(got, other), own_of(other, got)


def own_of(first, second):
    return jnp.where(lax.axis_index("core") == 0, first, second)


def fetch(pairs, sems):
    copies = [pltpu.make_async_copy(src, dst, sems.at[i]) for i, (src, dst) in enumerate(pairs)]
    for copy in copies:
        copy.start()
    for copy in copies:
        copy.wait()


def inner(other, first, even, start, size):
    own = other[start : start + size]
    below = other[first + start : first + start + size]
    above = other[2 * first + start : 2 * first + start + size]
    return jnp.where(even, below, own), jnp.where(even, own, above)


def slope_of(value, sigmoid):
    return sigmoid * (1.0 + value * (1.0 - sigmoid))


def low_onehot(low, dim=0):
    return (lax.broadcasted_iota(jnp.int32, (R, R), dim) == low).astype(BF16)


def low_table(tables):
    low = (tables & 255).astype(F32)
    padded = jnp.concatenate([low, jnp.zeros((128 - low.shape[0], R), F32)], axis=0)
    return jnp.transpose(padded).astype(jnp.int32)


def conv(blocks, pos, weight, picked_ref):
    stack = jnp.concatenate(blocks, axis=0)
    for k in range(TAPS):
        if k == 4:
            column = blocks[1]
        else:
            at = pos[k : k + 1]
            block = at >> 8
            found = jnp.dot(stack, low_onehot(at & 255), preferred_element_type=F32)
            column = jnp.where(
                block == 0,
                found[:C],
                jnp.where(block == 1, found[C : 2 * C], jnp.where(block == 2, found[2 * C :], 0.0)),
            ).astype(BF16)
        picked_ref[k * C : (k + 1) * C, :] = column
    return jnp.dot(weight, picked_ref[...], preferred_element_type=F32)


def spread(act, b, pos_ref, low_ref, weight, parts):
    terms = lax.dot_general(weight, act, (((0,), (0,)), ((), ())), preferred_element_type=F32)
    pos = pos_ref[16 * b : 16 * b + 16, :]
    total = None
    for k in range(TAPS):
        if k == 4:
            continue
        block = pos[k : k + 1] >> 8
        term = terms[k * C : (k + 1) * C].astype(BF16)
        zero = jnp.zeros_like(term)
        sent = jnp.concatenate([jnp.where(block == part, term, zero) for part in parts], axis=0)
        low = low_ref[:, 16 * b + k : 16 * b + k + 1]
        added = jnp.dot(sent, low_onehot(low, 1), preferred_element_type=F32)
        total = added if total is None else total + added
    out = {part: total[i * C : (i + 1) * C] for i, part in enumerate(parts)}
    if 1 in out:
        out[1] = out[1] + terms[4 * C : 5 * C]
    return out


def two_layers(blocks, pos, kept, w_ref, picked_ref, slopes_ref, last_ref, scratch):
    middle = []
    for b in (1, 2, 3, 4):
        target = picked_ref.at[0, b - 2] if b in (2, 3) else scratch.at[b // 4]
        pre = conv(blocks[b - 1 : b + 2], pos[b], w_ref[0], target)
        sigmoid = jax.nn.sigmoid(pre)
        slopes_ref[b - 1] = slope_of(pre, sigmoid)
        middle.append((kept[b] * (blocks[b].astype(F32) + pre * sigmoid)).astype(BF16))
    hidden = []
    for b in (2, 3):
        pre = conv(middle[b - 2 : b + 1], pos[b], w_ref[1], picked_ref.at[1, b - 2])
        sigmoid = jax.nn.sigmoid(pre)
        last_ref[b - 2] = slope_of(pre, sigmoid)
        hidden.append((kept[b] * (middle[b - 1].astype(F32) + pre * sigmoid)).astype(BF16))
    return hidden


def pair_kernel(own_ref, other_ref, out_ref, sent_ref):
    size = own_ref.shape[0]
    each = size - 16 - C
    own, other = own_ref[...], other_ref[...]
    first, second = own_of(own, other), own_of(other, own)
    out_ref[:size, :] = first
    out_ref[size:, :] = second
    sent_ref[:C, :] = first[:C]
    sent_ref[C : 2 * C, :] = second[:C]
    sent_ref[2 * C : 2 * C + 16, :] = first[C + each :]
    sent_ref[2 * C + 16 : 2 * C + 32, :] = second[C + each :]
    sent_ref[2 * C + 32 :, :] = own_of(second, first)[C : C + each]


def first_kernel(
    x_ref, got_ref, other_ref, w_ref,
    h_ref, picked_ref, slopes_ref, last_ref, pos_ref, kept_ref, low_ref, near_pos_ref, near_low_ref,
    cot_ref, scratch,
):
    size = x_ref.shape[0] // 2
    below, above = ordered(got_ref, other_ref)
    each = size - 16 - C
    pair = [x_ref[:size, :], x_ref[size:, :]]
    metas = [
        below[2 * C : 2 * C + 16], below[2 * C + 16 : 2 * C + 32], pair[0][C + each :],
        pair[1][C + each :], above[2 * C : 2 * C + 16], above[2 * C + 16 : 2 * C + 32],
    ]
    cots = [below[2 * C + 32 :], pair[0][C : C + each], pair[1][C : C + each], above[2 * C + 32 :]]
    blocks = [below[:C], below[C : 2 * C], pair[0][:C], pair[1][:C], above[:C], above[C : 2 * C]]
    column = lax.broadcasted_iota(jnp.int32, (16, R), 1)
    pos, kept = [], []
    for b, meta in enumerate(metas):
        offset = meta.astype(F32)
        at = jnp.where(offset > 400.0, 768, offset.astype(jnp.int32) + column + R)
        pos_ref[16 * b : 16 * (b + 1), :] = at
        keep = offset[TAPS : TAPS + 1]
        kept_ref[b : b + 1, :] = keep
        pos.append(at)
        kept.append(keep)
    kept_ref[6:8, :] = jnp.zeros((2, R), F32)
    near = jnp.concatenate([own_of(pos[i + 1], pos[i + 2]) for i in range(3)], axis=0)
    near_pos_ref[...] = near
    near_low_ref[...] = low_table(near)
    low_ref[...] = low_table(jnp.concatenate(pos, axis=0))
    for i in range(4):
        cot_ref[each * i : each * (i + 1), :] = cots[i]
    hidden = two_layers(blocks, pos, kept, w_ref, picked_ref, slopes_ref, last_ref, scratch)
    for i in range(2):
        h_ref[i * C : (i + 1) * C, :] = hidden[i]


def read_tables(pos_ref, kept_ref):
    pos = [pos_ref[16 * b : 16 * b + 16, :] for b in range(6)]
    kept = [kept_ref[b : b + 1, :] for b in range(6)]
    return pos, kept


def read_blocks(x_ref, got_ref, other_ref):
    below, above = ordered(got_ref, other_ref)
    return [below[:C], below[C:], x_ref[:C, :], x_ref[C:, :], above[:C], above[C:]]


def layers_kernel(
    x_ref, got_ref, other_ref, w_ref, pos_ref, kept_ref,
    h_ref, picked_ref, slopes_ref, last_ref, scratch,
):
    pos, kept = read_tables(pos_ref, kept_ref)
    blocks = read_blocks(x_ref, got_ref, other_ref)
    hidden = two_layers(blocks, pos, kept, w_ref, picked_ref, slopes_ref, last_ref, scratch)
    for i in range(2):
        h_ref[i * C : (i + 1) * C, :] = hidden[i]


def last_layers_kernel(
    x_ref, got_ref, other_ref, w_ref, pos_ref, kept_ref, joinw_ref, unit_ref,
    share_ref, picked_ref, slopes_ref, last_ref, scratch,
):
    pos, kept = read_tables(pos_ref, kept_ref)
    blocks = read_blocks(x_ref, got_ref, other_ref)
    hidden = two_layers(blocks, pos, kept, w_ref, picked_ref, slopes_ref, last_ref, scratch)
    count = share_ref.shape[0]
    each = share_ref.shape[1] // 4
    for i in range(2):
        partial = lax.dot_general(
            joinw_ref[...], hidden[i], (((0,), (0,)), ((), ())), preferred_element_type=F32
        ).astype(BF16)
        for c in range(count):
            share_ref[c, i * each : (i + 1) * each, :] = partial[c * each : (c + 1) * each]
            share_ref[c, (2 + i) * each : (3 + i) * each, :] = unit_ref[
                i, c * each : (c + 1) * each, :
            ]


def pack_kernel(
    maps_hbm, cot_hbm, near_hbm, foot_hbm, pack_ref, near_ref, foot_ref, sems
):
    each = cot_hbm.shape[0]
    fetch(
        [(near_hbm, near_ref), (foot_hbm, foot_ref), (maps_hbm, pack_ref.at[pl.ds(0, C)]),
         (cot_hbm, pack_ref.at[pl.ds(C, each)])], sems,
    )
    row = lax.axis_index(SKY) * R + lax.broadcasted_iota(jnp.int32, (TAPS, R), 1)
    near = near_ref[...]
    offset = jnp.where(near >= 0, near - row, 512).astype(F32)
    meta = jnp.concatenate(
        [offset, foot_ref[...].astype(F32), jnp.zeros((16 - TAPS - 1, R), F32)], axis=0
    )
    pack_ref[C + each :, :] = meta.astype(BF16)


def weights_kernel(w_hbm, *refs):
    outs, w_ref, sems = refs[:-2], refs[-2], refs[-1]
    fetch([(w_hbm, w_ref)], sems)
    for group, out_ref in enumerate(outs):
        for i in range(2):
            layer = 2 * group + i
            out_ref[i] = jnp.concatenate([w_ref[layer, k] for k in range(TAPS)], axis=1)


def unit_kernel(cot_ref, pos_ref, low_ref, dec_ref, unit_ref, scratch):
    each = cot_ref.shape[0] // 4
    cots = [cot_ref[each * i : each * (i + 1), :] for i in range(4)]
    targets = [(0,), (0, 1), (0, 1), (1,)]
    for k in range(TAPS):
        total = [None, None]
        for i in range(4):
            b = i + 1
            if k == 4:
                if b in (2, 3):
                    scratch[b - 2, k * each : (k + 1) * each, :] = cots[i]
                continue
            block = pos_ref[16 * b + k : 16 * b + k + 1, :] >> 8
            zero = jnp.zeros_like(cots[i])
            sent = jnp.concatenate(
                [jnp.where(block == t + 3 - b, cots[i], zero) for t in targets[i]], axis=0
            )
            low = low_ref[:, 16 * b + k : 16 * b + k + 1]
            added = jnp.dot(sent, low_onehot(low, 1), preferred_element_type=F32)
            for j, t in enumerate(targets[i]):
                part = added[j * each : (j + 1) * each]
                total[t] = part if total[t] is None else total[t] + part
        if k != 4:
            for t in range(2):
                scratch[t, k * each : (k + 1) * each, :] = total[t].astype(BF16)
    for t in range(2):
        unit_ref[t] = lax.dot_general(
            dec_ref[...], scratch[t], (((0,), (0,)), ((), ())), preferred_element_type=F32
        ).astype(BF16)


def slope_kernel(parts_ref, out_ref):
    total = parts_ref[0].astype(F32)
    for i in range(1, parts_ref.shape[0]):
        total = total + parts_ref[i].astype(F32)
    each = total.shape[0] // 2
    joined = total[:each]
    slope = slope_of(joined, jax.nn.sigmoid(joined)).astype(BF16).astype(F32)
    grad = (total[each:] * slope).astype(BF16)
    for i in range(out_ref.shape[0]):
        out_ref[i] = grad


def store_pack(pack_ref, masked_ref, acts, masked):
    for i in range(2):
        pack_ref[i * C : (i + 1) * C, :] = acts[i]
        masked_ref[i] = masked[i]
    pack_ref[2 * C :, :] = own_of(masked[1], masked[0]).astype(BF16)


def head_kernel(unit_ref, joinw_ref, kept_ref, last_ref, pack_ref, masked_ref):
    each = unit_ref.shape[1] // 2
    acts, masked = [], []
    for i in range(2):
        unit_grad = jnp.concatenate(
            [unit_ref[d, i * each : (i + 1) * each, :] for d in range(unit_ref.shape[0])], axis=0
        )
        gradient = jnp.dot(joinw_ref[...], unit_grad, preferred_element_type=F32)
        masked.append(kept_ref[2 + i : 3 + i, :] * gradient)
        acts.append((masked[i] * last_ref[i]).astype(BF16))
    store_pack(pack_ref, masked_ref, acts, masked)


def weight_grad(acts, picked):
    total = None
    for i in range(2):
        added = lax.dot_general(
            own_of(acts[i][: C // 2], acts[i][C // 2 :]), picked[i],
            (((1,), (1,)), ((), ())), preferred_element_type=F32,
        )
        total = added if total is None else total + added
    return total.astype(BF16)


def pair_of(ref):
    return [ref[:C, :], ref[C : 2 * C, :]]


def both(ref, layer):
    return [ref[layer, 0], ref[layer, 1]]


def beside_kernel(has_low, *refs):
    if has_low:
        x_ref, w_ref, pos_ref, low_ref, picked_ref, lower_ref, lower_picked_ref, own_ref, grad_ref = refs
        grad_ref[...] = jnp.concatenate(
            [weight_grad(pair_of(lower_ref), both(lower_picked_ref, 0)),
             weight_grad(pair_of(x_ref), both(picked_ref, 1))], axis=1,
        )
    else:
        x_ref, w_ref, pos_ref, low_ref, picked_ref, own_ref, grad_ref = refs
        grad_ref[...] = weight_grad(pair_of(x_ref), both(picked_ref, 1))
    first, second = [
        spread(act, b, pos_ref, low_ref, w_ref[1], (0, 1, 2))
        for b, act in zip((2, 3), pair_of(x_ref))
    ]
    own_ref[0] = first[0]
    own_ref[1] = first[1] + second[0]
    own_ref[2] = first[2] + second[1]
    own_ref[3] = second[2]


def upper_layer(
    x_ref, got_ref, other_ref, masked_ref, own_ref, w_ref, pos_ref, low_ref, kept_ref, slopes_ref
):
    below, above = ordered(got_ref, other_ref)
    acts = {0: below[:C], 1: below[C : 2 * C], 4: above[:C], 5: above[C : 2 * C]}
    masked = [
        below[2 * C :].astype(F32), masked_ref[0], masked_ref[1], above[2 * C :].astype(F32)
    ]
    gradient = [masked[i] + own_ref[i] for i in range(4)]
    for b, parts in ((0, (2,)), (1, (1, 2)), (4, (0, 1)), (5, (0,))):
        for part, value in spread(acts[b], b, pos_ref, low_ref, w_ref[1], parts).items():
            gradient[b + part - 2] = gradient[b + part - 2] + value
    lower = [kept_ref[i + 1 : i + 2, :] * gradient[i] for i in range(4)]
    low_acts = [(lower[i] * slopes_ref[i]).astype(BF16) for i in range(4)]
    return lower, low_acts


def back_kernel(
    x_ref, got_ref, other_ref, masked_ref, own_ref, w_ref, pos_ref, low_ref, kept_ref, slopes_ref,
    next_ref, pack_ref, out_ref, lower_ref,
):
    lower, low_acts = upper_layer(
        x_ref, got_ref, other_ref, masked_ref, own_ref, w_ref, pos_ref, low_ref, kept_ref,
        slopes_ref,
    )
    result = [lower[1], lower[2]]
    for b, parts in ((1, (2,)), (2, (1, 2)), (3, (0, 1)), (4, (0,))):
        for part, value in spread(low_acts[b - 1], b, pos_ref, low_ref, w_ref[0], parts).items():
            result[b + part - 3] = result[b + part - 3] + value
    masked = [kept_ref[2 + i : 3 + i, :] * result[i] for i in range(2)]
    acts = [(masked[i] * next_ref[i]).astype(BF16) for i in range(2)]
    store_pack(pack_ref, out_ref, acts, masked)
    for i in range(2):
        lower_ref[i * C : (i + 1) * C, :] = low_acts[1 + i]


def last_back_kernel(
    x_ref, got_ref, other_ref, masked_ref, own_ref, w_ref, pos_ref, low_ref, kept_ref, slopes_ref,
    picked_ref, grad5_ref, grad43_ref, grad21_ref, lower_ref, out_ref, keep_ref, send_ref,
):
    lower, low_acts = upper_layer(
        x_ref, got_ref, other_ref, masked_ref, own_ref, w_ref, pos_ref, low_ref, kept_ref,
        slopes_ref,
    )
    out_ref[...] = own_of(lower[1], lower[2])
    for i in range(3):
        lower_ref[i * C : (i + 1) * C, :] = own_of(low_acts[i], low_acts[i + 1])
    last = jnp.concatenate(
        [weight_grad(low_acts[1:3], both(picked_ref, 0)), grad5_ref[...]], axis=1
    )
    middle = grad21_ref[...]
    first = jnp.concatenate([grad43_ref[...], middle[: C // 4]], axis=0)
    second = jnp.concatenate([middle[C // 4 :], last], axis=0)
    low_half = lax.axis_index("yh") == 0
    keep_ref[...] = jnp.where(low_half, first, second)
    send_ref[...] = jnp.where(low_half, second, first)


def map_kernel(lower_ref, own_ref, w_ref, pos_ref, low_ref, map_ref, token_ref):
    own = own_ref[...]
    for i, part in ((0, 2), (1, 1), (2, 0)):
        act = lower_ref[i * C : (i + 1) * C, :]
        own = own + spread(act, i, pos_ref, low_ref, w_ref[0], (part,))[part]
    map_ref[...] = own.astype(BF16)
    token_ref[...] = own[:8, :128]


def add_kernel(keep_ref, got_ref, _, out_ref):
    out_ref[...] = (keep_ref[...].astype(F32) + got_ref[...].astype(F32)).astype(BF16)


def rows_kernel(own_ref, got_ref, out_ref):
    rows = own_ref.shape[0]
    low_half = lax.axis_index("yh") == 0
    own, got = own_ref[...], got_ref[...]
    out_ref[:rows, :] = jnp.where(low_half, own, got)
    out_ref[rows:, :] = jnp.where(low_half, got, own)


def final_kernel(scale, own_ref, other_ref, out_ref):
    wide = TAPS * C
    half_rows = C // 2
    for core, sums in enumerate(ordered(own_ref, other_ref)):
        rows = sums.astype(F32) * scale
        for slot, pair in enumerate(((4, 3), (2, 1), (0, 5))):
            for half, layer in enumerate(pair):
                for k in range(TAPS):
                    at = half * wide + k * C
                    out_ref[layer, k, core * half_rows : (core + 1) * half_rows, :] = rows[
                        slot * half_rows : (slot + 1) * half_rows, at : at + C
                    ]


def sds(shape, dtype):
    return jax.ShapeDtypeStruct(shape, dtype)


def call(body, name, ins, outs, scratch=(), limit=LIMIT):
    specs = [spec for spec, _ in ins]
    return pl.pallas_call(
        body,
        name=name,
        in_specs=specs,
        out_specs=[pl.BlockSpec(memory_space=pltpu.VMEM) for _ in outs],
        out_shape=outs,
        scratch_shapes=list(scratch),
        compiler_params=pltpu.CompilerParams(vmem_limit_bytes=limit),
    )(*[value for _, value in ins])


def v(value):
    return (VMEM, value)


def exchange(value, axes):
    return lax.all_to_all(value, axes, 0, 0, tiled=True)


def add_up(parts):
    return jnp.sum(parts.astype(F32), axis=0).astype(BF16)


def copies(value, count):
    return jnp.broadcast_to(value[None], (count,) + value.shape)


def swap_halves(value):
    return lax.ppermute(value, "yh", [(0, 1), (1, 0)])


def sum_over_sky(keep, send, length, after):
    rows, lanes = keep.shape
    out = [sds(keep.shape, BF16)]
    any_space = pl.BlockSpec(memory_space=pl.ANY)
    chunk = call(
        add_kernel, "add", [v(keep), v(swap_halves(send)), (any_space, after)], out
    )[0]
    tiles = (rows // 8) * (lanes // 128)
    each = -(-tiles // length)
    chunk = chunk.reshape(rows // 8, 8, lanes // 128, 128).transpose(0, 2, 1, 3)
    chunk = jnp.pad(chunk.reshape(tiles, 8, 128), ((0, each * length - tiles), (0, 0), (0, 0)))
    chunk = add_up(exchange(chunk.reshape(length, each, 8, 128), "z"))
    chunk = exchange(copies(chunk, length), "z").reshape(each * length, 8, 128)[:tiles]
    chunk = chunk.reshape(rows // 8, lanes // 128, 8, 128).transpose(0, 2, 1, 3)
    chunk = chunk.reshape(rows, lanes)
    return call(
        rows_kernel, "rows", [v(chunk), v(swap_halves(chunk))], [sds((2 * rows, lanes), BF16)]
    )[0]


def per_device(sky_maps, footprint, neighbours, enc_weight, join_weight, dec_weight, cotangent):
    depth = enc_weight.shape[1]
    branches = lax.axis_size("branch")
    peers = lax.axis_size(SKY)
    dma = pltpu.SemaphoreType.DMA
    weights = call(
        weights_kernel, "weights", [(HBM, enc_weight[0])],
        [sds((2, C, TAPS * C), BF16)] * (depth // 2),
        [pltpu.VMEM(enc_weight.shape[1:], BF16), dma((1,))],
    )
    joinw = join_weight.T
    dec = dec_weight.reshape(-1, dec_weight.shape[2])
    each = cotangent.shape[0]
    full = dec.shape[1]
    wide = TAPS * C
    size = C + each + 16
    pack = call(
        pack_kernel, "pack",
        [(HBM, sky_maps[0]), (HBM, cotangent), (HBM, neighbours), (HBM, footprint)],
        [sds((size, R), BF16)],
        [pltpu.VMEM((TAPS, R), jnp.int32), pltpu.VMEM((1, R), jnp.int32), dma((4,))], None,
    )[0]
    pack, sent = call(
        pair_kernel, "pair",
        [v(call(relay_kernel, "held", [v(pack)], [sds(pack.shape, BF16)])[0]), v(swap_cores(pack))],
        [sds((2 * size, R), BF16), sds((2 * C + 32 + each, R), BF16)],
    )
    pair = sds((2, C, R), F32)
    layer_outs = [sds((2 * C, R), BF16), sds((2, 2, wide, R), BF16), sds((4, C, R), F32), pair]
    scratch = [pltpu.VMEM((2, wide, R), BF16)]
    got, other = widen(sent, [weights[0]])
    low_lanes = sds((R, 128), jnp.int32)
    hidden, picked, slopes, last, pos, kept, low, near_pos, near_low, cots = call(
        first_kernel, "layers01", [v(pack), v(got), v(other), v(weights[0])],
        layer_outs
        + [sds((96, R), jnp.int32), sds((8, R), F32), low_lanes, sds((48, R), jnp.int32),
           low_lanes, sds((4 * each, R), BF16)],
        scratch,
    )
    saved = [(picked, slopes, last)]
    unit = call(
        unit_kernel, "unit", [v(cots), v(pos), v(low), v(dec)],
        [sds((2, full, R), BF16)], [pltpu.VMEM((2, TAPS * each, R), BF16)],
    )[0]
    for group in range(1, depth // 2):
        got, other = widen(hidden, [unit] if group == 1 else ())
        ins = [v(hidden), v(got), v(other), v(weights[group]), v(pos), v(kept)]
        if group < depth // 2 - 1:
            hidden, picked, slopes, last = call(layers_kernel, "layers", ins, layer_outs, scratch)
        else:
            share, picked, slopes, last = call(
                last_layers_kernel, "lastlayers", ins + [v(joinw), v(unit)],
                [sds((branches, 4 * each, R), BF16)] + layer_outs[1:], scratch,
            )
        saved.append((picked, slopes, last))
    parts = exchange(share, "branch")
    mine = call(slope_kernel, "slope", [v(parts)], [sds((branches, 2 * each, R), BF16)])[0]
    pack_outs = [sds((3 * C, R), BF16), pair]
    pack, masked = call(
        head_kernel, "head",
        [v(exchange(mine, "branch")), v(joinw), v(kept), v(saved[-1][2])], pack_outs,
    )
    grads = []
    lower = None
    for group in reversed(range(depth // 2)):
        picked, slopes, _ = saved[group]
        beside = [v(pack), v(weights[group]), v(pos), v(low), v(picked)]
        if lower is not None:
            beside = beside + [v(lower), v(saved[group + 1][0])]
        own, grad = call(
            functools.partial(beside_kernel, lower is not None), "beside", beside,
            [sds((4, C, R), F32), sds((C // 2, wide if lower is None else 2 * wide), BF16)],
        )
        grads.append(grad)
        got, other = widen(pack, [own])
        ins = [
            v(pack), v(got), v(other), v(masked), v(own), v(weights[group]), v(pos), v(low),
            v(kept), v(slopes),
        ]
        if group:
            pack, masked, lower = call(
                back_kernel, "back", ins + [v(saved[group - 1][2])],
                pack_outs + [sds((2 * C, R), BF16)],
            )
        else:
            half = sds((3 * C // 4, 2 * wide), BF16)
            lower, own, keep, send = call(
                last_back_kernel, "lastback", ins + [v(picked)] + [v(g) for g in grads],
                [sds((3 * C, R), BF16), sds((C, R), F32), half, half],
            )
    map_grads, token = call(
        map_kernel, "mapgrad", [v(lower), v(own), v(weights[0]), v(near_pos), v(near_low)],
        [sds((C, R), BF16), sds((8, 128), F32)],
    )
    total = sum_over_sky(keep, send, lax.axis_size("z"), token)
    summed = call(
        functools.partial(final_kernel, 1.0 / math.sqrt(R * peers)), "final",
        [v(total), v(swap_cores(total))],
        [sds((depth, TAPS, C, C), F32)],
    )[0]
    return map_grads[None], summed[None]


def solution(mesh):
    branches, sky = mesh.devices.shape
    mesh = Mesh(mesh.devices.reshape(branches, sky // 4, 2, 2), ("branch",) + SKY)
    in_specs = (
        P("branch", None, SKY),
        P("branch", SKY),
        P(None, SKY),
        P("branch", None, None, None, None),
        P(None, "branch"),
        P(None, "branch", None),
        P("branch", SKY),
    )
    out_specs = (P("branch", None, SKY), P("branch", None, None, None, None))
    return jax.shard_map(
        per_device, mesh=mesh, in_specs=in_specs, out_specs=out_specs, check_vma=False
    )
```

```python
import functools
import math

import jax
import jax.numpy as jnp
from jax import lax
from jax.experimental import pallas as pl
from jax.experimental.pallas import tpu as pltpu
from jax.sharding import Mesh, PartitionSpec as P

SKY = ("z", "yh", "core")
C = 64
R = 256
TAPS = 9
LIMIT = 16 * 1024 * 1024
F32 = jnp.float32
BF16 = jnp.bfloat16
VMEM = pl.BlockSpec(memory_space=pltpu.VMEM)
HBM = pl.BlockSpec(memory_space=pltpu.HBM)


def swap_cores(value):
    return lax.ppermute(value, "core", [(0, 1), (1, 0)])


def widen(value, after=()):
    peers = lax.axis_size(SKY)
    pairs = [(i, i + 2) for i in range(0, peers - 2, 2)] + [(i, i - 2) for i in range(3, peers, 2)]
    got = lax.ppermute(value, SKY, pairs)
    if after:
        got = call(
            relay_kernel, "relay",
            [v(got)] + [(pl.BlockSpec(memory_space=pl.ANY), x) for x in after],
            [sds(value.shape, value.dtype)],
        )[0]
    return got, swap_cores(got)


def relay_kernel(*refs):
    refs[-1][...] = refs[0][...]


def ordered(got, other):
    got, other = got[...], other[...]
    return own_of(got, other), own_of(other, got)


def own_of(first, second):
    return jnp.where(lax.axis_index("core") == 0, first, second)


def fetch(pairs, sems):
    copies = [pltpu.make_async_copy(src, dst, sems.at[i]) for i, (src, dst) in enumerate(pairs)]
    for copy in copies:
        copy.start()
    for copy in copies:
        copy.wait()


def inner(other, first, even, start, size):
    own = other[start : start + size]
    below = other[first + start : first + start + size]
    above = other[2 * first + start : 2 * first + start + size]
    return jnp.where(even, below, own), jnp.where(even, own, above)


def slope_of(value, sigmoid):
    return sigmoid * (1.0 + value * (1.0 - sigmoid))


def low_onehot(low, dim=0):
    return (lax.broadcasted_iota(jnp.int32, (R, R), dim) == low).astype(BF16)


def low_table(tables):
    low = (tables & 255).astype(F32)
    padded = jnp.concatenate([low, jnp.zeros((128 - low.shape[0], R), F32)], axis=0)
    return jnp.transpose(padded).astype(jnp.int32)


def conv(blocks, pos, weight, picked_ref):
    stack = jnp.concatenate(blocks, axis=0)
    for k in range(TAPS):
        if k == 4:
            column = blocks[1]
        else:
            at = pos[k : k + 1]
            block = at >> 8
            found = jnp.dot(stack, low_onehot(at & 255), preferred_element_type=F32)
            column = jnp.where(
                block == 0,
                found[:C],
                jnp.where(block == 1, found[C : 2 * C], jnp.where(block == 2, found[2 * C :], 0.0)),
            ).astype(BF16)
        picked_ref[k * C : (k + 1) * C, :] = column
    return jnp.dot(weight, picked_ref[...], preferred_element_type=F32)


def spread(act, b, pos_ref, low_ref, weight, parts):
    terms = lax.dot_general(weight, act, (((0,), (0,)), ((), ())), preferred_element_type=F32)
    pos = pos_ref[16 * b : 16 * b + 16, :]
    total = None
    for k in range(TAPS):
        if k == 4:
            continue
        block = pos[k : k + 1] >> 8
        term = terms[k * C : (k + 1) * C].astype(BF16)
        zero = jnp.zeros_like(term)
        sent = jnp.concatenate([jnp.where(block == part, term, zero) for part in parts], axis=0)
        low = low_ref[:, 16 * b + k : 16 * b + k + 1]
        added = jnp.dot(sent, low_onehot(low, 1), preferred_element_type=F32)
        total = added if total is None else total + added
    out = {part: total[i * C : (i + 1) * C] for i, part in enumerate(parts)}
    if 1 in out:
        out[1] = out[1] + terms[4 * C : 5 * C]
    return out


def two_layers(blocks, pos, kept, w_ref, picked_ref, slopes_ref, last_ref, scratch):
    middle = []
    for b in (1, 2, 3, 4):
        target = picked_ref.at[0, b - 2] if b in (2, 3) else scratch.at[b // 4]
        pre = conv(blocks[b - 1 : b + 2], pos[b], w_ref[0], target)
        sigmoid = jax.nn.sigmoid(pre)
        slopes_ref[b - 1] = slope_of(pre, sigmoid)
        middle.append((kept[b] * (blocks[b].astype(F32) + pre * sigmoid)).astype(BF16))
    hidden = []
    for b in (2, 3):
        pre = conv(middle[b - 2 : b + 1], pos[b], w_ref[1], picked_ref.at[1, b - 2])
        sigmoid = jax.nn.sigmoid(pre)
        last_ref[b - 2] = slope_of(pre, sigmoid)
        hidden.append((kept[b] * (middle[b - 1].astype(F32) + pre * sigmoid)).astype(BF16))
    return hidden


def pair_kernel(own_ref, other_ref, out_ref, sent_ref):
    size = own_ref.shape[0]
    each = size - 16 - C
    own, other = own_ref[...], other_ref[...]
    first, second = own_of(own, other), own_of(other, own)
    out_ref[:size, :] = first
    out_ref[size:, :] = second
    sent_ref[:C, :] = first[:C]
    sent_ref[C : 2 * C, :] = second[:C]
    sent_ref[2 * C : 2 * C + 16, :] = first[C + each :]
    sent_ref[2 * C + 16 : 2 * C + 32, :] = second[C + each :]
    sent_ref[2 * C + 32 :, :] = own_of(second, first)[C : C + each]


def first_kernel(
    x_ref, got_ref, other_ref, w_ref,
    h_ref, picked_ref, slopes_ref, last_ref, pos_ref, kept_ref, low_ref, near_pos_ref, near_low_ref,
    cot_ref, scratch,
):
    size = x_ref.shape[0] // 2
    below, above = ordered(got_ref, other_ref)
    each = size - 16 - C
    pair = [x_ref[:size, :], x_ref[size:, :]]
    metas = [
        below[2 * C : 2 * C + 16], below[2 * C + 16 : 2 * C + 32], pair[0][C + each :],
        pair[1][C + each :], above[2 * C : 2 * C + 16], above[2 * C + 16 : 2 * C + 32],
    ]
    cots = [below[2 * C + 32 :], pair[0][C : C + each], pair[1][C : C + each], above[2 * C + 32 :]]
    blocks = [below[:C], below[C : 2 * C], pair[0][:C], pair[1][:C], above[:C], above[C : 2 * C]]
    column = lax.broadcasted_iota(jnp.int32, (16, R), 1)
    pos, kept = [], []
    for b, meta in enumerate(metas):
        offset = meta.astype(F32)
        at = jnp.where(offset > 400.0, 768, offset.astype(jnp.int32) + column + R)
        pos_ref[16 * b : 16 * (b + 1), :] = at
        keep = offset[TAPS : TAPS + 1]
        kept_ref[b : b + 1, :] = keep
        pos.append(at)
        kept.append(keep)
    kept_ref[6:8, :] = jnp.zeros((2, R), F32)
    near = jnp.concatenate([own_of(pos[i + 1], pos[i + 2]) for i in range(3)], axis=0)
    near_pos_ref[...] = near
    near_low_ref[...] = low_table(near)
    low_ref[...] = low_table(jnp.concatenate(pos, axis=0))
    for i in range(4):
        cot_ref[each * i : each * (i + 1), :] = cots[i]
    hidden = two_layers(blocks, pos, kept, w_ref, picked_ref, slopes_ref, last_ref, scratch)
    for i in range(2):
        h_ref[i * C : (i + 1) * C, :] = hidden[i]


def read_tables(pos_ref, kept_ref):
    pos = [pos_ref[16 * b : 16 * b + 16, :] for b in range(6)]
    kept = [kept_ref[b : b + 1, :] for b in range(6)]
    return pos, kept


def read_blocks(x_ref, got_ref, other_ref):
    below, above = ordered(got_ref, other_ref)
    return [below[:C], below[C:], x_ref[:C, :], x_ref[C:, :], above[:C], above[C:]]


def layers_kernel(
    x_ref, got_ref, other_ref, w_ref, pos_ref, kept_ref,
    h_ref, picked_ref, slopes_ref, last_ref, scratch,
):
    pos, kept = read_tables(pos_ref, kept_ref)
    blocks = read_blocks(x_ref, got_ref, other_ref)
    hidden = two_layers(blocks, pos, kept, w_ref, picked_ref, slopes_ref, last_ref, scratch)
    for i in range(2):
        h_ref[i * C : (i + 1) * C, :] = hidden[i]


def last_layers_kernel(
    x_ref, got_ref, other_ref, w_ref, pos_ref, kept_ref, joinw_ref, unit_ref,
    share_ref, picked_ref, slopes_ref, last_ref, scratch,
):
    pos, kept = read_tables(pos_ref, kept_ref)
    blocks = read_blocks(x_ref, got_ref, other_ref)
    hidden = two_layers(blocks, pos, kept, w_ref, picked_ref, slopes_ref, last_ref, scratch)
    count = share_ref.shape[0]
    each = share_ref.shape[1] // 4
    for i in range(2):
        partial = lax.dot_general(
            joinw_ref[...], hidden[i], (((0,), (0,)), ((), ())), preferred_element_type=F32
        ).astype(BF16)
        for c in range(count):
            share_ref[c, i * each : (i + 1) * each, :] = partial[c * each : (c + 1) * each]
            share_ref[c, (2 + i) * each : (3 + i) * each, :] = unit_ref[
                i, c * each : (c + 1) * each, :
            ]


def pack_kernel(
    maps_hbm, cot_hbm, near_hbm, foot_hbm, pack_ref, near_ref, foot_ref, sems
):
    each = cot_hbm.shape[0]
    fetch(
        [(near_hbm, near_ref), (foot_hbm, foot_ref), (maps_hbm, pack_ref.at[pl.ds(0, C)]),
         (cot_hbm, pack_ref.at[pl.ds(C, each)])], sems,
    )
    row = lax.axis_index(SKY) * R + lax.broadcasted_iota(jnp.int32, (TAPS, R), 1)
    near = near_ref[...]
    offset = jnp.where(near >= 0, near - row, 512).astype(F32)
    meta = jnp.concatenate(
        [offset, foot_ref[...].astype(F32), jnp.zeros((16 - TAPS - 1, R), F32)], axis=0
    )
    pack_ref[C + each :, :] = meta.astype(BF16)


def weights_kernel(w_hbm, *refs):
    outs, w_ref, sems = refs[:-2], refs[-2], refs[-1]
    fetch([(w_hbm, w_ref)], sems)
    for group, out_ref in enumerate(outs):
        for i in range(2):
            layer = 2 * group + i
            out_ref[i] = jnp.concatenate([w_ref[layer, k] for k in range(TAPS)], axis=1)


def unit_kernel(cot_ref, pos_ref, low_ref, dec_ref, unit_ref, scratch):
    each = cot_ref.shape[0] // 4
    cots = [cot_ref[each * i : each * (i + 1), :] for i in range(4)]
    targets = [(0,), (0, 1), (0, 1), (1,)]
    for k in range(TAPS):
        total = [None, None]
        for i in range(4):
            b = i + 1
            if k == 4:
                if b in (2, 3):
                    scratch[b - 2, k * each : (k + 1) * each, :] = cots[i]
                continue
            block = pos_ref[16 * b + k : 16 * b + k + 1, :] >> 8
            zero = jnp.zeros_like(cots[i])
            sent = jnp.concatenate(
                [jnp.where(block == t + 3 - b, cots[i], zero) for t in targets[i]], axis=0
            )
            low = low_ref[:, 16 * b + k : 16 * b + k + 1]
            added = jnp.dot(sent, low_onehot(low, 1), preferred_element_type=F32)
            for j, t in enumerate(targets[i]):
                part = added[j * each : (j + 1) * each]
                total[t] = part if total[t] is None else total[t] + part
        if k != 4:
            for t in range(2):
                scratch[t, k * each : (k + 1) * each, :] = total[t].astype(BF16)
    for t in range(2):
        unit_ref[t] = lax.dot_general(
            dec_ref[...], scratch[t], (((0,), (0,)), ((), ())), preferred_element_type=F32
        ).astype(BF16)


def slope_kernel(parts_ref, out_ref):
    total = parts_ref[0].astype(F32)
    for i in range(1, parts_ref.shape[0]):
        total = total + parts_ref[i].astype(F32)
    each = total.shape[0] // 2
    joined = total[:each]
    slope = slope_of(joined, jax.nn.sigmoid(joined)).astype(BF16).astype(F32)
    grad = (total[each:] * slope).astype(BF16)
    for i in range(out_ref.shape[0]):
        out_ref[i] = grad


def store_pack(pack_ref, masked_ref, acts, masked):
    for i in range(2):
        pack_ref[i * C : (i + 1) * C, :] = acts[i]
        masked_ref[i] = masked[i]
    pack_ref[2 * C :, :] = own_of(masked[1], masked[0]).astype(BF16)


def head_kernel(unit_ref, joinw_ref, kept_ref, last_ref, pack_ref, masked_ref):
    each = unit_ref.shape[1] // 2
    acts, masked = [], []
    for i in range(2):
        unit_grad = jnp.concatenate(
            [unit_ref[d, i * each : (i + 1) * each, :] for d in range(unit_ref.shape[0])], axis=0
        )
        gradient = jnp.dot(joinw_ref[...], unit_grad, preferred_element_type=F32)
        masked.append(kept_ref[2 + i : 3 + i, :] * gradient)
        acts.append((masked[i] * last_ref[i]).astype(BF16))
    store_pack(pack_ref, masked_ref, acts, masked)


def weight_grad(acts, picked):
    total = None
    for i in range(2):
        added = lax.dot_general(
            own_of(acts[i][: C // 2], acts[i][C // 2 :]), picked[i],
            (((1,), (1,)), ((), ())), preferred_element_type=F32,
        )
        total = added if total is None else total + added
    return total.astype(BF16)


def pair_of(ref):
    return [ref[:C, :], ref[C : 2 * C, :]]


def both(ref, layer):
    return [ref[layer, 0], ref[layer, 1]]


def beside_kernel(has_low, *refs):
    if has_low:
        x_ref, w_ref, pos_ref, low_ref, picked_ref, lower_ref, lower_picked_ref, own_ref, grad_ref = refs
        grad_ref[...] = jnp.concatenate(
            [weight_grad(pair_of(lower_ref), both(lower_picked_ref, 0)),
             weight_grad(pair_of(x_ref), both(picked_ref, 1))], axis=1,
        )
    else:
        x_ref, w_ref, pos_ref, low_ref, picked_ref, own_ref, grad_ref = refs
        grad_ref[...] = weight_grad(pair_of(x_ref), both(picked_ref, 1))
    first, second = [
        spread(act, b, pos_ref, low_ref, w_ref[1], (0, 1, 2))
        for b, act in zip((2, 3), pair_of(x_ref))
    ]
    own_ref[0] = first[0]
    own_ref[1] = first[1] + second[0]
    own_ref[2] = first[2] + second[1]
    own_ref[3] = second[2]


def upper_layer(
    x_ref, got_ref, other_ref, masked_ref, own_ref, w_ref, pos_ref, low_ref, kept_ref, slopes_ref
):
    below, above = ordered(got_ref, other_ref)
    acts = {0: below[:C], 1: below[C : 2 * C], 4: above[:C], 5: above[C : 2 * C]}
    masked = [
        below[2 * C :].astype(F32), masked_ref[0], masked_ref[1], above[2 * C :].astype(F32)
    ]
    gradient = [masked[i] + own_ref[i] for i in range(4)]
    for b, parts in ((0, (2,)), (1, (1, 2)), (4, (0, 1)), (5, (0,))):
        for part, value in spread(acts[b], b, pos_ref, low_ref, w_ref[1], parts).items():
            gradient[b + part - 2] = gradient[b + part - 2] + value
    lower = [kept_ref[i + 1 : i + 2, :] * gradient[i] for i in range(4)]
    low_acts = [(lower[i] * slopes_ref[i]).astype(BF16) for i in range(4)]
    return lower, low_acts


def back_kernel(
    x_ref, got_ref, other_ref, masked_ref, own_ref, w_ref, pos_ref, low_ref, kept_ref, slopes_ref,
    next_ref, pack_ref, out_ref, lower_ref,
):
    lower, low_acts = upper_layer(
        x_ref, got_ref, other_ref, masked_ref, own_ref, w_ref, pos_ref, low_ref, kept_ref,
        slopes_ref,
    )
    result = [lower[1], lower[2]]
    for b, parts in ((1, (2,)), (2, (1, 2)), (3, (0, 1)), (4, (0,))):
        for part, value in spread(low_acts[b - 1], b, pos_ref, low_ref, w_ref[0], parts).items():
            result[b + part - 3] = result[b + part - 3] + value
    masked = [kept_ref[2 + i : 3 + i, :] * result[i] for i in range(2)]
    acts = [(masked[i] * next_ref[i]).astype(BF16) for i in range(2)]
    store_pack(pack_ref, out_ref, acts, masked)
    for i in range(2):
        lower_ref[i * C : (i + 1) * C, :] = low_acts[1 + i]


def last_back_kernel(
    x_ref, got_ref, other_ref, masked_ref, own_ref, w_ref, pos_ref, low_ref, kept_ref, slopes_ref,
    picked_ref, grad5_ref, grad43_ref, grad21_ref, lower_ref, out_ref, keep_ref, send_ref,
):
    lower, low_acts = upper_layer(
        x_ref, got_ref, other_ref, masked_ref, own_ref, w_ref, pos_ref, low_ref, kept_ref,
        slopes_ref,
    )
    out_ref[...] = own_of(lower[1], lower[2])
    for i in range(3):
        lower_ref[i * C : (i + 1) * C, :] = own_of(low_acts[i], low_acts[i + 1])
    last = jnp.concatenate(
        [weight_grad(low_acts[1:3], both(picked_ref, 0)), grad5_ref[...]], axis=1
    )
    middle = grad21_ref[...]
    first = jnp.concatenate([grad43_ref[...], middle[: C // 4]], axis=0)
    second = jnp.concatenate([middle[C // 4 :], last], axis=0)
    low_half = lax.axis_index("yh") == 0
    keep_ref[...] = jnp.where(low_half, first, second)
    send_ref[...] = jnp.where(low_half, second, first)


def map_kernel(lower_ref, own_ref, w_ref, pos_ref, low_ref, map_ref, token_ref):
    own = own_ref[...]
    for i, part in ((0, 2), (1, 1), (2, 0)):
        act = lower_ref[i * C : (i + 1) * C, :]
        own = own + spread(act, i, pos_ref, low_ref, w_ref[0], (part,))[part]
    map_ref[...] = own.astype(BF16)
    token_ref[...] = own[:8, :128]


def add_kernel(keep_ref, got_ref, out_ref):
    out_ref[...] = (keep_ref[...].astype(F32) + got_ref[...].astype(F32)).astype(BF16)


def rows_kernel(own_ref, got_ref, _, out_ref):
    rows = own_ref.shape[0]
    low_half = lax.axis_index("yh") == 0
    own, got = own_ref[...], got_ref[...]
    out_ref[:rows, :] = jnp.where(low_half, own, got)
    out_ref[rows:, :] = jnp.where(low_half, got, own)


def final_kernel(scale, own_ref, other_ref, out_ref):
    wide = TAPS * C
    half_rows = C // 2
    for core, sums in enumerate(ordered(own_ref, other_ref)):
        rows = sums.astype(F32) * scale
        for slot, pair in enumerate(((4, 3), (2, 1), (0, 5))):
            for half, layer in enumerate(pair):
                for k in range(TAPS):
                    at = half * wide + k * C
                    out_ref[layer, k, core * half_rows : (core + 1) * half_rows, :] = rows[
                        slot * half_rows : (slot + 1) * half_rows, at : at + C
                    ]


def sds(shape, dtype):
    return jax.ShapeDtypeStruct(shape, dtype)


def call(body, name, ins, outs, scratch=(), limit=LIMIT):
    specs = [spec for spec, _ in ins]
    return pl.pallas_call(
        body,
        name=name,
        in_specs=specs,
        out_specs=[pl.BlockSpec(memory_space=pltpu.VMEM) for _ in outs],
        out_shape=outs,
        scratch_shapes=list(scratch),
        compiler_params=pltpu.CompilerParams(vmem_limit_bytes=limit),
    )(*[value for _, value in ins])


def v(value):
    return (VMEM, value)


def exchange(value, axes):
    return lax.all_to_all(value, axes, 0, 0, tiled=True)


def add_up(parts):
    return jnp.sum(parts.astype(F32), axis=0).astype(BF16)


def copies(value, count):
    return jnp.broadcast_to(value[None], (count,) + value.shape)


def swap_halves(value):
    return lax.ppermute(value, "yh", [(0, 1), (1, 0)])


def sum_over_sky(keep, send, length, after):
    rows, lanes = keep.shape
    out = [sds(keep.shape, BF16)]
    any_space = pl.BlockSpec(memory_space=pl.ANY)
    chunk = call(
        add_kernel, "add", [v(keep), v(swap_halves(send))], out
    )[0]
    tiles = (rows // 8) * (lanes // 128)
    each = -(-tiles // length)
    chunk = chunk.reshape(rows // 8, 8, lanes // 128, 128).transpose(0, 2, 1, 3)
    chunk = jnp.pad(chunk.reshape(tiles, 8, 128), ((0, each * length - tiles), (0, 0), (0, 0)))
    chunk = add_up(exchange(chunk.reshape(length, each, 8, 128), "z"))
    chunk = exchange(copies(chunk, length), "z").reshape(each * length, 8, 128)[:tiles]
    chunk = chunk.reshape(rows // 8, lanes // 128, 8, 128).transpose(0, 2, 1, 3)
    chunk = chunk.reshape(rows, lanes)
    return call(
        rows_kernel, "rows", [v(chunk), v(swap_halves(chunk)), (any_space, after)], [sds((2 * rows, lanes), BF16)]
    )[0]


def per_device(sky_maps, footprint, neighbours, enc_weight, join_weight, dec_weight, cotangent):
    depth = enc_weight.shape[1]
    branches = lax.axis_size("branch")
    peers = lax.axis_size(SKY)
    dma = pltpu.SemaphoreType.DMA
    weights = call(
        weights_kernel, "weights", [(HBM, enc_weight[0])],
        [sds((2, C, TAPS * C), BF16)] * (depth // 2),
        [pltpu.VMEM(enc_weight.shape[1:], BF16), dma((1,))],
    )
    joinw = join_weight.T
    dec = dec_weight.reshape(-1, dec_weight.shape[2])
    each = cotangent.shape[0]
    full = dec.shape[1]
    wide = TAPS * C
    size = C + each + 16
    pack = call(
        pack_kernel, "pack",
        [(HBM, sky_maps[0]), (HBM, cotangent), (HBM, neighbours), (HBM, footprint)],
        [sds((size, R), BF16)],
        [pltpu.VMEM((TAPS, R), jnp.int32), pltpu.VMEM((1, R), jnp.int32), dma((4,))], None,
    )[0]
    pack, sent = call(
        pair_kernel, "pair",
        [v(call(relay_kernel, "held", [v(pack)], [sds(pack.shape, BF16)])[0]), v(swap_cores(pack))],
        [sds((2 * size, R), BF16), sds((2 * C + 32 + each, R), BF16)],
    )
    pair = sds((2, C, R), F32)
    layer_outs = [sds((2 * C, R), BF16), sds((2, 2, wide, R), BF16), sds((4, C, R), F32), pair]
    scratch = [pltpu.VMEM((2, wide, R), BF16)]
    got, other = widen(sent, [weights[0]])
    low_lanes = sds((R, 128), jnp.int32)
    hidden, picked, slopes, last, pos, kept, low, near_pos, near_low, cots = call(
        first_kernel, "layers01", [v(pack), v(got), v(other), v(weights[0])],
        layer_outs
        + [sds((96, R), jnp.int32), sds((8, R), F32), low_lanes, sds((48, R), jnp.int32),
           low_lanes, sds((4 * each, R), BF16)],
        scratch,
    )
    saved = [(picked, slopes, last)]
    unit = call(
        unit_kernel, "unit", [v(cots), v(pos), v(low), v(dec)],
        [sds((2, full, R), BF16)], [pltpu.VMEM((2, TAPS * each, R), BF16)],
    )[0]
    for group in range(1, depth // 2):
        got, other = widen(hidden, [unit] if group == 1 else ())
        ins = [v(hidden), v(got), v(other), v(weights[group]), v(pos), v(kept)]
        if group < depth // 2 - 1:
            hidden, picked, slopes, last = call(layers_kernel, "layers", ins, layer_outs, scratch)
        else:
            share, picked, slopes, last = call(
                last_layers_kernel, "lastlayers", ins + [v(joinw), v(unit)],
                [sds((branches, 4 * each, R), BF16)] + layer_outs[1:], scratch,
            )
        saved.append((picked, slopes, last))
    parts = exchange(share, "branch")
    mine = call(slope_kernel, "slope", [v(parts)], [sds((branches, 2 * each, R), BF16)])[0]
    pack_outs = [sds((3 * C, R), BF16), pair]
    pack, masked = call(
        head_kernel, "head",
        [v(exchange(mine, "branch")), v(joinw), v(kept), v(saved[-1][2])], pack_outs,
    )
    grads = []
    lower = None
    for group in reversed(range(depth // 2)):
        picked, slopes, _ = saved[group]
        beside = [v(pack), v(weights[group]), v(pos), v(low), v(picked)]
        if lower is not None:
            beside = beside + [v(lower), v(saved[group + 1][0])]
        own, grad = call(
            functools.partial(beside_kernel, lower is not None), "beside", beside,
            [sds((4, C, R), F32), sds((C // 2, wide if lower is None else 2 * wide), BF16)],
        )
        grads.append(grad)
        got, other = widen(pack, [own])
        ins = [
            v(pack), v(got), v(other), v(masked), v(own), v(weights[group]), v(pos), v(low),
            v(kept), v(slopes),
        ]
        if group:
            pack, masked, lower = call(
                back_kernel, "back", ins + [v(saved[group - 1][2])],
                pack_outs + [sds((2 * C, R), BF16)],
            )
        else:
            half = sds((3 * C // 4, 2 * wide), BF16)
            lower, own, keep, send = call(
                last_back_kernel, "lastback", ins + [v(picked)] + [v(g) for g in grads],
                [sds((3 * C, R), BF16), sds((C, R), F32), half, half],
            )
    map_grads, token = call(
        map_kernel, "mapgrad", [v(lower), v(own), v(weights[0]), v(near_pos), v(near_low)],
        [sds((C, R), BF16), sds((8, 128), F32)],
    )
    total = sum_over_sky(keep, send, lax.axis_size("z"), token)
    summed = call(
        functools.partial(final_kernel, 1.0 / math.sqrt(R * peers)), "final",
        [v(total), v(swap_cores(total))],
        [sds((depth, TAPS, C, C), F32)],
    )[0]
    return map_grads[None], summed[None]


def solution(mesh):
    branches, sky = mesh.devices.shape
    mesh = Mesh(mesh.devices.reshape(branches, sky // 4, 2, 2), ("branch",) + SKY)
    in_specs = (
        P("branch", None, SKY),
        P("branch", SKY),
        P(None, SKY),
        P("branch", None, None, None, None),
        P(None, "branch"),
        P(None, "branch", None),
        P("branch", SKY),
    )
    out_specs = (P("branch", None, SKY), P("branch", None, None, None, None))
    return jax.shard_map(
        per_device, mesh=mesh, in_specs=in_specs, out_specs=out_specs, check_vma=False
    )
```
